128 devices in a mesh: rows: 8 (over z, core), cols: 16 (over y, x).
Axes of the slice: x: 4, y: 4, z: 4, core: 2. Of those that a mesh axis runs over, the one named last changes fastest.
Arguments:
- pivot_rhs: float32 [4, 4096, 1024], P(None, 'cols'), may hold values from -6 to 6
- bound_sol: bfloat16 [16384, 1024], P('rows'), may hold values from -6 to 6
- border_tiles: bfloat16 [16384, 4, 4096], P('rows', None, 'cols'), may hold values from -0.046875 to 0.046875
- lower_tiles: bfloat16 [6, 4096, 4096], P(None, 'rows', 'cols'), may hold values from -0.09375 to 0.09375
- inverse_diag: bfloat16 [4, 4096, 4096], P(None, 'cols', 'rows'), may hold values from -0.09375 to 0.09375
- owner_map: int32 [128, 128, 1], P(('rows', 'cols')), may hold values from 0 to 127; in each aligned block of 128 rows (0 to 127, 128 to 255, ..., all dimensions but the last counted through in order) at most 2 rows name the same one
Outputs:
- child_rows: float32 [32768, 1024], P(('rows', 'cols'))
The draws below stay inside these ranges and needn't reach their ends.
Inputs may be any that keep to these rules, and one draw needn't show every extreme that they name: `owner_map`: among the rows of one device (one index of the first dimension), no owner is named more than 2 times, a bound that some block reaches; every owner is named somewhere.
All inputs are finite; a program needn't handle non-finite values.
Results may differ from the reference program's by a relative error of at most 0.008.
Values may be sent and summed in bfloat16 or wider, within the bound.
No kernel may reach another device: no remote copies, remote signals or barrier semaphores. Data moves between devices by JAX's collectives and lax.ppermute only.
A program may use at most 64 MiB of HBM per device.

```python
import math
import jax
import jax.numpy as jnp
import numpy as np
from jax import lax

NB = 4
BS = 4096
BND = 16384
NRHS = 1024
NPAIR = 6
ROWS_DEV = 128
MOST = 2
DEVICES = 128


def block_scale(rng, dims, split, smallest, largest):
    gain = 1.0
    for position, parts in split:
        steps = jax.random.uniform(jax.random.fold_in(jax.random.fold_in(rng, 6), position), (parts,), jnp.float32, smallest / len(split), largest / len(split))
        gain = gain * jnp.repeat(jnp.exp(steps), dims[position] // parts).reshape((-1,) + (1,) * (len(dims) - 1 - position))
    return gain


def shared_out(key, own, number, rows, amount, top, bound, slope):
    sequence = jax.random.permutation(key, amount)
    packed, ordinary = shares(amount, rows * top, bound, slope, True), shares(amount, rows * top, bound, slope, False)
    places = jnp.arange(amount)

    def named(tallies, offset_by):
        used = int((tallies > 0).sum())
        fixed = max(1, used // 4)
        moved = fixed + (places - fixed + offset_by * (used - fixed)) % max(1, amount - fixed)
        return jnp.zeros((amount,), jnp.int32).at[sequence[jnp.where(places < fixed, places, moved)]].set(jnp.asarray(tallies, jnp.int32))

    tallies = jnp.where(number % 4 == 0, named(packed, number // 4), named(ordinary, number - number // 4 - 1))
    mixed = jax.random.permutation(jax.random.fold_in(own, 3), amount)
    donor, sink = mixed[0:amount // 2 * 2:2], mixed[1:amount // 2 * 2:2]
    room = jnp.minimum(tallies[donor] - 1, bound - tallies[sink]) // 2
    room = jnp.where((donor == sequence[0]) | (sink == sequence[0]) | (tallies[sink] == 0), 0, jnp.maximum(room, 0))
    moved = jax.random.randint(jax.random.fold_in(own, 4), (amount // 2,), 0, 1 << 20) % (room + 1)
    tallies = tallies.at[donor].add(-moved).at[sink].add(moved)
    labels = jnp.searchsorted(jnp.cumsum(tallies), jnp.arange(rows * top), side="right").astype(jnp.int32)
    listing = labels.reshape(top, rows).T
    listing = listing[jax.random.permutation(jax.random.fold_in(own, 1), rows)]
    offset_by = jax.random.randint(jax.random.fold_in(own, 2), (rows, 1), 0, top)
    return jnp.take_along_axis(listing, (jnp.arange(top)[None, :] + offset_by) % top, axis=1)


def shares(count, total, most, lean, full):
    portions = [(1 << 20) // math.isqrt(rank ** lean) + 1 for rank in range(1, count + 1)]
    largest = most if full else min(most, max(-(-total // count), total * portions[0] // sum(portions)))
    least = 1 if total - largest >= count - 1 else 0
    counts, rest = [largest] + [least] * (count - 1), total - largest - least * (count - 1)
    while rest > 0:
        candidates = [i for i in range(1, count) if counts[i] < largest] or [i for i in range(1, count) if counts[i] < most]
        mass, budget = sum([portions[i] for i in candidates]), rest
        for i in candidates:
            addition = min(most - counts[i], max(1, budget * portions[i] // mass), rest)
            counts[i] = counts[i] + addition
            rest = rest - addition
    return np.array(counts)


def bell_draw(rng, extent, spread, bound, split=(), held_as=jnp.bfloat16):
    entries = jax.random.normal(rng, extent, jnp.float32) * spread
    if len(split) > 0:
        entries = block_scale(rng, extent, split, -0.22, 0.18) * entries
    return jnp.clip(entries, min=-bound, max=bound).astype(held_as)


def setup_inputs(seed: int = 0) -> dict:
    seeds = jax.random.split(jax.random.key(seed), 7)
    pivot_rhs = bell_draw(seeds[0], (NB, BS, NRHS), 1.0, 6.0, ((1, 16),), jnp.float32)
    bound_sol = bell_draw(seeds[1], (BND, NRHS), 1.0, 6.0, ((0, 8),))
    border_tiles = bell_draw(seeds[2], (BND, NB, BS), BND ** -0.5, 0.046875, ((0, 8), (2, 16)))
    lower_tiles = bell_draw(seeds[3], (NPAIR, BS, BS), BS ** -0.5, 0.09375, ((1, 8), (2, 16)))
    inverse_diag = bell_draw(seeds[4], (NB, BS, BS), BS ** -0.5, 0.09375, ((1, 16), (2, 8)))
    owner_map_keys = jax.random.split(jax.random.fold_in(seeds[5], 1), DEVICES * ROWS_DEV // ROWS_DEV)
    owner_map_turns = jax.random.permutation(jax.random.fold_in(seeds[5], 3), DEVICES * ROWS_DEV // ROWS_DEV)
    owner_map = jax.vmap(lambda own, number: shared_out(jax.random.fold_in(seeds[5], 2), own, number, ROWS_DEV, DEVICES, 1, MOST, 2))(owner_map_keys, owner_map_turns).reshape((DEVICES, ROWS_DEV, 1))
    return {"pivot_rhs": pivot_rhs, "bound_sol": bound_sol, "border_tiles": border_tiles, "lower_tiles": lower_tiles, "inverse_diag": inverse_diag, "owner_map": owner_map}


def pair_slot(later, earlier):
    return later * (later - 1) // 2 + earlier


def pack_rows(rows_here, owners, devices, most):
    onehot = (owners[:, None] == jnp.arange(devices, dtype=jnp.int32)[None, :]).astype(jnp.int32)
    ranks = jnp.cumsum(onehot, axis=0) - onehot
    slots = jnp.sum(ranks * onehot, axis=1)
    target = owners * most + slots
    select = (jnp.arange(devices * most, dtype=jnp.int32)[:, None] == target[None, :]).astype(jnp.float32)
    return jnp.dot(select, rows_here, precision=lax.Precision.HIGHEST, preferred_element_type=jnp.float32)


def reference(pivot_rhs, bound_sol, border_tiles, lower_tiles, inverse_diag, owner_map):
    border_term = lax.dot_general(border_tiles, bound_sol, (((0,), (0,)), ((), ())), preferred_element_type=jnp.float32)
    solved = [None] * NB
    rounded = [None] * NB
    for k in reversed(range(NB)):
        total = border_term[k]
        for j in range(k + 1, NB):
            total = total + lax.dot_general(lower_tiles[pair_slot(j, k)], rounded[j], (((0,), (0,)), ((), ())), preferred_element_type=jnp.float32)
        residual = (pivot_rhs[k] - total).astype(jnp.bfloat16)
        solved[k] = lax.dot_general(inverse_diag[k], residual, (((0,), (0,)), ((), ())), preferred_element_type=jnp.float32)
        rounded[k] = solved[k].astype(jnp.bfloat16)
    solution = jnp.stack(solved)
    per_block = BS // DEVICES
    by_sender = solution.reshape(NB, DEVICES, per_block, NRHS).transpose(1, 0, 2, 3).reshape(DEVICES, ROWS_DEV, NRHS)
    owners = owner_map[:, :, 0]

    def packer(pair):
        return pack_rows(pair[0], pair[1], DEVICES, MOST)

    buffers = lax.map(packer, (by_sender, owners))
    buffers = buffers.reshape(DEVICES, DEVICES, MOST, NRHS).transpose(1, 0, 2, 3)
    return buffers.reshape(DEVICES * DEVICES * MOST, NRHS)
```

```python
import jax
import jax.numpy as jnp
from jax import lax
from jax.experimental import pallas as pl
from jax.experimental.pallas import tpu as pltpu
from jax.sharding import Mesh, PartitionSpec as P

BF16 = jnp.bfloat16
F32 = jnp.float32
VMEM_LIMIT = 48 * 1024 * 1024


def pair_slot(later, earlier):
    return later * (later - 1) // 2 + earlier


def shift(value, axis, by):
    return lax.ppermute(value, axis, [(i, (i + by) % 4) for i in range(4)])


def swap(value):
    return lax.ppermute(value, "core", [(0, 1), (1, 0)])


def spread(value, axis):
    far = shift(value, axis, 2)
    right = shift(value, axis, 1)
    left = shift(value, axis, 3)
    return (value, right, far, left)


def deal(pieces, axis):
    far = shift(pieces[2], axis, 2)
    right = shift(pieces[1], axis, 1)
    left = shift(pieces[3], axis, 3)
    return (pieces[0], right, far, left)


def add_up(refs):
    total = refs[0][...].astype(F32)
    for ref in refs[1:]:
        total = total + ref[...].astype(F32)
    return total


def params(**extra):
    return pltpu.CompilerParams(vmem_limit_bytes=VMEM_LIMIT, **extra)


def cost(flops, moved):
    return pl.CostEstimate(flops=flops, bytes_accessed=moved, transcendentals=0)


def whole(shape):
    return pl.BlockSpec(shape, lambda *_: (0,) * len(shape))


SCALARS = pl.BlockSpec(memory_space=pltpu.SMEM)


def first_kernel(place, v0, v1, v2, v3, mine, other, o0, o1, o2, o3, turned):
    core, x = place[0], place[2]
    turned[...] = add_up((v0, v1, v2, v3)).T.astype(BF16)
    here = pl.ds(pl.multiple_of(core * 512, 512), 512)
    there = pl.ds(pl.multiple_of((1 - core) * 512, 512), 512)
    for step, out in enumerate((o0, o1, o2, o3)):
        rows = pl.ds(pl.multiple_of(lax.rem(x + step, 4) * 128, 128), 128)
        left = turned[rows, :]
        out[:, here] = jnp.dot(left, mine[...], preferred_element_type=F32).astype(BF16)
        out[:, there] = jnp.dot(left, other[...], preferred_element_type=F32).astype(BF16)


def first_product(place, pieces, mine, other):
    shape = jax.ShapeDtypeStruct((128, 1024), BF16)
    return pl.pallas_call(
        first_kernel,
        out_shape=(shape,) * 4,
        in_specs=[SCALARS] + [pl.BlockSpec(memory_space=pltpu.VMEM)] * 6,
        out_specs=(pl.BlockSpec(memory_space=pltpu.VMEM),) * 4,
        scratch_shapes=[pltpu.VMEM((512, 256), BF16)],
        compiler_params=params(),
        cost_estimate=cost(2 * 512 * 256 * 1024, 3 << 20),
        name="first_product",
    )(place, *pieces, mine, other)


def turn_kernel(place, v0, v1, v2, v3, out):
    x = place[2]
    for step, ref in enumerate((v0, v1, v2, v3)):
        lanes = pl.ds(pl.multiple_of(lax.rem(x + 4 - step, 4) * 256, 256), 256)
        for k in range(3):
            out[k, :, lanes] = ref[k].astype(F32).T


def turn(place, pieces):
    return pl.pallas_call(
        turn_kernel,
        out_shape=jax.ShapeDtypeStruct((3, 128, 1024), F32),
        in_specs=[SCALARS] + [pl.BlockSpec(memory_space=pltpu.VMEM)] * 4,
        out_specs=pl.BlockSpec(memory_space=pltpu.VMEM),
        compiler_params=params(),
        cost_estimate=cost(3 * 128 * 1024, 3 << 20),
        name="turn",
    )(place, *pieces)


def lower_step(base, pieces, tiles, at, dtype):
    count = len(pieces)

    def kernel(*refs):
        parts = refs[:count]
        base_ref, tile, out, kept, vec = refs[count:]

        @pl.when(pl.program_id(0) == 0)
        def _():
            vec[...] = add_up(parts).astype(BF16)
            kept[...] = vec[...]

        total = base_ref[...].astype(F32)
        total = total - jnp.dot(vec[:, :512], tile[0, 0], preferred_element_type=F32)
        total = total - jnp.dot(vec[:, 512:], tile[1, 0], preferred_element_type=F32)
        out[...] = total.astype(dtype)

    return pl.pallas_call(
        kernel,
        grid=(4,),
        out_shape=(
            jax.ShapeDtypeStruct((128, 1024), dtype),
            jax.ShapeDtypeStruct((128, 1024), BF16),
        ),
        in_specs=[whole((128, 1024))] * count
        + [
            pl.BlockSpec((128, 256), lambda i: (0, i)),
            pl.BlockSpec((2, 1, 512, 256), lambda i: (0, i, at, 0)),
        ],
        out_specs=(pl.BlockSpec((128, 256), lambda i: (0, i)), whole((128, 1024))),
        scratch_shapes=[pltpu.VMEM((128, 1024), BF16)],
        compiler_params=params(),
        cost_estimate=cost(2 * 128 * 1024 * 1024, 4 << 20),
        name="lower_step",
    )(*pieces, base, tiles)


def diag_step(pieces, tiles, at):
    def kernel(v0, v1, v2, v3, tile, out, vec):
        @pl.when(pl.program_id(0) == 0)
        def _():
            vec[...] = add_up((v0, v1, v2, v3)).astype(BF16)

        total = jnp.dot(vec[:, :256], tile[0, 0], preferred_element_type=F32)
        for x in range(1, 4):
            total = total + jnp.dot(
                vec[:, x * 256 : (x + 1) * 256], tile[0, x], preferred_element_type=F32
            )
        out[...] = total.astype(BF16)

    return pl.pallas_call(
        kernel,
        grid=(4,),
        out_shape=jax.ShapeDtypeStruct((128, 1024), BF16),
        in_specs=[whole((128, 1024))] * 4
        + [pl.BlockSpec((1, 4, 256, 256), lambda i: (i // 2, 0, 2 * at + i % 2, 0))],
        out_specs=pl.BlockSpec((128, 256), lambda i: (0, i)),
        scratch_shapes=[pltpu.VMEM((128, 1024), BF16)],
        compiler_params=params(),
        cost_estimate=cost(2 * 128 * 1024 * 1024, 4 << 20),
        name="diag_step",
    )(*pieces, tiles)


def last_step(place, pieces, tiles, at):
    def kernel(place_ref, v0, v1, v2, v3, tile, o0, o1, o2, o3, vec, full):
        step = pl.program_id(0)

        @pl.when(step == 0)
        def _():
            vec[...] = add_up((v0, v1, v2, v3)).astype(BF16)

        total = jnp.dot(vec[:, :256], tile[0, 0], preferred_element_type=F32)
        for x in range(1, 4):
            total = total + jnp.dot(
                vec[:, x * 256 : (x + 1) * 256], tile[0, x], preferred_element_type=F32
            )
        full[:, pl.ds(pl.multiple_of(step * 256, 256), 256)] = total.astype(BF16)

        @pl.when(step == 3)
        def _():
            y = place_ref[1]
            for by, out in enumerate((o0, o1, o2, o3)):
                start = lax.rem(y + by, 4) * 128
                out[:, :128] = full[:, pl.ds(pl.multiple_of(start, 128), 128)]
                out[:, 128:] = full[:, pl.ds(pl.multiple_of(start + 512, 128), 128)]

    return pl.pallas_call(
        kernel,
        grid=(4,),
        out_shape=(jax.ShapeDtypeStruct((128, 256), BF16),) * 4,
        in_specs=[SCALARS]
        + [whole((128, 1024))] * 4
        + [pl.BlockSpec((1, 4, 256, 256), lambda i: (i // 2, 0, 2 * at + i % 2, 0))],
        out_specs=(whole((128, 256)),) * 4,
        scratch_shapes=[pltpu.VMEM((128, 1024), BF16), pltpu.VMEM((128, 1024), BF16)],
        compiler_params=params(),
        cost_estimate=cost(2 * 128 * 1024 * 1024, 4 << 20),
        name="last_step",
    )(place, *pieces, tiles)


def chosen(target, block):
    slots = lax.broadcasted_iota(jnp.int32, (256, 256), 0) + block * 256
    return jnp.where(slots == target, 1.0, 0.0).astype(BF16)


def picked(target, block, rows):
    return lax.dot_general(
        chosen(target, block), rows, (((1,), (1,)), ((), ())), preferred_element_type=F32
    )


def pack_known(place, target, known):
    def kernel(place_ref, target_ref, x1, x2, x3, out):
        block = pl.program_id(0)
        start = pl.multiple_of(place_ref[1] * 128, 128)
        again = pl.multiple_of(place_ref[1] * 128 + 512, 128)
        total = jnp.zeros((256, 128), F32)
        for k, ref in ((1, x1), (2, x2), (3, x3)):
            rows = jnp.concatenate([ref[:, pl.ds(start, 128)], ref[:, pl.ds(again, 128)]], axis=1)
            total = total + picked(target_ref[k], block, rows)
        out[...] = total.astype(BF16)

    return pl.pallas_call(
        kernel,
        grid=(8,),
        out_shape=jax.ShapeDtypeStruct((2048, 128), BF16),
        in_specs=[SCALARS, whole((4, 1, 256))] + [whole((128, 1024))] * 3,
        out_specs=pl.BlockSpec((256, 128), lambda i: (i, 0)),
        compiler_params=params(),
        cost_estimate=cost(2 * 2048 * 768 * 128, 2 << 20),
        name="pack_known",
    )(place, target, *known)


def pack_last(target, pieces, base):
    def kernel(target_ref, v0, v1, v2, v3, base_ref, out, rows):
        block = pl.program_id(0)

        @pl.when(block == 0)
        def _():
            rows[...] = add_up((v0, v1, v2, v3)).astype(BF16)

        total = base_ref[...].astype(F32) + picked(target_ref[0], block, rows[...])
        out[...] = total.astype(BF16)

    return pl.pallas_call(
        kernel,
        grid=(8,),
        out_shape=jax.ShapeDtypeStruct((2048, 128), BF16),
        in_specs=[whole((4, 1, 256))]
        + [whole((128, 256))] * 4
        + [pl.BlockSpec((256, 128), lambda i: (i, 0))],
        out_specs=pl.BlockSpec((256, 128), lambda i: (i, 0)),
        scratch_shapes=[pltpu.VMEM((128, 256), BF16)],
        compiler_params=params(),
        cost_estimate=cost(2 * 2048 * 256 * 128, 2 << 20),
        name="pack_last",
    )(target, *pieces, base)


def unpack(received):
    def kernel(got, out):
        for core in range(2):
            for y in range(4):
                for x in range(4):
                    tile = got[0, core, y, x].astype(F32)
                    lanes = pl.ds((core * 4 + x) * 128, 128)
                    for half in range(2):
                        out[pl.ds(half * 32 + y * 8, 8), lanes] = tile[half * 8 : half * 8 + 8]

    return pl.pallas_call(
        kernel,
        grid=(4,),
        out_shape=jax.ShapeDtypeStruct((256, 1024), F32),
        in_specs=[pl.BlockSpec((1, 2, 4, 4, 16, 128), lambda i: (i, 0, 0, 0, 0, 0))],
        out_specs=pl.BlockSpec((64, 1024), lambda i: (i, 0)),
        compiler_params=params(),
        cost_estimate=cost(256 * 1024, 2 << 20),
        name="unpack",
    )(received.reshape(4, 2, 4, 4, 16, 128))


def slots_of(owners, core, x):
    pair = swap(owners)
    both = jnp.where(core == 0, jnp.stack([owners, pair]), jnp.stack([pair, owners]))
    around = [both] + [shift(both, "x", -by) for by in (1, 2, 3)]
    twice = jnp.stack(around + around)
    ordered = lax.dynamic_slice_in_dim(twice, lax.rem(4 - x, 4), 4, axis=0)
    named = ordered.transpose(1, 0, 2).reshape(8, 128)
    same = named[:, :, None] == named[:, None, :]
    earlier = jnp.arange(128)[None, :, None] > jnp.arange(128)[None, None, :]
    ranks = jnp.sum((same & earlier).astype(jnp.int32), axis=2)
    target = named * 16 + jnp.arange(8, dtype=jnp.int32)[:, None] * 2 + ranks
    return target.reshape(8, 4, 32).transpose(1, 0, 2).reshape(4, 1, 256)


def halves(tile):
    return [tile[:, :256], tile[:, 256:]]


def gathered(parts):
    rows = sum(part.shape[0] for part in parts)
    joined = jnp.concatenate(parts, axis=0) if len(parts) > 1 else parts[0]
    return lax.all_gather(joined, ("core", "x"), axis=0, tiled=False).reshape(2, 4, rows, 256)


def local(pivot_rhs, bound_sol, border_tiles, lower_tiles, inverse_diag, owner_map):
    z, core, y, x = (lax.axis_index(name) for name in ("z", "core", "y", "x"))
    place = jnp.stack([core, y, x, z]).astype(jnp.int32)
    lead = jnp.where((z == 0) & (core == 0), 1.0, 0.0).astype(F32)

    def lower(j, k):
        return lower_tiles[pair_slot(j, k)]

    early = gathered([lower(3, 2)] + halves(inverse_diag[2]))
    middle = gathered([lower(3, 1), lower(2, 1)] + halves(inverse_diag[1]))
    late = gathered([lower(3, 0), lower(2, 0), lower(1, 0)])
    end = gathered(halves(inverse_diag[0]))
    other_diag = swap(inverse_diag[3])

    def border(tiles):
        return lax.dot_general(
            tiles, bound_sol, (((0,), (0,)), ((), ())), preferred_element_type=F32
        )

    def paired(part):
        axis = part.ndim - 1
        away = lax.dynamic_slice_in_dim(part, (1 - core) * 512, 512, axis=axis)
        home = lax.dynamic_slice_in_dim(part, core * 512, 512, axis=axis)
        return (home.astype(F32) + swap(away).astype(F32)).astype(BF16)

    top = (lead * pivot_rhs[3] - border(border_tiles[:, 3, :])).astype(BF16)
    products = first_product(place, spread(paired(top), "z"), inverse_diag[3], other_diag)

    rest = paired((lead * pivot_rhs[:3] - border(border_tiles[:, :3, :])).astype(BF16))
    cut = [
        lax.dynamic_slice_in_dim(rest, lax.rem(x + by, 4) * 128, 128, axis=2) for by in range(4)
    ]
    base = turn(place, deal(cut, "x"))
    target = slots_of(owner_map[0, :, 0], core, x)

    over_x = deal(products, "x")
    partial = sum(piece.astype(F32) for piece in over_x).astype(BF16)
    pieces = spread(partial, "y")
    residual, x3 = lower_step(base[2], pieces, early, 0, BF16)
    over_z = spread(residual, "z")
    base1, _ = lower_step(base[1], (x3,), middle, 0, F32)
    pieces = spread(diag_step(over_z, early, 1), "y")
    residual, x2 = lower_step(base1, pieces, middle, 1, BF16)
    over_z = spread(residual, "z")
    base0, _ = lower_step(base[0], (x3,), late, 0, F32)
    pieces = spread(diag_step(over_z, middle, 2), "y")
    base0, _ = lower_step(base0, (x2,), late, 1, F32)
    residual, x1 = lower_step(base0, pieces, late, 2, BF16)
    over_z = spread(residual, "z")
    packed = pack_known(place, target, (x1, x2, x3))
    rows = deal(last_step(place, over_z, end, 0), "y")
    packed = pack_last(target, rows, packed).reshape(128, 16, 128)
    received = lax.all_to_all(
        packed, ("z", "core", "y", "x"), split_axis=0, concat_axis=0, tiled=True
    )
    return unpack(received)


def solution(mesh):
    fine = Mesh(mesh.devices.reshape(4, 2, 4, 4), ("z", "core", "y", "x"))
    rows, cols = ("z", "core"), ("y", "x")
    placed = (
        P(None, cols, None),
        P(rows, None),
        P(rows, None, cols),
        P(None, rows, cols),
        P(None, cols, rows),
        P(rows + cols, None, None),
    )
    return jax.shard_map(
        local, mesh=fine, in_specs=placed, out_specs=P(rows + cols, None), check_vma=False
    )
```

```python
import jax
import jax.numpy as jnp
from jax import lax
from jax.experimental import pallas as pl
from jax.experimental.pallas import tpu as pltpu
from jax.sharding import Mesh, PartitionSpec as P

BF16 = jnp.bfloat16
F32 = jnp.float32
VMEM_LIMIT = 48 * 1024 * 1024


def pair_slot(later, earlier):
    return later * (later - 1) // 2 + earlier


def shift(value, axis, by):
    return lax.ppermute(value, axis, [(i, (i + by) % 4) for i in range(4)])


def swap(value):
    return lax.ppermute(value, "core", [(0, 1), (1, 0)])


def spread(value, axis):
    far = shift(value, axis, 2)
    right = shift(value, axis, 1)
    left = shift(value, axis, 3)
    return (value, right, far, left)


def deal(pieces, axis):
    far = shift(pieces[2], axis, 2)
    right = shift(pieces[1], axis, 1)
    left = shift(pieces[3], axis, 3)
    return (pieces[0], right, far, left)


def add_up(refs):
    total = refs[0][...].astype(F32)
    for ref in refs[1:]:
        total = total + ref[...].astype(F32)
    return total


def params(**extra):
    return pltpu.CompilerParams(vmem_limit_bytes=VMEM_LIMIT, **extra)


def cost(flops, moved):
    return pl.CostEstimate(flops=flops, bytes_accessed=moved, transcendentals=0)


def whole(shape):
    return pl.BlockSpec(shape, lambda *_: (0,) * len(shape))


SCALARS = pl.BlockSpec(memory_space=pltpu.SMEM)
VMEM = pl.BlockSpec(memory_space=pltpu.VMEM)


def turn(place, pieces, dtype):
    blocks = pieces[0].shape[0]

    def kernel(place_ref, v0, v1, v2, v3, out):
        for step, ref in enumerate((v0, v1, v2, v3)):
            start = lax.rem(place_ref[2] + 4 - step, 4) * 256
            lanes = pl.ds(pl.multiple_of(start, 256), 256)
            for k in range(blocks):
                out[k, :, lanes] = ref[k].astype(F32).T.astype(dtype)

    return pl.pallas_call(
        kernel,
        out_shape=jax.ShapeDtypeStruct((blocks, 128, 1024), dtype),
        in_specs=[SCALARS] + [VMEM] * 4,
        out_specs=VMEM,
        compiler_params=params(),
        cost_estimate=cost(blocks * 128 * 1024, blocks << 20),
        name="turn",
    )(place, *pieces)


def lower_step(base, pieces, tiles, at, dtype):
    count = len(pieces)

    def kernel(*refs):
        parts = refs[:count]
        base_ref, tiles_ref, out, kept, tile, sems = refs[count:]
        copies = [
            pltpu.make_async_copy(
                tiles_ref.at[:, i, pl.ds(at * 512, 512), :], tile.at[:, i], sems.at[i]
            )
            for i in range(4)
        ]
        for copy in copies:
            copy.start()
        kept[...] = add_up(parts).astype(BF16)
        for i, copy in enumerate(copies):
            lanes = slice(i * 256, (i + 1) * 256)
            copy.wait()
            total = base_ref[:, lanes].astype(F32)
            total = total - jnp.dot(kept[:, :512], tile[0, i], preferred_element_type=F32)
            total = total - jnp.dot(kept[:, 512:], tile[1, i], preferred_element_type=F32)
            out[:, lanes] = total.astype(dtype)

    return pl.pallas_call(
        kernel,
        out_shape=(
            jax.ShapeDtypeStruct((128, 1024), dtype),
            jax.ShapeDtypeStruct((128, 1024), BF16),
        ),
        in_specs=[VMEM] * count + [VMEM, pl.BlockSpec(memory_space=pltpu.HBM)],
        out_specs=(VMEM, VMEM),
        scratch_shapes=[
            pltpu.VMEM((2, 4, 512, 256), BF16),
            pltpu.SemaphoreType.DMA((4,)),
        ],
        compiler_params=params(),
        cost_estimate=cost(2 * 128 * 1024 * 1024, 4 << 20),
        name="lower_step",
    )(*pieces, base, tiles)


def times_diag(place_ref, vec, tiles, out):
    core, x = place_ref[0], place_ref[2]
    for side, group in ((core, tiles[:4]), (1 - core, tiles[4:])):
        total = None
        for step, tile in enumerate(group):
            start = lax.rem(x + 4 - step, 4) * 256
            left = vec[:, pl.ds(pl.multiple_of(start, 256), 256)]
            term = jnp.dot(left, tile[...], preferred_element_type=F32)
            total = term if total is None else total + term
        out[:, pl.ds(pl.multiple_of(side * 512, 512), 512)] = total.astype(BF16)


def diag_step(place, pieces, tiles):
    def kernel(place_ref, *refs):
        out, vec = refs[12:]
        vec[...] = add_up(refs[:4]).astype(BF16)
        times_diag(place_ref, vec, refs[4:12], out)

    return pl.pallas_call(
        kernel,
        out_shape=jax.ShapeDtypeStruct((128, 1024), BF16),
        in_specs=[SCALARS] + [VMEM] * 12,
        out_specs=VMEM,
        scratch_shapes=[pltpu.VMEM((128, 1024), BF16)],
        compiler_params=params(),
        cost_estimate=cost(2 * 128 * 1024 * 1024, 4 << 20),
        name="diag_step",
    )(place, *pieces, *tiles)


def last_step(place, pieces, tiles):
    def kernel(place_ref, *refs):
        vec, full = refs[16:]
        vec[...] = add_up(refs[:4]).astype(BF16)
        times_diag(place_ref, vec, refs[4:12], full)
        for by, out in enumerate(refs[12:16]):
            start = lax.rem(place_ref[1] + by, 4) * 128
            out[:, :128] = full[:, pl.ds(pl.multiple_of(start, 128), 128)]
            out[:, 128:] = full[:, pl.ds(pl.multiple_of(start + 512, 128), 128)]

    return pl.pallas_call(
        kernel,
        out_shape=(jax.ShapeDtypeStruct((128, 256), BF16),) * 4,
        in_specs=[SCALARS] + [VMEM] * 12,
        out_specs=(VMEM,) * 4,
        scratch_shapes=[pltpu.VMEM((128, 1024), BF16), pltpu.VMEM((128, 1024), BF16)],
        compiler_params=params(),
        cost_estimate=cost(2 * 128 * 1024 * 1024, 4 << 20),
        name="last_step",
    )(place, *pieces, *tiles)


def chosen(target, block):
    slots = lax.broadcasted_iota(jnp.int32, (256, 256), 0) + block * 256
    return jnp.where(slots == target, 1.0, 0.0).astype(BF16)


def picked(select, rows):
    return lax.dot_general(
        select, rows, (((1,), (1,)), ((), ())), preferred_element_type=F32
    )


def pack_known(place, target, known):
    def kernel(place_ref, target_ref, x1, x2, x3, out, still):
        block = pl.program_id(0)
        start = pl.multiple_of(place_ref[1] * 128, 128)
        again = pl.multiple_of(place_ref[1] * 128 + 512, 128)
        total = jnp.zeros((256, 128), F32)
        for k, ref in ((1, x1), (2, x2), (3, x3)):
            rows = jnp.concatenate([ref[:, pl.ds(start, 128)], ref[:, pl.ds(again, 128)]], axis=1)
            total = total + picked(chosen(target_ref[k], block), rows)
        out[...] = total.astype(BF16)
        still[...] = chosen(target_ref[0], block)

    return pl.pallas_call(
        kernel,
        grid=(8,),
        out_shape=(
            jax.ShapeDtypeStruct((2048, 128), BF16),
            jax.ShapeDtypeStruct((2048, 256), BF16),
        ),
        in_specs=[SCALARS, whole((4, 1, 256))] + [whole((128, 1024))] * 3,
        out_specs=(
            pl.BlockSpec((256, 128), lambda i: (i, 0)),
            pl.BlockSpec((256, 256), lambda i: (i, 0)),
        ),
        compiler_params=params(),
        cost_estimate=cost(2 * 2048 * 768 * 128, 2 << 20),
        name="pack_known",
    )(place, target, *known)


def pack_last(still, pieces, base):
    def kernel(still_ref, v0, v1, v2, v3, base_ref, out):
        rows = add_up((v0, v1, v2, v3)).astype(BF16)
        out[...] = (base_ref[...].astype(F32) + picked(still_ref[...], rows)).astype(BF16)

    return pl.pallas_call(
        kernel,
        out_shape=jax.ShapeDtypeStruct((2048, 128), BF16),
        in_specs=[VMEM] * 6,
        out_specs=VMEM,
        compiler_params=params(),
        cost_estimate=cost(2 * 2048 * 256 * 128, 2 << 20),
        name="pack_last",
    )(still, *pieces, base)


def unpack(received):
    def kernel(got, out):
        for core in range(2):
            for y in range(4):
                for x in range(4):
                    tile = got[0, core, y, x].astype(F32)
                    lanes = pl.ds((core * 4 + x) * 128, 128)
                    for half in range(2):
                        out[pl.ds(half * 32 + y * 8, 8), lanes] = tile[half * 8 : half * 8 + 8]

    return pl.pallas_call(
        kernel,
        grid=(4,),
        out_shape=jax.ShapeDtypeStruct((256, 1024), F32),
        in_specs=[pl.BlockSpec((1, 2, 4, 4, 16, 128), lambda i: (i, 0, 0, 0, 0, 0))],
        out_specs=pl.BlockSpec((64, 1024), lambda i: (i, 0)),
        compiler_params=params(),
        cost_estimate=cost(256 * 1024, 2 << 20),
        name="unpack",
    )(received.reshape(4, 2, 4, 4, 16, 128))


def slots_of(owners, core, x):
    pair = swap(owners)
    both = jnp.where(core == 0, jnp.stack([owners, pair]), jnp.stack([pair, owners]))
    around = [both] + [shift(both, "x", -by) for by in (1, 2, 3)]
    twice = jnp.stack(around + around)
    ordered = lax.dynamic_slice_in_dim(twice, lax.rem(4 - x, 4), 4, axis=0)
    named = ordered.transpose(1, 0, 2).reshape(8, 128)
    same = named[:, :, None] == named[:, None, :]
    earlier = jnp.arange(128)[None, :, None] > jnp.arange(128)[None, None, :]
    ranks = jnp.sum((same & earlier).astype(jnp.int32), axis=2)
    target = named * 16 + jnp.arange(8, dtype=jnp.int32)[:, None] * 2 + ranks
    return target.reshape(8, 4, 32).transpose(1, 0, 2).reshape(4, 1, 256)


def gathered(parts):
    rows = sum(part.shape[0] for part in parts)
    joined = jnp.concatenate(parts, axis=0) if len(parts) > 1 else parts[0]
    return lax.all_gather(joined, ("core", "x"), axis=0, tiled=False).reshape(2, 4, rows, 256)


def after(value, event):
    return value + (event[0, 0] * 0).astype(value.dtype)


def collected(tile):
    around = spread(tile, "x")
    return around + tuple(swap(piece) for piece in around)


def local(pivot_rhs, bound_sol, border_tiles, lower_tiles, inverse_diag, owner_map):
    z, core, y, x = (lax.axis_index(name) for name in ("z", "core", "y", "x"))
    place = jnp.stack([core, y, x, z]).astype(jnp.int32)
    lead = jnp.where((z == 0) & (core == 0), 1.0, 0.0).astype(F32)

    def lower(j, k):
        return lower_tiles[pair_slot(j, k)]

    early = gathered([lower(3, 2)])
    middle = gathered([lower(3, 1), lower(2, 1)])
    late = gathered([lower(3, 0), lower(2, 0), lower(1, 0)])

    flat = lax.optimization_barrier(border_tiles.reshape(border_tiles.shape[0], -1))

    def border(tiles):
        return lax.dot_general(
            tiles, bound_sol, (((0,), (0,)), ((), ())), preferred_element_type=F32
        )

    def paired(part):
        axis = part.ndim - 1
        away = lax.dynamic_slice_in_dim(part, (1 - core) * 512, 512, axis=axis)
        home = lax.dynamic_slice_in_dim(part, core * 512, 512, axis=axis)
        return (home + swap(away)).astype(BF16)

    def dealt(part):
        cut = [
            lax.dynamic_slice_in_dim(part, lax.rem(x + by, 4) * 128, 128, axis=2)
            for by in range(4)
        ]
        return deal(cut, "x")

    top = lead * pivot_rhs[3] - border(flat[:, 768:])
    top = paired(top[None])
    tiles3 = collected(after(inverse_diag[3], top[0]))
    residual = turn(place, dealt(top), BF16)[0]
    over_z = spread(residual, "z")
    rest = border(after(flat[:, :768], residual)).reshape(3, 256, 1024)
    base = turn(place, dealt(paired(lead * pivot_rhs[:3] - rest)), F32)
    pieces = spread(diag_step(place, over_z, tiles3), "y")
    tiles2 = collected(after(inverse_diag[2], pieces[0]))
    residual, x3 = lower_step(base[2], pieces, early, 0, BF16)
    over_z = spread(residual, "z")
    target = slots_of(owner_map[0, :, 0], core, x)
    pieces = spread(diag_step(place, over_z, tiles2), "y")
    base1, _ = lower_step(base[1], (x3,), middle, 0, F32)
    tiles1 = collected(after(inverse_diag[1], pieces[0]))
    residual, x2 = lower_step(base1, pieces, middle, 1, BF16)
    over_z = spread(residual, "z")
    pieces = spread(diag_step(place, over_z, tiles1), "y")
    base0, _ = lower_step(base[0], (x3,), late, 0, F32)
    base0, _ = lower_step(base0, (x2,), late, 1, F32)
    tiles0 = collected(after(inverse_diag[0], pieces[0]))
    residual, x1 = lower_step(base0, pieces, late, 2, BF16)
    over_z = spread(residual, "z")
    packed, still = pack_known(place, target, (x1, x2, x3))
    rows = deal(last_step(place, over_z, tiles0), "y")
    packed = pack_last(still, rows, packed).reshape(128, 16, 128)
    received = lax.all_to_all(
        packed, ("z", "core", "y", "x"), split_axis=0, concat_axis=0, tiled=True
    )
    return unpack(received)


def solution(mesh):
    fine = Mesh(mesh.devices.reshape(4, 2, 4, 4), ("z", "core", "y", "x"))
    rows, cols = ("z", "core"), ("y", "x")
    placed = (
        P(None, cols, None),
        P(rows, None),
        P(rows, None, cols),
        P(None, rows, cols),
        P(None, cols, rows),
        P(rows + cols, None, None),
    )
    return jax.shard_map(
        local, mesh=fine, in_specs=placed, out_specs=P(rows + cols, None), check_vma=False
    )
```

```python
import jax
import jax.numpy as jnp
from jax import lax
from jax.experimental import pallas as pl
from jax.experimental.pallas import tpu as pltpu
from jax.sharding import Mesh, PartitionSpec as P

BF16 = jnp.bfloat16
F32 = jnp.float32
VMEM_LIMIT = 48 * 1024 * 1024


def pair_slot(later, earlier):
    return later * (later - 1) // 2 + earlier


def shift(value, axis, by):
    return lax.ppermute(value, axis, [(i, (i + by) % 4) for i in range(4)])


def swap(value):
    return lax.ppermute(value, "core", [(0, 1), (1, 0)])


def spread(value, axis):
    far = shift(value, axis, 2)
    right = shift(value, axis, 1)
    left = shift(value, axis, 3)
    return (value, right, far, left)


def deal(pieces, axis):
    far = shift(pieces[2], axis, 2)
    right = shift(pieces[1], axis, 1)
    left = shift(pieces[3], axis, 3)
    return (pieces[0], right, far, left)


def add_up(refs):
    total = refs[0][...].astype(F32)
    for ref in refs[1:]:
        total = total + ref[...].astype(F32)
    return total


def params(limit=VMEM_LIMIT):
    return pltpu.CompilerParams(vmem_limit_bytes=limit)


def cost(flops, moved):
    return pl.CostEstimate(flops=flops, bytes_accessed=moved, transcendentals=0)


def whole(shape):
    return pl.BlockSpec(shape, lambda *_: (0,) * len(shape))


SCALARS = pl.BlockSpec(memory_space=pltpu.SMEM)
VMEM = pl.BlockSpec(memory_space=pltpu.VMEM)
HBM = pl.BlockSpec(memory_space=pltpu.HBM)


def turn(place, pieces, dtype):
    blocks = pieces[0].shape[0]

    def kernel(place_ref, v0, v1, v2, v3, out):
        for step, ref in enumerate((v0, v1, v2, v3)):
            start = lax.rem(place_ref[2] + 4 - step, 4) * 256
            lanes = pl.ds(pl.multiple_of(start, 256), 256)
            for k in range(blocks):
                out[k, :, lanes] = ref[k].astype(F32).T.astype(dtype)

    return pl.pallas_call(
        kernel,
        out_shape=jax.ShapeDtypeStruct((blocks, 128, 1024), dtype),
        in_specs=[SCALARS] + [VMEM] * 4,
        out_specs=VMEM,
        compiler_params=params(),
        cost_estimate=cost(blocks * 128 * 1024, blocks << 20),
        name="turn",
    )(place, *pieces)


def lower_step(base, pieces, tiles, at, dtype):
    count = len(pieces)

    def kernel(*refs):
        parts = refs[:count]
        base_ref, tiles_ref, out, kept, tile, sems = refs[count:]
        copies = [
            pltpu.make_async_copy(
                tiles_ref.at[:, i, pl.ds(at * 512, 512), :], tile.at[:, i], sems.at[i]
            )
            for i in range(4)
        ]
        for copy in copies:
            copy.start()
        kept[...] = add_up(parts).astype(BF16)
        for i, copy in enumerate(copies):
            lanes = slice(i * 256, (i + 1) * 256)
            copy.wait()
            total = base_ref[:, lanes].astype(F32)
            total = total - jnp.dot(kept[:, :512], tile[0, i], preferred_element_type=F32)
            total = total - jnp.dot(kept[:, 512:], tile[1, i], preferred_element_type=F32)
            out[:, lanes] = total.astype(dtype)

    return pl.pallas_call(
        kernel,
        out_shape=(
            jax.ShapeDtypeStruct((128, 1024), dtype),
            jax.ShapeDtypeStruct((128, 1024), BF16),
        ),
        in_specs=[VMEM] * count + [VMEM, HBM],
        out_specs=(VMEM, VMEM),
        scratch_shapes=[
            pltpu.VMEM((2, 4, 512, 256), BF16),
            pltpu.SemaphoreType.DMA((4,)),
        ],
        compiler_params=params(),
        cost_estimate=cost(2 * 128 * 1024 * 1024, 4 << 20),
        name="lower_step",
    )(*pieces, base, tiles)


def times_diag(place_ref, vec, tiles, out):
    core, x = place_ref[0], place_ref[2]
    for side, group in ((core, tiles[:4]), (1 - core, tiles[4:])):
        total = None
        for step, tile in enumerate(group):
            start = lax.rem(x + 4 - step, 4) * 256
            left = vec[:, pl.ds(pl.multiple_of(start, 256), 256)]
            term = jnp.dot(left, tile[...], preferred_element_type=F32)
            total = term if total is None else total + term
        out[:, pl.ds(pl.multiple_of(side * 512, 512), 512)] = total.astype(BF16)


def diag_near(place, pieces, tiles):
    def kernel(place_ref, *refs):
        out, vec = refs[12:]
        vec[...] = add_up(refs[:4]).astype(BF16)
        times_diag(place_ref, vec, refs[4:12], out)

    return pl.pallas_call(
        kernel,
        out_shape=jax.ShapeDtypeStruct((128, 1024), BF16),
        in_specs=[SCALARS] + [VMEM] * 12,
        out_specs=VMEM,
        scratch_shapes=[pltpu.VMEM((128, 1024), BF16)],
        compiler_params=params(),
        cost_estimate=cost(2 * 128 * 1024 * 1024, 4 << 20),
        name="diag_near",
    )(place, *pieces, *tiles)


def fetch_diag(tiles_ref, at, tile, sems):
    copies = [
        pltpu.make_async_copy(
            tiles_ref.at[side, :, pl.ds(at * 512, 512), :], tile.at[side], sems.at[side]
        )
        for side in range(2)
    ]
    for copy in copies:
        copy.start()
    return copies


def times_fetched(copies, vec, tile, out):
    for side, copy in enumerate(copies):
        copy.wait()
        for half in range(2):
            rows = slice(half * 256, (half + 1) * 256)
            total = None
            for x in range(4):
                left = vec[:, x * 256 : (x + 1) * 256]
                term = jnp.dot(left, tile[side, x, rows], preferred_element_type=F32)
                total = term if total is None else total + term
            start = side * 512 + half * 256
            out[:, start : start + 256] = total.astype(BF16)


DIAG_SCRATCH = [
    pltpu.VMEM((128, 1024), BF16),
    pltpu.VMEM((2, 4, 512, 256), BF16),
    pltpu.SemaphoreType.DMA((2,)),
]


def diag_step(pieces, tiles, at):
    def kernel(v0, v1, v2, v3, tiles_ref, out, vec, tile, sems):
        copies = fetch_diag(tiles_ref, at, tile, sems)
        vec[...] = add_up((v0, v1, v2, v3)).astype(BF16)
        times_fetched(copies, vec, tile, out)

    return pl.pallas_call(
        kernel,
        out_shape=jax.ShapeDtypeStruct((128, 1024), BF16),
        in_specs=[VMEM] * 4 + [HBM],
        out_specs=VMEM,
        scratch_shapes=DIAG_SCRATCH,
        compiler_params=params(),
        cost_estimate=cost(2 * 128 * 1024 * 1024, 4 << 20),
        name="diag_step",
    )(*pieces, tiles)


def last_step(place, pieces, tiles, at):
    def kernel(place_ref, v0, v1, v2, v3, tiles_ref, o0, o1, o2, o3, vec, tile, sems, full):
        copies = fetch_diag(tiles_ref, at, tile, sems)
        vec[...] = add_up((v0, v1, v2, v3)).astype(BF16)
        times_fetched(copies, vec, tile, full)
        for by, out in enumerate((o0, o1, o2, o3)):
            start = lax.rem(place_ref[1] + by, 4) * 128
            out[:, :128] = full[:, pl.ds(pl.multiple_of(start, 128), 128)]
            out[:, 128:] = full[:, pl.ds(pl.multiple_of(start + 512, 128), 128)]

    return pl.pallas_call(
        kernel,
        out_shape=(jax.ShapeDtypeStruct((128, 256), BF16),) * 4,
        in_specs=[SCALARS] + [VMEM] * 4 + [HBM],
        out_specs=(VMEM,) * 4,
        scratch_shapes=DIAG_SCRATCH + [pltpu.VMEM((128, 1024), BF16)],
        compiler_params=params(),
        cost_estimate=cost(2 * 128 * 1024 * 1024, 4 << 20),
        name="last_step",
    )(place, *pieces, tiles)


def stage(lower_tiles, inverse_diag, order, owners, event):
    rows = 512 * len(order) + (0 if owners is None else 16)
    moves = []
    for at, (kind, index) in enumerate(order):
        if kind == "L":
            moves.append((0, index, slice(None), at * 512, 512))
        else:
            moves.append((1, index, slice(0, 256), at * 512, 256))
            moves.append((1, index, slice(256, 512), at * 512 + 256, 256))
    extra = [value for value in (owners, event) if value is not None]

    def kernel(lower_ref, diag_ref, *refs):
        out, sems = refs[len(extra) :]
        copies = [
            pltpu.make_async_copy(
                (lower_ref, diag_ref)[which].at[index, :, lanes],
                out.at[pl.ds(start, height)],
                sems.at[number],
            )
            for number, (which, index, lanes, start, height) in enumerate(moves)
        ]
        if owners is not None:
            copies.append(
                pltpu.make_async_copy(refs[0], out.at[pl.ds(rows - 16, 16)], sems.at[len(moves)])
            )
        for copy in copies:
            copy.start()
        for copy in copies:
            copy.wait()

    return pl.pallas_call(
        kernel,
        out_shape=jax.ShapeDtypeStruct((rows, 256), BF16),
        in_specs=[HBM] * (2 + len(extra)),
        out_specs=HBM,
        scratch_shapes=[pltpu.SemaphoreType.DMA((len(moves) + 1,))],
        compiler_params=params(60 * 1024 * 1024),
        cost_estimate=cost(0, 2 * rows * 512),
        name="stage",
    )(lower_tiles, inverse_diag, *extra)


def chosen(target, block):
    slots = lax.broadcasted_iota(jnp.int32, (256, 256), 0) + block * 256
    return jnp.where(slots == target, 1.0, 0.0).astype(BF16)


def picked(select, rows):
    return lax.dot_general(
        select, rows, (((1,), (1,)), ((), ())), preferred_element_type=F32
    )


def pack_known(place, target, known):
    def kernel(place_ref, target_ref, x1, x2, x3, out, still):
        block = pl.program_id(0)
        start = pl.multiple_of(place_ref[1] * 128, 128)
        again = pl.multiple_of(place_ref[1] * 128 + 512, 128)
        total = jnp.zeros((256, 128), F32)
        for k, ref in ((1, x1), (2, x2), (3, x3)):
            rows = jnp.concatenate([ref[:, pl.ds(start, 128)], ref[:, pl.ds(again, 128)]], axis=1)
            total = total + picked(chosen(target_ref[k], block), rows)
        out[...] = total.astype(BF16)
        still[...] = chosen(target_ref[0], block)

    return pl.pallas_call(
        kernel,
        grid=(8,),
        out_shape=(
            jax.ShapeDtypeStruct((2048, 128), BF16),
            jax.ShapeDtypeStruct((2048, 256), BF16),
        ),
        in_specs=[SCALARS, whole((4, 1, 256))] + [whole((128, 1024))] * 3,
        out_specs=(
            pl.BlockSpec((256, 128), lambda i: (i, 0)),
            pl.BlockSpec((256, 256), lambda i: (i, 0)),
        ),
        compiler_params=params(),
        cost_estimate=cost(2 * 2048 * 768 * 128, 2 << 20),
        name="pack_known",
    )(place, target, *known)


def pack_last(still, pieces, base):
    def kernel(still_ref, v0, v1, v2, v3, base_ref, out):
        rows = add_up((v0, v1, v2, v3)).astype(BF16)
        out[...] = (base_ref[...].astype(F32) + picked(still_ref[...], rows)).astype(BF16)

    return pl.pallas_call(
        kernel,
        out_shape=jax.ShapeDtypeStruct((2048, 128), BF16),
        in_specs=[VMEM] * 6,
        out_specs=VMEM,
        compiler_params=params(),
        cost_estimate=cost(2 * 2048 * 256 * 128, 2 << 20),
        name="pack_last",
    )(still, *pieces, base)


def unpack(received):
    def kernel(got, out):
        for core in range(2):
            for y in range(4):
                for x in range(4):
                    tile = got[0, core, y, x].astype(F32)
                    lanes = pl.ds((core * 4 + x) * 128, 128)
                    for half in range(2):
                        out[pl.ds(half * 32 + y * 8, 8), lanes] = tile[half * 8 : half * 8 + 8]

    return pl.pallas_call(
        kernel,
        grid=(4,),
        out_shape=jax.ShapeDtypeStruct((256, 1024), F32),
        in_specs=[pl.BlockSpec((1, 2, 4, 4, 16, 128), lambda i: (i, 0, 0, 0, 0, 0))],
        out_specs=pl.BlockSpec((64, 1024), lambda i: (i, 0)),
        compiler_params=params(),
        cost_estimate=cost(256 * 1024, 2 << 20),
        name="unpack",
    )(received.reshape(4, 2, 4, 4, 16, 128))


def slots_of(named):
    same = named[:, :, None] == named[:, None, :]
    earlier = jnp.arange(128)[None, :, None] > jnp.arange(128)[None, None, :]
    ranks = jnp.sum((same & earlier).astype(jnp.int32), axis=2)
    target = named * 16 + jnp.arange(8, dtype=jnp.int32)[:, None] * 2 + ranks
    return target.reshape(8, 4, 32).transpose(1, 0, 2).reshape(4, 1, 256)


def gathered(joined):
    rows = joined.shape[0]
    return lax.all_gather(joined, ("core", "x"), axis=0, tiled=False).reshape(2, 4, rows, 256)


def nothing(*arrays):
    return sum(array[0, 0] for array in arrays) * 0


def local(pivot_rhs, bound_sol, border_tiles, lower_tiles, inverse_diag, owner_map):
    z, core, y, x = (lax.axis_index(name) for name in ("z", "core", "y", "x"))
    place = jnp.stack([core, y, x, z]).astype(jnp.int32)
    lead = jnp.where((z == 0) & (core == 0), 1.0, 0.0).astype(F32)

    def tile(j, k):
        return ("L", pair_slot(j, k))

    order = [tile(3, 2), ("D", 2), tile(3, 1), tile(2, 1), ("D", 1)]
    early = gathered(stage(lower_tiles, inverse_diag, order, None, None))
    around = spread(inverse_diag[3], "x")

    term = lead * pivot_rhs - lax.dot_general(
        border_tiles, bound_sol, (((0,), (0,)), ((), ())), preferred_element_type=F32
    )
    away = lax.dynamic_slice_in_dim(term, (1 - core) * 512, 512, axis=2).astype(BF16)
    away = away + nothing(*around[1:])
    tiles3 = around + tuple(swap(piece) for piece in around)
    home = lax.dynamic_slice_in_dim(term, core * 512, 512, axis=2)
    both = (home + swap(away).astype(F32)).astype(BF16)
    cut = [
        lax.dynamic_slice_in_dim(both, lax.rem(x + by, 4) * 128, 128, axis=2) for by in range(4)
    ]

    owners = jnp.pad(owner_map[0, :, 0].astype(BF16)[None], ((0, 15), (0, 128)))
    order = [tile(3, 0), tile(2, 0), tile(1, 0), ("D", 0)]
    late = gathered(stage(lower_tiles, inverse_diag, order, owners, both))
    named = late[:, :, 2048, :128].astype(jnp.int32).reshape(8, 128)

    base = turn(place, deal(cut, "x"), F32)
    over_z = spread(base[3].astype(BF16), "z")
    pieces = spread(diag_near(place, over_z, tiles3), "y")
    residual, x3 = lower_step(base[2], pieces, early, 0, BF16)
    over_z = spread(residual, "z")
    pieces = spread(diag_step(over_z, early, 1), "y")
    base1, _ = lower_step(base[1], (x3,), early, 2, F32)
    residual, x2 = lower_step(base1, pieces, early, 3, BF16)
    over_z = spread(residual, "z")
    pieces = spread(diag_step(over_z, early, 4), "y")
    base0, _ = lower_step(base[0], (x3,), late, 0, F32)
    base0, _ = lower_step(base0, (x2,), late, 1, F32)
    residual, x1 = lower_step(base0, pieces, late, 2, BF16)
    over_z = spread(residual, "z")
    packed, still = pack_known(place, slots_of(named), (x1, x2, x3))
    rows = deal(last_step(place, over_z, late, 3), "y")
    packed = pack_last(still, rows, packed).reshape(128, 16, 128)
    received = lax.all_to_all(
        packed, ("z", "core", "y", "x"), split_axis=0, concat_axis=0, tiled=True
    )
    return unpack(received)


def solution(mesh):
    fine = Mesh(mesh.devices.reshape(4, 2, 4, 4), ("z", "core", "y", "x"))
    rows, cols = ("z", "core"), ("y", "x")
    placed = (
        P(None, cols, None),
        P(rows, None),
        P(rows, None, cols),
        P(None, rows, cols),
        P(None, cols, rows),
        P(rows + cols, None, None),
    )
    return jax.shard_map(
        local, mesh=fine, in_specs=placed, out_specs=P(rows + cols, None), check_vma=False
    )
```

```python
import jax
import jax.numpy as jnp
from jax import lax
from jax.experimental import pallas as pl
from jax.experimental.pallas import tpu as pltpu
from jax.sharding import Mesh, PartitionSpec as P

BF16 = jnp.bfloat16
F32 = jnp.float32
VMEM_LIMIT = 48 * 1024 * 1024


def pair_slot(later, earlier):
    return later * (later - 1) // 2 + earlier


def shift(value, axis, by):
    return lax.ppermute(value, axis, [(i, (i + by) % 4) for i in range(4)])


def swap(value):
    return lax.ppermute(value, "core", [(0, 1), (1, 0)])


def spread(value, axis):
    far = shift(value, axis, 2)
    right = shift(value, axis, 1)
    left = shift(value, axis, 3)
    return (value, right, far, left)


def deal(pieces, axis):
    far = shift(pieces[2], axis, 2)
    right = shift(pieces[1], axis, 1)
    left = shift(pieces[3], axis, 3)
    return (pieces[0], right, far, left)


def add_up(refs):
    total = refs[0][...].astype(F32)
    for ref in refs[1:]:
        total = total + ref[...].astype(F32)
    return total


def params(limit=VMEM_LIMIT):
    return pltpu.CompilerParams(vmem_limit_bytes=limit)


def cost(flops, moved):
    return pl.CostEstimate(flops=flops, bytes_accessed=moved, transcendentals=0)


def whole(shape):
    return pl.BlockSpec(shape, lambda *_: (0,) * len(shape))


SCALARS = pl.BlockSpec(memory_space=pltpu.SMEM)
VMEM = pl.BlockSpec(memory_space=pltpu.VMEM)
HBM = pl.BlockSpec(memory_space=pltpu.HBM)


def turn(place, pieces, dtype):
    blocks = pieces[0].shape[0]

    def kernel(place_ref, v0, v1, v2, v3, out):
        for step, ref in enumerate((v0, v1, v2, v3)):
            start = lax.rem(place_ref[2] + 4 - step, 4) * 256
            lanes = pl.ds(pl.multiple_of(start, 256), 256)
            for k in range(blocks):
                out[k, :, lanes] = ref[k].astype(F32).T.astype(dtype)

    return pl.pallas_call(
        kernel,
        out_shape=jax.ShapeDtypeStruct((blocks, 128, 1024), dtype),
        in_specs=[SCALARS] + [VMEM] * 4,
        out_specs=VMEM,
        compiler_params=params(),
        cost_estimate=cost(blocks * 128 * 1024, blocks << 20),
        name="turn",
    )(place, *pieces)


def lower_step(base, pieces, tiles, at, dtype):
    count = len(pieces)

    def kernel(*refs):
        parts = refs[:count]
        base_ref, tiles_ref, out, kept, tile, sems = refs[count:]
        copies = [
            pltpu.make_async_copy(
                tiles_ref.at[:, i, pl.ds(at * 512, 512), :], tile.at[:, i], sems.at[i]
            )
            for i in range(4)
        ]
        for copy in copies:
            copy.start()
        kept[...] = add_up(parts).astype(BF16)
        for i, copy in enumerate(copies):
            lanes = slice(i * 256, (i + 1) * 256)
            copy.wait()
            total = base_ref[:, lanes].astype(F32)
            total = total - jnp.dot(kept[:, :512], tile[0, i], preferred_element_type=F32)
            total = total - jnp.dot(kept[:, 512:], tile[1, i], preferred_element_type=F32)
            out[:, lanes] = total.astype(dtype)

    return pl.pallas_call(
        kernel,
        out_shape=(
            jax.ShapeDtypeStruct((128, 1024), dtype),
            jax.ShapeDtypeStruct((128, 1024), BF16),
        ),
        in_specs=[VMEM] * count + [VMEM, HBM],
        out_specs=(VMEM, VMEM),
        scratch_shapes=[
            pltpu.VMEM((2, 4, 512, 256), BF16),
            pltpu.SemaphoreType.DMA((4,)),
        ],
        compiler_params=params(),
        cost_estimate=cost(2 * 128 * 1024 * 1024, 4 << 20),
        name="lower_step",
    )(*pieces, base, tiles)


def fetch_diag(tiles_ref, at, tile, sems):
    copies = [
        pltpu.make_async_copy(
            tiles_ref.at[side, :, pl.ds(at * 512, 512), :], tile.at[side], sems.at[side]
        )
        for side in range(2)
    ]
    for copy in copies:
        copy.start()
    return copies


def times_fetched(copies, vec, tile, out):
    for side, copy in enumerate(copies):
        copy.wait()
        for half in range(2):
            rows = slice(half * 256, (half + 1) * 256)
            total = None
            for x in range(4):
                left = vec[:, x * 256 : (x + 1) * 256]
                term = jnp.dot(left, tile[side, x, rows], preferred_element_type=F32)
                total = term if total is None else total + term
            start = side * 512 + half * 256
            out[:, start : start + 256] = total.astype(BF16)


DIAG_SCRATCH = [
    pltpu.VMEM((128, 1024), BF16),
    pltpu.VMEM((2, 4, 512, 256), BF16),
    pltpu.SemaphoreType.DMA((2,)),
]


def diag_step(pieces, tiles, at):
    def kernel(v0, v1, v2, v3, tiles_ref, out, vec, tile, sems):
        copies = fetch_diag(tiles_ref, at, tile, sems)
        vec[...] = add_up((v0, v1, v2, v3)).astype(BF16)
        times_fetched(copies, vec, tile, out)

    return pl.pallas_call(
        kernel,
        out_shape=jax.ShapeDtypeStruct((128, 1024), BF16),
        in_specs=[VMEM] * 4 + [HBM],
        out_specs=VMEM,
        scratch_shapes=DIAG_SCRATCH,
        compiler_params=params(),
        cost_estimate=cost(2 * 128 * 1024 * 1024, 4 << 20),
        name="diag_step",
    )(*pieces, tiles)


def last_step(place, pieces, tiles, at):
    def kernel(place_ref, v0, v1, v2, v3, tiles_ref, o0, o1, o2, o3, vec, tile, sems, full):
        copies = fetch_diag(tiles_ref, at, tile, sems)
        vec[...] = add_up((v0, v1, v2, v3)).astype(BF16)
        times_fetched(copies, vec, tile, full)
        for by, out in enumerate((o0, o1, o2, o3)):
            start = lax.rem(place_ref[1] + by, 4) * 128
            out[:, :128] = full[:, pl.ds(pl.multiple_of(start, 128), 128)]
            out[:, 128:] = full[:, pl.ds(pl.multiple_of(start + 512, 128), 128)]

    return pl.pallas_call(
        kernel,
        out_shape=(jax.ShapeDtypeStruct((128, 256), BF16),) * 4,
        in_specs=[SCALARS] + [VMEM] * 4 + [HBM],
        out_specs=(VMEM,) * 4,
        scratch_shapes=DIAG_SCRATCH + [pltpu.VMEM((128, 1024), BF16)],
        compiler_params=params(52 * 1024 * 1024),
        cost_estimate=cost(2 * 128 * 1024 * 1024, 4 << 20),
        name="last_step",
    )(place, *pieces, tiles)


def stage(lower_tiles, inverse_diag, orders, owners):
    moves = []
    for number, order in enumerate(orders):
        for at, (kind, index) in enumerate(order):
            if kind == "L":
                moves.append((0, index, slice(None), number, at * 512, 512))
            else:
                moves.append((1, index, slice(0, 256), number, at * 512, 256))
                moves.append((1, index, slice(256, 512), number, at * 512 + 256, 256))
    heights = [512 * len(order) for order in orders]
    heights[-1] += 16
    count = len(orders)

    def kernel(lower_ref, diag_ref, owners_ref, *refs):
        outs, held, sems = refs[:count], refs[count : 2 * count], refs[2 * count]
        plan = [
            ((lower_ref, diag_ref)[which].at[index, :, lanes], number, pl.ds(start, height))
            for which, index, lanes, number, start, height in moves
        ]
        plan.append((owners_ref, count - 1, pl.ds(heights[-1] - 16, 16)))
        into, onward = [], []
        for at, (source, number, where) in enumerate(plan):
            middle = held[number].at[where]
            into.append(pltpu.make_async_copy(source, middle, sems.at[0, at]))
            onward.append(pltpu.make_async_copy(middle, outs[number].at[where], sems.at[1, at]))
        for copy in into:
            copy.start()
        for first, second in zip(into, onward):
            first.wait()
            second.start()
        for copy in onward:
            copy.wait()

    return pl.pallas_call(
        kernel,
        out_shape=tuple(jax.ShapeDtypeStruct((height, 256), BF16) for height in heights),
        in_specs=[HBM] * 3,
        out_specs=(HBM,) * count,
        scratch_shapes=[pltpu.VMEM((height, 256), BF16) for height in heights]
        + [pltpu.SemaphoreType.DMA((2, len(moves) + 1))],
        compiler_params=params(60 * 1024 * 1024),
        cost_estimate=cost(0, 6 << 20),
        name="stage",
    )(lower_tiles, inverse_diag, owners)


def chosen(target, block):
    slots = lax.broadcasted_iota(jnp.int32, (256, 256), 0) + block * 256
    return jnp.where(slots == target, 1.0, 0.0).astype(BF16)


def picked(select, rows):
    return lax.dot_general(
        select, rows, (((1,), (1,)), ((), ())), preferred_element_type=F32
    )


def pack_known(place, target, known):
    def kernel(place_ref, target_ref, x1, x2, x3, out, still):
        block = pl.program_id(0)
        start = pl.multiple_of(place_ref[1] * 128, 128)
        again = pl.multiple_of(place_ref[1] * 128 + 512, 128)
        total = jnp.zeros((256, 128), F32)
        for k, ref in ((1, x1), (2, x2), (3, x3)):
            rows = jnp.concatenate([ref[:, pl.ds(start, 128)], ref[:, pl.ds(again, 128)]], axis=1)
            total = total + picked(chosen(target_ref[k], block), rows)
        out[...] = total.astype(BF16)
        still[...] = chosen(target_ref[0], block)

    return pl.pallas_call(
        kernel,
        grid=(8,),
        out_shape=(
            jax.ShapeDtypeStruct((2048, 128), BF16),
            jax.ShapeDtypeStruct((2048, 256), BF16),
        ),
        in_specs=[SCALARS, whole((4, 1, 256))] + [whole((128, 1024))] * 3,
        out_specs=(
            pl.BlockSpec((256, 128), lambda i: (i, 0)),
            pl.BlockSpec((256, 256), lambda i: (i, 0)),
        ),
        compiler_params=params(),
        cost_estimate=cost(2 * 2048 * 768 * 128, 2 << 20),
        name="pack_known",
    )(place, target, *known)


def pack_last(still, pieces, base):
    def kernel(still_ref, v0, v1, v2, v3, base_ref, out):
        rows = add_up((v0, v1, v2, v3)).astype(BF16)
        out[...] = (base_ref[...].astype(F32) + picked(still_ref[...], rows)).astype(BF16)

    return pl.pallas_call(
        kernel,
        out_shape=jax.ShapeDtypeStruct((2048, 128), BF16),
        in_specs=[VMEM] * 6,
        out_specs=VMEM,
        compiler_params=params(),
        cost_estimate=cost(2 * 2048 * 256 * 128, 2 << 20),
        name="pack_last",
    )(still, *pieces, base)


def unpack(received):
    def kernel(got, out):
        for core in range(2):
            for y in range(4):
                for x in range(4):
                    tile = got[0, core, y, x].astype(F32)
                    lanes = pl.ds((core * 4 + x) * 128, 128)
                    for half in range(2):
                        out[pl.ds(half * 32 + y * 8, 8), lanes] = tile[half * 8 : half * 8 + 8]

    return pl.pallas_call(
        kernel,
        grid=(4,),
        out_shape=jax.ShapeDtypeStruct((256, 1024), F32),
        in_specs=[pl.BlockSpec((1, 2, 4, 4, 16, 128), lambda i: (i, 0, 0, 0, 0, 0))],
        out_specs=pl.BlockSpec((64, 1024), lambda i: (i, 0)),
        compiler_params=params(),
        cost_estimate=cost(256 * 1024, 2 << 20),
        name="unpack",
    )(received.reshape(4, 2, 4, 4, 16, 128))


def slots_of(named):
    same = named[:, :, None] == named[:, None, :]
    earlier = jnp.arange(128)[None, :, None] > jnp.arange(128)[None, None, :]
    ranks = jnp.sum((same & earlier).astype(jnp.int32), axis=2)
    target = named * 16 + jnp.arange(8, dtype=jnp.int32)[:, None] * 2 + ranks
    return target.reshape(8, 4, 32).transpose(1, 0, 2).reshape(4, 1, 256)


def gathered(joined):
    rows = joined.shape[0]
    return lax.all_gather(joined, ("core", "x"), axis=0, tiled=False).reshape(2, 4, rows, 256)


def local(pivot_rhs, bound_sol, border_tiles, lower_tiles, inverse_diag, owner_map):
    z, core, y, x = (lax.axis_index(name) for name in ("z", "core", "y", "x"))
    place = jnp.stack([core, y, x, z]).astype(jnp.int32)
    lead = jnp.where((z == 0) & (core == 0), 1.0, 0.0).astype(F32)

    def tile(j, k):
        return ("L", pair_slot(j, k))

    owners = jnp.pad(owner_map[0, :, 0].astype(BF16)[None], ((0, 15), (0, 128)))
    orders = [
        [("D", 3), tile(3, 2), ("D", 2), tile(3, 1)],
        [tile(2, 1), ("D", 1), tile(3, 0)],
        [tile(2, 0), tile(1, 0), ("D", 0)],
    ]
    early, middle, late = map(gathered, stage(lower_tiles, inverse_diag, orders, owners))
    named = late[:, :, 1536, :128].astype(jnp.int32).reshape(8, 128)

    def term(side):
        start = side * 512
        rhs = lax.dynamic_slice_in_dim(pivot_rhs, start, 512, axis=2)
        bound = lax.dynamic_slice_in_dim(bound_sol, start, 512, axis=1)
        product = lax.dot_general(
            border_tiles, bound, (((0,), (0,)), ((), ())), preferred_element_type=F32
        )
        return (lead * rhs - product).astype(BF16)

    away = swap(term(1 - core))
    home = lax.optimization_barrier(term(core))
    both = (home.astype(F32) + away.astype(F32)).astype(BF16)
    cut = [
        lax.dynamic_slice_in_dim(both, lax.rem(x + by, 4) * 128, 128, axis=2) for by in range(4)
    ]

    base = turn(place, deal(cut, "x"), F32)
    base3 = base[3].astype(BF16)
    over_z = spread(base3, "z")
    pieces = spread(diag_step(over_z, early, 0), "y")
    residual, x3 = lower_step(base[2], pieces, early, 1, BF16)
    over_z = spread(residual, "z")
    pieces = spread(diag_step(over_z, early, 2), "y")
    base1, _ = lower_step(base[1], (x3,), early, 3, F32)
    residual, x2 = lower_step(base1, pieces, middle, 0, BF16)
    over_z = spread(residual, "z")
    base0, _ = lower_step(base[0], (x3,), middle, 2, F32)
    pieces = spread(diag_step(over_z, middle, 1), "y")
    base0, _ = lower_step(base0, (x2,), late, 0, F32)
    residual, x1 = lower_step(base0, pieces, late, 1, BF16)
    over_z = spread(residual, "z")
    packed, still = pack_known(place, slots_of(named), (x1, x2, x3))
    rows = deal(last_step(place, over_z, late, 2), "y")
    packed = pack_last(still, rows, packed).reshape(128, 16, 128)
    received = lax.all_to_all(
        packed, ("z", "core", "y", "x"), split_axis=0, concat_axis=0, tiled=True
    )
    return unpack(received)


def solution(mesh):
    fine = Mesh(mesh.devices.reshape(4, 2, 4, 4), ("z", "core", "y", "x"))
    rows, cols = ("z", "core"), ("y", "x")
    placed = (
        P(None, cols, None),
        P(rows, None),
        P(rows, None, cols),
        P(None, rows, cols),
        P(None, cols, rows),
        P(rows + cols, None, None),
    )
    return jax.shard_map(
        local, mesh=fine, in_specs=placed, out_specs=P(rows + cols, None), check_vma=False
    )
```

```python
import jax
import jax.numpy as jnp
from jax import lax
from jax.experimental import pallas as pl
from jax.experimental.pallas import tpu as pltpu
from jax.sharding import Mesh, PartitionSpec as P

BF16 = jnp.bfloat16
F32 = jnp.float32
VMEM_LIMIT = 48 * 1024 * 1024


def pair_slot(later, earlier):
    return later * (later - 1) // 2 + earlier


def shift(value, axis, by):
    return lax.ppermute(value, axis, [(i, (i + by) % 4) for i in range(4)])


def swap(value):
    return lax.ppermute(value, "core", [(0, 1), (1, 0)])


def along_x(value, core, by):
    pairs = [(core * 4 + i, core * 4 + (i + by) % 4) for i in range(4)]
    return lax.ppermute(value, ("core", "x"), pairs)


def spread(value, axis):
    far = shift(value, axis, 2)
    right = shift(value, axis, 1)
    left = shift(value, axis, 3)
    return (value, right, far, left)


def deal(pieces, axis):
    far = shift(pieces[2], axis, 2)
    right = shift(pieces[1], axis, 1)
    left = shift(pieces[3], axis, 3)
    return (pieces[0], right, far, left)


def add_up(refs):
    total = refs[0][...].astype(F32)
    for ref in refs[1:]:
        total = total + ref[...].astype(F32)
    return total


def params(limit=VMEM_LIMIT):
    return pltpu.CompilerParams(vmem_limit_bytes=limit)


def cost(flops, moved):
    return pl.CostEstimate(flops=flops, bytes_accessed=moved, transcendentals=0)


def whole(shape):
    return pl.BlockSpec(shape, lambda *_: (0,) * len(shape))


SCALARS = pl.BlockSpec(memory_space=pltpu.SMEM)
VMEM = pl.BlockSpec(memory_space=pltpu.VMEM)
HBM = pl.BlockSpec(memory_space=pltpu.HBM)


def first_product(place, pieces, mine, other, rest):
    def kernel(place_ref, v0, v1, v2, v3, mine_ref, other_ref, rest_ref, *refs):
        outs, turned = refs[:4], refs[4]
        core, x = place_ref[0], place_ref[2]
        turned[...] = add_up((v0, v1, v2, v3)).T.astype(BF16)
        for step, out in enumerate(outs):
            start = pl.multiple_of(lax.rem(x + step, 4) * 128, 128)
            left = turned[pl.ds(start, 128), :]
            for side, tile in ((core, mine_ref), (1 - core, other_ref)):
                product = jnp.dot(left, tile[...], preferred_element_type=F32).astype(BF16)
                for block in range(4):
                    rows = pl.ds(pl.multiple_of((side * 4 + block) * 128, 128), 128)
                    out[rows, :] = product[:, block * 128 : (block + 1) * 128]
            for k in range(3):
                out[1024 + k * 256 : 1280 + k * 256, :] = rest_ref[k, :, pl.ds(start, 128)]

    return pl.pallas_call(
        kernel,
        out_shape=(jax.ShapeDtypeStruct((1792, 128), BF16),) * 4,
        in_specs=[SCALARS] + [VMEM] * 7,
        out_specs=(VMEM,) * 4,
        scratch_shapes=[pltpu.VMEM((512, 256), BF16)],
        compiler_params=params(),
        cost_estimate=cost(2 * 512 * 256 * 1024, 4 << 20),
        name="first_product",
    )(place, *pieces, mine, other, rest)


def by_core(place_ref, parcels, body):
    own, zero, one = parcels[0], parcels[1:4], parcels[4:7]

    @pl.when(place_ref[0] == 0)
    def _():
        body((own, *zero))

    @pl.when(place_ref[0] == 1)
    def _():
        body((own, *one))


def first_sum(place, parcels):
    def kernel(place_ref, *refs):
        out = refs[7]

        def body(parts):
            for block in range(8):
                rows = slice(block * 128, (block + 1) * 128)
                out[:, rows] = add_up([part.at[rows] for part in parts]).astype(BF16)

        by_core(place_ref, refs[:7], body)

    return pl.pallas_call(
        kernel,
        out_shape=jax.ShapeDtypeStruct((128, 1024), BF16),
        in_specs=[SCALARS] + [VMEM] * 7,
        out_specs=VMEM,
        compiler_params=params(),
        cost_estimate=cost(4 * 128 * 1024, 2 << 20),
        name="first_sum",
    )(place, *parcels)


def turn(place, parcels):
    def kernel(place_ref, *refs):
        out = refs[7]

        def body(parts):
            for step, part in enumerate(parts):
                start = lax.rem(place_ref[2] + 4 - step, 4) * 256
                lanes = pl.ds(pl.multiple_of(start, 256), 256)
                for k in range(3):
                    rows = part[1024 + k * 256 : 1280 + k * 256, :]
                    out[k, :, lanes] = rows.astype(F32).T

        by_core(place_ref, refs[:7], body)

    return pl.pallas_call(
        kernel,
        out_shape=jax.ShapeDtypeStruct((3, 128, 1024), F32),
        in_specs=[SCALARS] + [VMEM] * 7,
        out_specs=VMEM,
        compiler_params=params(),
        cost_estimate=cost(3 * 128 * 1024, 4 << 20),
        name="turn",
    )(place, *parcels)


def lower_step(base, pieces, tiles, at, dtype):
    count = len(pieces)

    def kernel(*refs):
        parts = refs[:count]
        base_ref, tiles_ref, out, kept, tile, sems = refs[count:]
        copies = [
            pltpu.make_async_copy(
                tiles_ref.at[:, i, pl.ds(at * 512, 512), :], tile.at[:, i], sems.at[i]
            )
            for i in range(4)
        ]
        for copy in copies:
            copy.start()
        kept[...] = add_up(parts).astype(BF16)
        for i, copy in enumerate(copies):
            lanes = slice(i * 256, (i + 1) * 256)
            copy.wait()
            total = base_ref[:, lanes].astype(F32)
            total = total - jnp.dot(kept[:, :512], tile[0, i], preferred_element_type=F32)
            total = total - jnp.dot(kept[:, 512:], tile[1, i], preferred_element_type=F32)
            out[:, lanes] = total.astype(dtype)

    return pl.pallas_call(
        kernel,
        out_shape=(
            jax.ShapeDtypeStruct((128, 1024), dtype),
            jax.ShapeDtypeStruct((128, 1024), BF16),
        ),
        in_specs=[VMEM] * count + [VMEM, HBM],
        out_specs=(VMEM, VMEM),
        scratch_shapes=[
            pltpu.VMEM((2, 4, 512, 256), BF16),
            pltpu.SemaphoreType.DMA((4,)),
        ],
        compiler_params=params(),
        cost_estimate=cost(2 * 128 * 1024 * 1024, 4 << 20),
        name="lower_step",
    )(*pieces, base, tiles)


def fetch_diag(tiles_ref, at, tile, sems):
    copies = [
        pltpu.make_async_copy(
            tiles_ref.at[side, :, pl.ds(at * 512, 512), :], tile.at[side], sems.at[side]
        )
        for side in range(2)
    ]
    for copy in copies:
        copy.start()
    return copies


def times_fetched(copies, vec, tile, out):
    for side, copy in enumerate(copies):
        copy.wait()
        for half in range(2):
            rows = slice(half * 256, (half + 1) * 256)
            total = None
            for x in range(4):
                left = vec[:, x * 256 : (x + 1) * 256]
                term = jnp.dot(left, tile[side, x, rows], preferred_element_type=F32)
                total = term if total is None else total + term
            start = side * 512 + half * 256
            out[:, start : start + 256] = total.astype(BF16)


DIAG_SCRATCH = [
    pltpu.VMEM((128, 1024), BF16),
    pltpu.VMEM((2, 4, 512, 256), BF16),
    pltpu.SemaphoreType.DMA((2,)),
]


def diag_step(pieces, tiles, at):
    def kernel(v0, v1, v2, v3, tiles_ref, out, vec, tile, sems):
        copies = fetch_diag(tiles_ref, at, tile, sems)
        vec[...] = add_up((v0, v1, v2, v3)).astype(BF16)
        times_fetched(copies, vec, tile, out)

    return pl.pallas_call(
        kernel,
        out_shape=jax.ShapeDtypeStruct((128, 1024), BF16),
        in_specs=[VMEM] * 4 + [HBM],
        out_specs=VMEM,
        scratch_shapes=DIAG_SCRATCH,
        compiler_params=params(),
        cost_estimate=cost(2 * 128 * 1024 * 1024, 4 << 20),
        name="diag_step",
    )(*pieces, tiles)


def last_step(place, pieces, tiles, at):
    def kernel(place_ref, v0, v1, v2, v3, tiles_ref, o0, o1, o2, o3, vec, tile, sems, full):
        copies = fetch_diag(tiles_ref, at, tile, sems)
        vec[...] = add_up((v0, v1, v2, v3)).astype(BF16)
        times_fetched(copies, vec, tile, full)
        for by, out in enumerate((o0, o1, o2, o3)):
            start = lax.rem(place_ref[1] + by, 4) * 128
            out[:, :128] = full[:, pl.ds(pl.multiple_of(start, 128), 128)]
            out[:, 128:] = full[:, pl.ds(pl.multiple_of(start + 512, 128), 128)]

    return pl.pallas_call(
        kernel,
        out_shape=(jax.ShapeDtypeStruct((128, 256), BF16),) * 4,
        in_specs=[SCALARS] + [VMEM] * 4 + [HBM],
        out_specs=(VMEM,) * 4,
        scratch_shapes=DIAG_SCRATCH + [pltpu.VMEM((128, 1024), BF16)],
        compiler_params=params(52 * 1024 * 1024),
        cost_estimate=cost(2 * 128 * 1024 * 1024, 4 << 20),
        name="last_step",
    )(place, *pieces, tiles)


def stage(lower_tiles, inverse_diag, orders, owners):
    moves = []
    for number, order in enumerate(orders):
        for at, (kind, index) in enumerate(order):
            if kind == "L":
                moves.append((0, index, slice(None), number, at * 512, 512))
            else:
                moves.append((1, index, slice(0, 256), number, at * 512, 256))
                moves.append((1, index, slice(256, 512), number, at * 512 + 256, 256))
    heights = [512 * len(order) for order in orders]
    heights[-1] += 16
    count = len(orders)

    def kernel(lower_ref, diag_ref, owners_ref, *refs):
        outs, held, sems = refs[:count], refs[count : 2 * count], refs[2 * count]
        plan = [
            ((lower_ref, diag_ref)[which].at[index, :, lanes], number, pl.ds(start, height))
            for which, index, lanes, number, start, height in moves
        ]
        plan.append((owners_ref, count - 1, pl.ds(heights[-1] - 16, 16)))
        into, onward = [], []
        for at, (source, number, where) in enumerate(plan):
            middle = held[number].at[where]
            into.append(pltpu.make_async_copy(source, middle, sems.at[0, at]))
            onward.append(pltpu.make_async_copy(middle, outs[number].at[where], sems.at[1, at]))
        for copy in into:
            copy.start()
        for first, second in zip(into, onward):
            first.wait()
            second.start()
        for copy in onward:
            copy.wait()

    return pl.pallas_call(
        kernel,
        out_shape=tuple(jax.ShapeDtypeStruct((height, 256), BF16) for height in heights),
        in_specs=[HBM] * 3,
        out_specs=(HBM,) * count,
        scratch_shapes=[pltpu.VMEM((height, 256), BF16) for height in heights]
        + [pltpu.SemaphoreType.DMA((2, len(moves) + 1))],
        compiler_params=params(60 * 1024 * 1024),
        cost_estimate=cost(0, 6 << 20),
        name="stage",
    )(lower_tiles, inverse_diag, owners)


def chosen(target, block):
    slots = lax.broadcasted_iota(jnp.int32, (256, 256), 0) + block * 256
    return jnp.where(slots == target, 1.0, 0.0).astype(BF16)


def picked(select, rows):
    return lax.dot_general(
        select, rows, (((1,), (1,)), ((), ())), preferred_element_type=F32
    )


def pack_known(place, target, known):
    def kernel(place_ref, target_ref, x1, x2, x3, out, still):
        block = pl.program_id(0)
        start = pl.multiple_of(place_ref[1] * 128, 128)
        again = pl.multiple_of(place_ref[1] * 128 + 512, 128)
        total = jnp.zeros((256, 128), F32)
        for k, ref in ((1, x1), (2, x2), (3, x3)):
            rows = jnp.concatenate([ref[:, pl.ds(start, 128)], ref[:, pl.ds(again, 128)]], axis=1)
            total = total + picked(chosen(target_ref[k], block), rows)
        out[...] = total.astype(BF16)
        still[...] = chosen(target_ref[0], block)

    return pl.pallas_call(
        kernel,
        grid=(8,),
        out_shape=(
            jax.ShapeDtypeStruct((2048, 128), BF16),
            jax.ShapeDtypeStruct((2048, 256), BF16),
        ),
        in_specs=[SCALARS, whole((4, 1, 256))] + [whole((128, 1024))] * 3,
        out_specs=(
            pl.BlockSpec((256, 128), lambda i: (i, 0)),
            pl.BlockSpec((256, 256), lambda i: (i, 0)),
        ),
        compiler_params=params(),
        cost_estimate=cost(2 * 2048 * 768 * 128, 2 << 20),
        name="pack_known",
    )(place, target, *known)


def pack_last(still, pieces, base):
    def kernel(still_ref, v0, v1, v2, v3, base_ref, out):
        rows = add_up((v0, v1, v2, v3)).astype(BF16)
        out[...] = (base_ref[...].astype(F32) + picked(still_ref[...], rows)).astype(BF16)

    return pl.pallas_call(
        kernel,
        out_shape=jax.ShapeDtypeStruct((2048, 128), BF16),
        in_specs=[VMEM] * 6,
        out_specs=VMEM,
        compiler_params=params(),
        cost_estimate=cost(2 * 2048 * 256 * 128, 2 << 20),
        name="pack_last",
    )(still, *pieces, base)


def unpack(received):
    def kernel(got, out):
        for core in range(2):
            for y in range(4):
                for x in range(4):
                    tile = got[0, core, y, x].astype(F32)
                    lanes = pl.ds((core * 4 + x) * 128, 128)
                    for half in range(2):
                        out[pl.ds(half * 32 + y * 8, 8), lanes] = tile[half * 8 : half * 8 + 8]

    return pl.pallas_call(
        kernel,
        grid=(4,),
        out_shape=jax.ShapeDtypeStruct((256, 1024), F32),
        in_specs=[pl.BlockSpec((1, 2, 4, 4, 16, 128), lambda i: (i, 0, 0, 0, 0, 0))],
        out_specs=pl.BlockSpec((64, 1024), lambda i: (i, 0)),
        compiler_params=params(),
        cost_estimate=cost(256 * 1024, 2 << 20),
        name="unpack",
    )(received.reshape(4, 2, 4, 4, 16, 128))


def slots_of(named):
    same = named[:, :, None] == named[:, None, :]
    earlier = jnp.arange(128)[None, :, None] > jnp.arange(128)[None, None, :]
    ranks = jnp.sum((same & earlier).astype(jnp.int32), axis=2)
    target = named * 16 + jnp.arange(8, dtype=jnp.int32)[:, None] * 2 + ranks
    return target.reshape(8, 4, 32).transpose(1, 0, 2).reshape(4, 1, 256)


def gathered(joined):
    rows = joined.shape[0]
    return lax.all_gather(joined, ("core", "x"), axis=0, tiled=False).reshape(2, 4, rows, 256)


def local(pivot_rhs, bound_sol, border_tiles, lower_tiles, inverse_diag, owner_map):
    z, core, y, x = (lax.axis_index(name) for name in ("z", "core", "y", "x"))
    place = jnp.stack([core, y, x, z]).astype(jnp.int32)
    lead = jnp.where((z == 0) & (core == 0), 1.0, 0.0).astype(F32)

    def tile(j, k):
        return ("L", pair_slot(j, k))

    owners = jnp.pad(owner_map[0, :, 0].astype(BF16)[None], ((0, 15), (0, 128)))
    orders = [
        [tile(3, 2), ("D", 2), tile(3, 1), tile(2, 1), ("D", 1)],
        [tile(3, 0), tile(2, 0), tile(1, 0), ("D", 0)],
    ]
    early, late = map(gathered, stage(lower_tiles, inverse_diag, orders, owners))
    named = late[:, :, 2048, :128].astype(jnp.int32).reshape(8, 128)
    other = swap(inverse_diag[3])

    def term(side):
        start = side * 512
        rhs = lax.dynamic_slice_in_dim(pivot_rhs, start, 512, axis=2)
        bound = lax.dynamic_slice_in_dim(bound_sol, start, 512, axis=1)
        product = lax.dot_general(
            border_tiles, bound, (((0,), (0,)), ((), ())), preferred_element_type=F32
        )
        return (lead * rhs - product).astype(BF16)

    away = swap(term(1 - core))
    home = lax.optimization_barrier(term(core))
    both = (home.astype(F32) + away.astype(F32)).astype(BF16)
    over_z = spread(both[3], "z")
    own, *parcels = first_product(place, over_z, inverse_diag[3], other, both[:3])
    zero = [along_x(parcels[by - 1], 0, by) for by in (1, 2, 3)]
    token = lax.ppermute(sum(parcel[:8] for parcel in zero), "core", [(0, 1)])
    one = [along_x(parcels[by - 1] + token[0, 0] * 0, 1, by) for by in (1, 2, 3)]
    parcels = (own, *zero, *one)
    pieces = spread(first_sum(place, parcels), "y")
    base = turn(place, parcels)
    residual, x3 = lower_step(base[2], pieces, early, 0, BF16)
    over_z = spread(residual, "z")
    pieces = spread(diag_step(over_z, early, 1), "y")
    base1, _ = lower_step(base[1], (x3,), early, 2, F32)
    residual, x2 = lower_step(base1, pieces, early, 3, BF16)
    over_z = spread(residual, "z")
    pieces = spread(diag_step(over_z, early, 4), "y")
    base0, _ = lower_step(base[0], (x3,), late, 0, F32)
    base0, _ = lower_step(base0, (x2,), late, 1, F32)
    residual, x1 = lower_step(base0, pieces, late, 2, BF16)
    over_z = spread(residual, "z")
    packed, still = pack_known(place, slots_of(named), (x1, x2, x3))
    rows = deal(last_step(place, over_z, late, 3), "y")
    packed = pack_last(still, rows, packed).reshape(128, 16, 128)
    received = lax.all_to_all(
        packed, ("z", "core", "y", "x"), split_axis=0, concat_axis=0, tiled=True
    )
    return unpack(received)


def solution(mesh):
    fine = Mesh(mesh.devices.reshape(4, 2, 4, 4), ("z", "core", "y", "x"))
    rows, cols = ("z", "core"), ("y", "x")
    placed = (
        P(None, cols, None),
        P(rows, None),
        P(rows, None, cols),
        P(None, rows, cols),
        P(None, cols, rows),
        P(rows + cols, None, None),
    )
    return jax.shard_map(
        local, mesh=fine, in_specs=placed, out_specs=P(rows + cols, None), check_vma=False
    )
```

```python
import jax
import jax.numpy as jnp
from jax import lax
from jax.experimental import pallas as pl
from jax.experimental.pallas import tpu as pltpu
from jax.sharding import Mesh, PartitionSpec as P

BF16 = jnp.bfloat16
F32 = jnp.float32
VMEM_LIMIT = 48 * 1024 * 1024


def pair_slot(later, earlier):
    return later * (later - 1) // 2 + earlier


def shift(value, axis, by):
    return lax.ppermute(value, axis, [(i, (i + by) % 4) for i in range(4)])


def swap(value):
    return lax.ppermute(value, "core", [(0, 1), (1, 0)])


def spread(value, axis):
    far = shift(value, axis, 2)
    right = shift(value, axis, 1)
    left = shift(value, axis, 3)
    return (value, right, far, left)


def deal(pieces, axis):
    far = shift(pieces[2], axis, 2)
    right = shift(pieces[1], axis, 1)
    left = shift(pieces[3], axis, 3)
    return (pieces[0], right, far, left)


def add_up(refs):
    total = refs[0][...].astype(F32)
    for ref in refs[1:]:
        total = total + ref[...].astype(F32)
    return total


def params(limit=VMEM_LIMIT):
    return pltpu.CompilerParams(vmem_limit_bytes=limit)


def cost(flops, moved):
    return pl.CostEstimate(flops=flops, bytes_accessed=moved, transcendentals=0)


def whole(shape):
    return pl.BlockSpec(shape, lambda *_: (0,) * len(shape))


SCALARS = pl.BlockSpec(memory_space=pltpu.SMEM)
VMEM = pl.BlockSpec(memory_space=pltpu.VMEM)
HBM = pl.BlockSpec(memory_space=pltpu.HBM)


def first_product(place, pieces, mine, other):
    def kernel(place_ref, v0, v1, v2, v3, mine_ref, other_ref, *refs):
        outs, turned = refs[:4], refs[4]
        core, x = place_ref[0], place_ref[2]
        turned[...] = add_up((v0, v1, v2, v3)).T.astype(BF16)
        for step, out in enumerate(outs):
            start = pl.multiple_of(lax.rem(x + step, 4) * 128, 128)
            left = turned[pl.ds(start, 128), :]
            for side, tile in ((core, mine_ref), (1 - core, other_ref)):
                product = jnp.dot(left, tile[...], preferred_element_type=F32)
                lanes = pl.ds(pl.multiple_of(side * 512, 512), 512)
                out[:, lanes] = product.astype(BF16)

    return pl.pallas_call(
        kernel,
        out_shape=(jax.ShapeDtypeStruct((128, 1024), BF16),) * 4,
        in_specs=[SCALARS] + [VMEM] * 6,
        out_specs=(VMEM,) * 4,
        scratch_shapes=[pltpu.VMEM((512, 256), BF16)],
        compiler_params=params(),
        cost_estimate=cost(2 * 512 * 256 * 1024, 3 << 20),
        name="first_product",
    )(place, *pieces, mine, other)


def turn(place, pieces):
    def kernel(place_ref, v0, v1, v2, v3, out):
        for step, ref in enumerate((v0, v1, v2, v3)):
            start = lax.rem(place_ref[2] + 4 - step, 4) * 256
            lanes = pl.ds(pl.multiple_of(start, 256), 256)
            for k in range(3):
                out[k, :, lanes] = ref[k].astype(F32).T

    return pl.pallas_call(
        kernel,
        out_shape=jax.ShapeDtypeStruct((3, 128, 1024), F32),
        in_specs=[SCALARS] + [VMEM] * 4,
        out_specs=VMEM,
        compiler_params=params(),
        cost_estimate=cost(3 * 128 * 1024, 3 << 20),
        name="turn",
    )(place, *pieces)


def lower_step(base, pieces, tiles, at, dtype):
    count = len(pieces)

    def kernel(*refs):
        parts = refs[:count]
        base_ref, tiles_ref, out, kept, tile, sems = refs[count:]
        copies = [
            pltpu.make_async_copy(
                tiles_ref.at[:, i, pl.ds(at * 512, 512), :], tile.at[:, i], sems.at[i]
            )
            for i in range(4)
        ]
        for copy in copies:
            copy.start()
        kept[...] = add_up(parts).astype(BF16)
        for i, copy in enumerate(copies):
            lanes = slice(i * 256, (i + 1) * 256)
            copy.wait()
            total = base_ref[:, lanes].astype(F32)
            total = total - jnp.dot(kept[:, :512], tile[0, i], preferred_element_type=F32)
            total = total - jnp.dot(kept[:, 512:], tile[1, i], preferred_element_type=F32)
            out[:, lanes] = total.astype(dtype)

    return pl.pallas_call(
        kernel,
        out_shape=(
            jax.ShapeDtypeStruct((128, 1024), dtype),
            jax.ShapeDtypeStruct((128, 1024), BF16),
        ),
        in_specs=[VMEM] * count + [VMEM, HBM],
        out_specs=(VMEM, VMEM),
        scratch_shapes=[
            pltpu.VMEM((2, 4, 512, 256), BF16),
            pltpu.SemaphoreType.DMA((4,)),
        ],
        compiler_params=params(),
        cost_estimate=cost(2 * 128 * 1024 * 1024, 4 << 20),
        name="lower_step",
    )(*pieces, base, tiles)


def fetch_diag(tiles_ref, at, tile, sems):
    copies = [
        pltpu.make_async_copy(
            tiles_ref.at[side, :, pl.ds(at * 512, 512), :], tile.at[side], sems.at[side]
        )
        for side in range(2)
    ]
    for copy in copies:
        copy.start()
    return copies


def times_fetched(copies, vec, tile, out):
    for side, copy in enumerate(copies):
        copy.wait()
        for half in range(2):
            rows = slice(half * 256, (half + 1) * 256)
            total = None
            for x in range(4):
                left = vec[:, x * 256 : (x + 1) * 256]
                term = jnp.dot(left, tile[side, x, rows], preferred_element_type=F32)
                total = term if total is None else total + term
            start = side * 512 + half * 256
            out[:, start : start + 256] = total.astype(BF16)


DIAG_SCRATCH = [
    pltpu.VMEM((128, 1024), BF16),
    pltpu.VMEM((2, 4, 512, 256), BF16),
    pltpu.SemaphoreType.DMA((2,)),
]


def diag_step(pieces, tiles, at):
    def kernel(v0, v1, v2, v3, tiles_ref, out, vec, tile, sems):
        copies = fetch_diag(tiles_ref, at, tile, sems)
        vec[...] = add_up((v0, v1, v2, v3)).astype(BF16)
        times_fetched(copies, vec, tile, out)

    return pl.pallas_call(
        kernel,
        out_shape=jax.ShapeDtypeStruct((128, 1024), BF16),
        in_specs=[VMEM] * 4 + [HBM],
        out_specs=VMEM,
        scratch_shapes=DIAG_SCRATCH,
        compiler_params=params(),
        cost_estimate=cost(2 * 128 * 1024 * 1024, 4 << 20),
        name="diag_step",
    )(*pieces, tiles)


def last_step(place, pieces, tiles, at):
    def kernel(place_ref, v0, v1, v2, v3, tiles_ref, o0, o1, o2, o3, vec, tile, sems, full):
        copies = fetch_diag(tiles_ref, at, tile, sems)
        vec[...] = add_up((v0, v1, v2, v3)).astype(BF16)
        times_fetched(copies, vec, tile, full)
        for by, out in enumerate((o0, o1, o2, o3)):
            start = lax.rem(place_ref[1] + by, 4) * 128
            out[:, :128] = full[:, pl.ds(pl.multiple_of(start, 128), 128)]
            out[:, 128:] = full[:, pl.ds(pl.multiple_of(start + 512, 128), 128)]

    return pl.pallas_call(
        kernel,
        out_shape=(jax.ShapeDtypeStruct((128, 256), BF16),) * 4,
        in_specs=[SCALARS] + [VMEM] * 4 + [HBM],
        out_specs=(VMEM,) * 4,
        scratch_shapes=DIAG_SCRATCH + [pltpu.VMEM((128, 1024), BF16)],
        compiler_params=params(52 * 1024 * 1024),
        cost_estimate=cost(2 * 128 * 1024 * 1024, 4 << 20),
        name="last_step",
    )(place, *pieces, tiles)


def stage(lower_tiles, inverse_diag, orders, owners):
    moves = []
    for number, order in enumerate(orders):
        for at, (kind, index) in enumerate(order):
            if kind == "L":
                moves.append((0, index, slice(None), number, at * 512, 512))
            else:
                moves.append((1, index, slice(0, 256), number, at * 512, 256))
                moves.append((1, index, slice(256, 512), number, at * 512 + 256, 256))
    heights = [512 * len(order) for order in orders]
    heights[-1] += 16
    count = len(orders)

    def kernel(lower_ref, diag_ref, owners_ref, *refs):
        outs, held, sems = refs[:count], refs[count : 2 * count], refs[2 * count]
        plan = [
            ((lower_ref, diag_ref)[which].at[index, :, lanes], number, pl.ds(start, height))
            for which, index, lanes, number, start, height in moves
        ]
        plan.append((owners_ref, count - 1, pl.ds(heights[-1] - 16, 16)))
        into, onward = [], []
        for at, (source, number, where) in enumerate(plan):
            middle = held[number].at[where]
            into.append(pltpu.make_async_copy(source, middle, sems.at[0, at]))
            onward.append(pltpu.make_async_copy(middle, outs[number].at[where], sems.at[1, at]))
        for copy in into:
            copy.start()
        for first, second in zip(into, onward):
            first.wait()
            second.start()
        for copy in onward:
            copy.wait()

    return pl.pallas_call(
        kernel,
        out_shape=tuple(jax.ShapeDtypeStruct((height, 256), BF16) for height in heights),
        in_specs=[HBM] * 3,
        out_specs=(HBM,) * count,
        scratch_shapes=[pltpu.VMEM((height, 256), BF16) for height in heights]
        + [pltpu.SemaphoreType.DMA((2, len(moves) + 1))],
        compiler_params=params(60 * 1024 * 1024),
        cost_estimate=cost(0, 6 << 20),
        name="stage",
    )(lower_tiles, inverse_diag, owners)


def chosen(target, block):
    slots = lax.broadcasted_iota(jnp.int32, (256, 256), 0) + block * 256
    return jnp.where(slots == target, 1.0, 0.0).astype(BF16)


def picked(select, rows):
    return lax.dot_general(
        select, rows, (((1,), (1,)), ((), ())), preferred_element_type=F32
    )


def pack_known(place, target, known):
    def kernel(place_ref, target_ref, x1, x2, x3, out, still):
        block = pl.program_id(0)
        start = pl.multiple_of(place_ref[1] * 128, 128)
        again = pl.multiple_of(place_ref[1] * 128 + 512, 128)
        total = jnp.zeros((256, 128), F32)
        for k, ref in ((1, x1), (2, x2), (3, x3)):
            rows = jnp.concatenate([ref[:, pl.ds(start, 128)], ref[:, pl.ds(again, 128)]], axis=1)
            total = total + picked(chosen(target_ref[k], block), rows)
        out[...] = total.astype(BF16)
        still[...] = chosen(target_ref[0], block)

    return pl.pallas_call(
        kernel,
        grid=(8,),
        out_shape=(
            jax.ShapeDtypeStruct((2048, 128), BF16),
            jax.ShapeDtypeStruct((2048, 256), BF16),
        ),
        in_specs=[SCALARS, whole((4, 1, 256))] + [whole((128, 1024))] * 3,
        out_specs=(
            pl.BlockSpec((256, 128), lambda i: (i, 0)),
            pl.BlockSpec((256, 256), lambda i: (i, 0)),
        ),
        compiler_params=params(),
        cost_estimate=cost(2 * 2048 * 768 * 128, 2 << 20),
        name="pack_known",
    )(place, target, *known)


def pack_last(still, pieces, base):
    def kernel(still_ref, v0, v1, v2, v3, base_ref, out):
        rows = add_up((v0, v1, v2, v3)).astype(BF16)
        out[...] = (base_ref[...].astype(F32) + picked(still_ref[...], rows)).astype(BF16)

    return pl.pallas_call(
        kernel,
        out_shape=jax.ShapeDtypeStruct((2048, 128), BF16),
        in_specs=[VMEM] * 6,
        out_specs=VMEM,
        compiler_params=params(),
        cost_estimate=cost(2 * 2048 * 256 * 128, 2 << 20),
        name="pack_last",
    )(still, *pieces, base)


def unpack(received):
    def kernel(got, out):
        for core in range(2):
            for y in range(4):
                for x in range(4):
                    tile = got[0, core, y, x].astype(F32)
                    lanes = pl.ds((core * 4 + x) * 128, 128)
                    for half in range(2):
                        out[pl.ds(half * 32 + y * 8, 8), lanes] = tile[half * 8 : half * 8 + 8]

    return pl.pallas_call(
        kernel,
        grid=(4,),
        out_shape=jax.ShapeDtypeStruct((256, 1024), F32),
        in_specs=[pl.BlockSpec((1, 2, 4, 4, 16, 128), lambda i: (i, 0, 0, 0, 0, 0))],
        out_specs=pl.BlockSpec((64, 1024), lambda i: (i, 0)),
        compiler_params=params(),
        cost_estimate=cost(256 * 1024, 2 << 20),
        name="unpack",
    )(received.reshape(4, 2, 4, 4, 16, 128))


def slots_of(named):
    same = named[:, :, None] == named[:, None, :]
    earlier = jnp.arange(128)[None, :, None] > jnp.arange(128)[None, None, :]
    ranks = jnp.sum((same & earlier).astype(jnp.int32), axis=2)
    target = named * 16 + jnp.arange(8, dtype=jnp.int32)[:, None] * 2 + ranks
    return target.reshape(8, 4, 32).transpose(1, 0, 2).reshape(4, 1, 256)


def gathered(joined):
    rows = joined.shape[0]
    return lax.all_gather(joined, ("core", "x"), axis=0, tiled=False).reshape(2, 4, rows, 256)


def local(pivot_rhs, bound_sol, border_tiles, lower_tiles, inverse_diag, owner_map):
    z, core, y, x = (lax.axis_index(name) for name in ("z", "core", "y", "x"))
    place = jnp.stack([core, y, x, z]).astype(jnp.int32)
    lead = jnp.where((z == 0) & (core == 0), 1.0, 0.0).astype(F32)

    def tile(j, k):
        return ("L", pair_slot(j, k))

    owners = jnp.pad(owner_map[0, :, 0].astype(BF16)[None], ((0, 15), (0, 128)))
    orders = [
        [tile(3, 2), ("D", 2), tile(3, 1), tile(2, 1), ("D", 1)],
        [tile(3, 0), tile(2, 0), tile(1, 0), ("D", 0)],
    ]
    early, late = map(gathered, stage(lower_tiles, inverse_diag, orders, owners))
    named = late[:, :, 2048, :128].astype(jnp.int32).reshape(8, 128)
    other = swap(inverse_diag[3])

    def term(side):
        start = side * 512
        rhs = lax.dynamic_slice_in_dim(pivot_rhs, start, 512, axis=2)
        bound = lax.dynamic_slice_in_dim(bound_sol, start, 512, axis=1)
        product = lax.dot_general(
            border_tiles, bound, (((0,), (0,)), ((), ())), preferred_element_type=F32
        )
        return (lead * rhs - product).astype(BF16)

    away = swap(term(1 - core))
    home = lax.optimization_barrier(term(core))
    both = (home.astype(F32) + away.astype(F32)).astype(BF16)
    over_z = spread(both[3], "z")
    products = first_product(place, over_z, inverse_diag[3], other)
    rest = both[:3] + over_z[1][0, 0] * 0
    cut = [
        lax.dynamic_slice_in_dim(rest, lax.rem(x + by, 4) * 128, 128, axis=2) for by in range(4)
    ]
    base = turn(place, deal(cut, "x"))
    over_x = deal(products, "x")
    partial = sum(piece.astype(F32) for piece in over_x).astype(BF16)
    pieces = spread(partial, "y")
    residual, x3 = lower_step(base[2], pieces, early, 0, BF16)
    over_z = spread(residual, "z")
    pieces = spread(diag_step(over_z, early, 1), "y")
    base1, _ = lower_step(base[1], (x3,), early, 2, F32)
    residual, x2 = lower_step(base1, pieces, early, 3, BF16)
    over_z = spread(residual, "z")
    pieces = spread(diag_step(over_z, early, 4), "y")
    base0, _ = lower_step(base[0], (x3,), late, 0, F32)
    base0, _ = lower_step(base0, (x2,), late, 1, F32)
    residual, x1 = lower_step(base0, pieces, late, 2, BF16)
    over_z = spread(residual, "z")
    packed, still = pack_known(place, slots_of(named), (x1, x2, x3))
    rows = deal(last_step(place, over_z, late, 3), "y")
    packed = pack_last(still, rows, packed).reshape(128, 16, 128)
    received = lax.all_to_all(
        packed, ("z", "core", "y", "x"), split_axis=0, concat_axis=0, tiled=True
    )
    return unpack(received)


def solution(mesh):
    fine = Mesh(mesh.devices.reshape(4, 2, 4, 4), ("z", "core", "y", "x"))
    rows, cols = ("z", "core"), ("y", "x")
    placed = (
        P(None, cols, None),
        P(rows, None),
        P(rows, None, cols),
        P(None, rows, cols),
        P(None, cols, rows),
        P(rows + cols, None, None),
    )
    return jax.shard_map(
        local, mesh=fine, in_specs=placed, out_specs=P(rows + cols, None), check_vma=False
    )
```

```python
import jax
import jax.numpy as jnp
from jax import lax
from jax.experimental import pallas as pl
from jax.experimental.pallas import tpu as pltpu
from jax.sharding import Mesh, PartitionSpec as P

BF16 = jnp.bfloat16
F32 = jnp.float32
VMEM_LIMIT = 48 * 1024 * 1024


def pair_slot(later, earlier):
    return later * (later - 1) // 2 + earlier


def shift(value, axis, by):
    return lax.ppermute(value, axis, [(i, (i + by) % 4) for i in range(4)])


def swap(value):
    return lax.ppermute(value, "core", [(0, 1), (1, 0)])


def spread(value, axis):
    far = shift(value, axis, 2)
    right = shift(value, axis, 1)
    left = shift(value, axis, 3)
    return (value, right, far, left)


def deal(pieces, axis):
    far = shift(pieces[2], axis, 2)
    right = shift(pieces[1], axis, 1)
    left = shift(pieces[3], axis, 3)
    return (pieces[0], right, far, left)


def add_up(refs):
    total = refs[0][...].astype(F32)
    for ref in refs[1:]:
        total = total + ref[...].astype(F32)
    return total


def params(limit=VMEM_LIMIT):
    return pltpu.CompilerParams(vmem_limit_bytes=limit)


def cost(flops, moved):
    return pl.CostEstimate(flops=flops, bytes_accessed=moved, transcendentals=0)


def whole(shape):
    return pl.BlockSpec(shape, lambda *_: (0,) * len(shape))


SCALARS = pl.BlockSpec(memory_space=pltpu.SMEM)
VMEM = pl.BlockSpec(memory_space=pltpu.VMEM)
HBM = pl.BlockSpec(memory_space=pltpu.HBM)


def first_product(place, pieces, mine, other):
    def kernel(place_ref, v0, v1, v2, v3, mine_ref, other_ref, *refs):
        outs, turned = refs[:4], refs[4]
        core, x = place_ref[0], place_ref[2]
        turned[...] = add_up((v0, v1, v2, v3)).T.astype(BF16)
        for step, out in enumerate(outs):
            start = pl.multiple_of(lax.rem(x + step, 4) * 128, 128)
            left = turned[pl.ds(start, 128), :]
            for side, tile in ((core, mine_ref), (1 - core, other_ref)):
                product = jnp.dot(left, tile[...], preferred_element_type=F32)
                lanes = pl.ds(pl.multiple_of(side * 512, 512), 512)
                out[:, lanes] = product.astype(BF16)

    return pl.pallas_call(
        kernel,
        out_shape=(jax.ShapeDtypeStruct((128, 1024), BF16),) * 4,
        in_specs=[SCALARS] + [VMEM] * 6,
        out_specs=(VMEM,) * 4,
        scratch_shapes=[pltpu.VMEM((512, 256), BF16)],
        compiler_params=params(),
        cost_estimate=cost(2 * 512 * 256 * 1024, 3 << 20),
        name="first_product",
    )(place, *pieces, mine, other)


def turn(place, pieces):
    def kernel(place_ref, v0, v1, v2, v3, out):
        for step, ref in enumerate((v0, v1, v2, v3)):
            start = lax.rem(place_ref[2] + 4 - step, 4) * 256
            lanes = pl.ds(pl.multiple_of(start, 256), 256)
            for k in range(3):
                out[k, :, lanes] = ref[k].astype(F32).T

    return pl.pallas_call(
        kernel,
        out_shape=jax.ShapeDtypeStruct((3, 128, 1024), F32),
        in_specs=[SCALARS] + [VMEM] * 4,
        out_specs=VMEM,
        compiler_params=params(),
        cost_estimate=cost(3 * 128 * 1024, 3 << 20),
        name="turn",
    )(place, *pieces)


def lower_step(base, pieces, tiles, at, dtype):
    count = len(pieces)

    def kernel(*refs):
        parts = refs[:count]
        base_ref, tiles_ref, out, kept, tile, sems = refs[count:]
        copies = [
            pltpu.make_async_copy(
                tiles_ref.at[:, i, pl.ds(at * 512, 512), :], tile.at[:, i], sems.at[i]
            )
            for i in range(4)
        ]
        for copy in copies:
            copy.start()
        kept[...] = add_up(parts).astype(BF16)
        for i, copy in enumerate(copies):
            lanes = slice(i * 256, (i + 1) * 256)
            copy.wait()
            total = base_ref[:, lanes].astype(F32)
            total = total - jnp.dot(kept[:, :512], tile[0, i], preferred_element_type=F32)
            total = total - jnp.dot(kept[:, 512:], tile[1, i], preferred_element_type=F32)
            out[:, lanes] = total.astype(dtype)

    return pl.pallas_call(
        kernel,
        out_shape=(
            jax.ShapeDtypeStruct((128, 1024), dtype),
            jax.ShapeDtypeStruct((128, 1024), BF16),
        ),
        in_specs=[VMEM] * count + [VMEM, HBM],
        out_specs=(VMEM, VMEM),
        scratch_shapes=[
            pltpu.VMEM((2, 4, 512, 256), BF16),
            pltpu.SemaphoreType.DMA((4,)),
        ],
        compiler_params=params(),
        cost_estimate=cost(2 * 128 * 1024 * 1024, 4 << 20),
        name="lower_step",
    )(*pieces, base, tiles)


def fetch_diag(tiles_ref, at, tile, sems):
    copies = [
        pltpu.make_async_copy(
            tiles_ref.at[side, :, pl.ds(at * 512, 512), :], tile.at[side], sems.at[side]
        )
        for side in range(2)
    ]
    for copy in copies:
        copy.start()
    return copies


def times_fetched(copies, vec, tile, out):
    for side, copy in enumerate(copies):
        copy.wait()
        for half in range(2):
            rows = slice(half * 256, (half + 1) * 256)
            total = None
            for x in range(4):
                left = vec[:, x * 256 : (x + 1) * 256]
                term = jnp.dot(left, tile[side, x, rows], preferred_element_type=F32)
                total = term if total is None else total + term
            start = side * 512 + half * 256
            out[:, start : start + 256] = total.astype(BF16)


DIAG_SCRATCH = [
    pltpu.VMEM((128, 1024), BF16),
    pltpu.VMEM((2, 4, 512, 256), BF16),
    pltpu.SemaphoreType.DMA((2,)),
]


def diag_step(pieces, tiles, at):
    def kernel(v0, v1, v2, v3, tiles_ref, out, vec, tile, sems):
        copies = fetch_diag(tiles_ref, at, tile, sems)
        vec[...] = add_up((v0, v1, v2, v3)).astype(BF16)
        times_fetched(copies, vec, tile, out)

    return pl.pallas_call(
        kernel,
        out_shape=jax.ShapeDtypeStruct((128, 1024), BF16),
        in_specs=[VMEM] * 4 + [HBM],
        out_specs=VMEM,
        scratch_shapes=DIAG_SCRATCH,
        compiler_params=params(),
        cost_estimate=cost(2 * 128 * 1024 * 1024, 4 << 20),
        name="diag_step",
    )(*pieces, tiles)


def last_step(place, pieces, tiles, at):
    def kernel(place_ref, v0, v1, v2, v3, tiles_ref, o0, o1, o2, o3, vec, tile, sems, full):
        copies = fetch_diag(tiles_ref, at, tile, sems)
        vec[...] = add_up((v0, v1, v2, v3)).astype(BF16)
        times_fetched(copies, vec, tile, full)
        for by, out in enumerate((o0, o1, o2, o3)):
            start = lax.rem(place_ref[1] + by, 4) * 128
            out[:, :128] = full[:, pl.ds(pl.multiple_of(start, 128), 128)]
            out[:, 128:] = full[:, pl.ds(pl.multiple_of(start + 512, 128), 128)]

    return pl.pallas_call(
        kernel,
        out_shape=(jax.ShapeDtypeStruct((128, 256), BF16),) * 4,
        in_specs=[SCALARS] + [VMEM] * 4 + [HBM],
        out_specs=(VMEM,) * 4,
        scratch_shapes=DIAG_SCRATCH + [pltpu.VMEM((128, 1024), BF16)],
        compiler_params=params(52 * 1024 * 1024),
        cost_estimate=cost(2 * 128 * 1024 * 1024, 4 << 20),
        name="last_step",
    )(place, *pieces, tiles)


def stage(lower_tiles, inverse_diag, orders, owners):
    moves = []
    for number, order in enumerate(orders):
        for at, (kind, index) in enumerate(order):
            if kind == "L":
                moves.append((0, index, slice(None), number, at * 512, 512))
            else:
                moves.append((1, index, slice(0, 256), number, at * 512, 256))
                moves.append((1, index, slice(256, 512), number, at * 512 + 256, 256))
    heights = [512 * len(order) for order in orders]
    heights[-1] += 16
    count = len(orders)

    def kernel(lower_ref, diag_ref, owners_ref, *refs):
        outs, held, sems = refs[:count], refs[count : 2 * count], refs[2 * count]
        plan = [
            ((lower_ref, diag_ref)[which].at[index, :, lanes], number, pl.ds(start, height))
            for which, index, lanes, number, start, height in moves
        ]
        named = pl.ds(heights[-1] - 16, 16)
        spread_out = jnp.broadcast_to(owners_ref[...].astype(F32), (16, 128)).astype(BF16)
        held[-1][named, :128] = spread_out
        held[-1][named, 128:] = jnp.zeros((16, 128), BF16)
        into, onward = [], []
        for at, (source, number, where) in enumerate(plan):
            middle = held[number].at[where]
            into.append(pltpu.make_async_copy(source, middle, sems.at[0, at]))
            onward.append(pltpu.make_async_copy(middle, outs[number].at[where], sems.at[1, at]))
        last = pltpu.make_async_copy(
            held[-1].at[named], outs[-1].at[named], sems.at[1, len(moves)]
        )
        for copy in into:
            copy.start()
        last.start()
        for first, second in zip(into, onward):
            first.wait()
            second.start()
        for copy in onward:
            copy.wait()
        last.wait()

    return pl.pallas_call(
        kernel,
        out_shape=tuple(jax.ShapeDtypeStruct((height, 256), BF16) for height in heights),
        in_specs=[HBM, HBM, VMEM],
        out_specs=(HBM,) * count,
        scratch_shapes=[pltpu.VMEM((height, 256), BF16) for height in heights]
        + [pltpu.SemaphoreType.DMA((2, len(moves) + 1))],
        compiler_params=params(60 * 1024 * 1024),
        cost_estimate=cost(0, 6 << 20),
        name="stage",
    )(lower_tiles, inverse_diag, owners)


def chosen(target, block):
    slots = lax.broadcasted_iota(jnp.int32, (256, 256), 0) + block * 256
    return jnp.where(slots == target, 1.0, 0.0).astype(BF16)


def picked(select, rows):
    return lax.dot_general(
        select, rows, (((1,), (1,)), ((), ())), preferred_element_type=F32
    )


def pack_known(place, target, known):
    def kernel(place_ref, target_ref, x1, x2, x3, out, still):
        block = pl.program_id(0)
        start = pl.multiple_of(place_ref[1] * 128, 128)
        again = pl.multiple_of(place_ref[1] * 128 + 512, 128)
        total = jnp.zeros((256, 128), F32)
        for k, ref in ((1, x1), (2, x2), (3, x3)):
            rows = jnp.concatenate([ref[:, pl.ds(start, 128)], ref[:, pl.ds(again, 128)]], axis=1)
            total = total + picked(chosen(target_ref[k], block), rows)
        out[...] = total.astype(BF16)
        still[...] = chosen(target_ref[0], block)

    return pl.pallas_call(
        kernel,
        grid=(8,),
        out_shape=(
            jax.ShapeDtypeStruct((2048, 128), BF16),
            jax.ShapeDtypeStruct((2048, 256), BF16),
        ),
        in_specs=[SCALARS, whole((4, 1, 256))] + [whole((128, 1024))] * 3,
        out_specs=(
            pl.BlockSpec((256, 128), lambda i: (i, 0)),
            pl.BlockSpec((256, 256), lambda i: (i, 0)),
        ),
        compiler_params=params(),
        cost_estimate=cost(2 * 2048 * 768 * 128, 2 << 20),
        name="pack_known",
    )(place, target, *known)


def pack_last(still, pieces, base):
    def kernel(still_ref, v0, v1, v2, v3, base_ref, out):
        rows = add_up((v0, v1, v2, v3)).astype(BF16)
        out[...] = (base_ref[...].astype(F32) + picked(still_ref[...], rows)).astype(BF16)

    return pl.pallas_call(
        kernel,
        out_shape=jax.ShapeDtypeStruct((2048, 128), BF16),
        in_specs=[VMEM] * 6,
        out_specs=VMEM,
        compiler_params=params(),
        cost_estimate=cost(2 * 2048 * 256 * 128, 2 << 20),
        name="pack_last",
    )(still, *pieces, base)


def unpack(received):
    def kernel(got, out):
        for core in range(2):
            for y in range(4):
                for x in range(4):
                    tile = got[0, core, y, x].astype(F32)
                    lanes = pl.ds((core * 4 + x) * 128, 128)
                    for half in range(2):
                        out[pl.ds(half * 32 + y * 8, 8), lanes] = tile[half * 8 : half * 8 + 8]

    return pl.pallas_call(
        kernel,
        grid=(4,),
        out_shape=jax.ShapeDtypeStruct((256, 1024), F32),
        in_specs=[pl.BlockSpec((1, 2, 4, 4, 16, 128), lambda i: (i, 0, 0, 0, 0, 0))],
        out_specs=pl.BlockSpec((64, 1024), lambda i: (i, 0)),
        compiler_params=params(),
        cost_estimate=cost(256 * 1024, 2 << 20),
        name="unpack",
    )(received.reshape(4, 2, 4, 4, 16, 128))


def slots_of(named):
    same = named[:, :, None] == named[:, None, :]
    earlier = jnp.arange(128)[None, :, None] > jnp.arange(128)[None, None, :]
    ranks = jnp.sum((same & earlier).astype(jnp.int32), axis=2)
    target = named * 16 + jnp.arange(8, dtype=jnp.int32)[:, None] * 2 + ranks
    return target.reshape(8, 4, 32).transpose(1, 0, 2).reshape(4, 1, 256)


def gathered(joined):
    rows = joined.shape[0]
    return lax.all_gather(joined, ("core", "x"), axis=0, tiled=False).reshape(2, 4, rows, 256)


def local(pivot_rhs, bound_sol, border_tiles, lower_tiles, inverse_diag, owner_map):
    z, core, y, x = (lax.axis_index(name) for name in ("z", "core", "y", "x"))
    place = jnp.stack([core, y, x, z]).astype(jnp.int32)
    lead = jnp.where((z == 0) & (core == 0), 1.0, 0.0).astype(F32)

    def tile(j, k):
        return ("L", pair_slot(j, k))

    owners = owner_map[:, :, 0]
    orders = [
        [tile(3, 2), ("D", 2)],
        [tile(3, 1), tile(2, 1), ("D", 1)],
        [tile(3, 0), tile(2, 0), tile(1, 0), ("D", 0)],
    ]
    early, middle, late = map(gathered, stage(lower_tiles, inverse_diag, orders, owners))
    named = late[:, :, 2048, :128].astype(jnp.int32).reshape(8, 128)
    other = swap(inverse_diag[3])

    def term(side):
        start = side * 512
        rhs = lax.dynamic_slice_in_dim(pivot_rhs, start, 512, axis=2)
        bound = lax.dynamic_slice_in_dim(bound_sol, start, 512, axis=1)
        product = lax.dot_general(
            border_tiles, bound, (((0,), (0,)), ((), ())), preferred_element_type=F32
        )
        return (lead * rhs - product).astype(BF16)

    away = swap(term(1 - core))
    home = lax.optimization_barrier(term(core))
    both = (home.astype(F32) + away.astype(F32)).astype(BF16)
    over_z = spread(both[3], "z")
    products = first_product(place, over_z, inverse_diag[3], other)
    rest = both[:3] + over_z[1][0, 0] * 0
    cut = [
        lax.dynamic_slice_in_dim(rest, lax.rem(x + by, 4) * 128, 128, axis=2) for by in range(4)
    ]
    base = turn(place, deal(cut, "x"))
    over_x = deal(products, "x")
    partial = sum(piece.astype(F32) for piece in over_x).astype(BF16)
    pieces = spread(partial, "y")
    residual, x3 = lower_step(base[2], pieces, early, 0, BF16)
    over_z = spread(residual, "z")
    pieces = spread(diag_step(over_z, early, 1), "y")
    base1, _ = lower_step(base[1], (x3,), middle, 0, F32)
    residual, x2 = lower_step(base1, pieces, middle, 1, BF16)
    over_z = spread(residual, "z")
    pieces = spread(diag_step(over_z, middle, 2), "y")
    base0, _ = lower_step(base[0], (x3,), late, 0, F32)
    base0, _ = lower_step(base0, (x2,), late, 1, F32)
    residual, x1 = lower_step(base0, pieces, late, 2, BF16)
    over_z = spread(residual, "z")
    packed, still = pack_known(place, slots_of(named), (x1, x2, x3))
    rows = deal(last_step(place, over_z, late, 3), "y")
    packed = pack_last(still, rows, packed).reshape(128, 16, 128)
    received = lax.all_to_all(
        packed, ("z", "core", "y", "x"), split_axis=0, concat_axis=0, tiled=True
    )
    return unpack(received)


def solution(mesh):
    fine = Mesh(mesh.devices.reshape(4, 2, 4, 4), ("z", "core", "y", "x"))
    rows, cols = ("z", "core"), ("y", "x")
    placed = (
        P(None, cols, None),
        P(rows, None),
        P(rows, None, cols),
        P(None, rows, cols),
        P(None, cols, rows),
        P(rows + cols, None, None),
    )
    return jax.shard_map(
        local, mesh=fine, in_specs=placed, out_specs=P(rows + cols, None), check_vma=False
    )
```

```python
import jax
import jax.numpy as jnp
from jax import lax
from jax.experimental import pallas as pl
from jax.experimental.pallas import tpu as pltpu
from jax.sharding import Mesh, PartitionSpec as P

BF16 = jnp.bfloat16
F32 = jnp.float32
VMEM_LIMIT = 48 * 1024 * 1024


def pair_slot(later, earlier):
    return later * (later - 1) // 2 + earlier


def shift(value, axis, by):
    return lax.ppermute(value, axis, [(i, (i + by) % 4) for i in range(4)])


def swap(value):
    return lax.ppermute(value, "core", [(0, 1), (1, 0)])


def along_x(value, core, by):
    pairs = [(core * 4 + i, core * 4 + (i + by) % 4) for i in range(4)]
    return lax.ppermute(value, ("core", "x"), pairs)


def spread(value, axis):
    far = shift(value, axis, 2)
    right = shift(value, axis, 1)
    left = shift(value, axis, 3)
    return (value, right, far, left)


def deal(pieces, axis):
    far = shift(pieces[2], axis, 2)
    right = shift(pieces[1], axis, 1)
    left = shift(pieces[3], axis, 3)
    return (pieces[0], right, far, left)


def add_up(refs):
    total = refs[0][...].astype(F32)
    for ref in refs[1:]:
        total = total + ref[...].astype(F32)
    return total


def params(limit=VMEM_LIMIT):
    return pltpu.CompilerParams(vmem_limit_bytes=limit)


def cost(flops, moved):
    return pl.CostEstimate(flops=flops, bytes_accessed=moved, transcendentals=0)


def whole(shape):
    return pl.BlockSpec(shape, lambda *_: (0,) * len(shape))


SCALARS = pl.BlockSpec(memory_space=pltpu.SMEM)
VMEM = pl.BlockSpec(memory_space=pltpu.VMEM)
HBM = pl.BlockSpec(memory_space=pltpu.HBM)


def first_product(place, pieces, mine, other, sent):
    def kernel(place_ref, v0, v1, v2, v3, mine_ref, other_ref, *refs):
        outs, turned = refs[len(sent) : len(sent) + 4], refs[len(sent) + 4]
        core, x = place_ref[0], place_ref[2]
        turned[...] = add_up((v0, v1, v2, v3)).T.astype(BF16)
        for step, out in enumerate(outs):
            start = pl.multiple_of(lax.rem(x + step, 4) * 128, 128)
            left = turned[pl.ds(start, 128), :]
            for side, tile in ((core, mine_ref), (1 - core, other_ref)):
                product = jnp.dot(left, tile[...], preferred_element_type=F32)
                lanes = pl.ds(pl.multiple_of(side * 512, 512), 512)
                out[:, lanes] = product.astype(BF16)

    return pl.pallas_call(
        kernel,
        out_shape=(jax.ShapeDtypeStruct((128, 1024), BF16),) * 4,
        in_specs=[SCALARS] + [VMEM] * 6 + [pl.BlockSpec(memory_space=pl.ANY)] * len(sent),
        out_specs=(VMEM,) * 4,
        scratch_shapes=[pltpu.VMEM((512, 256), BF16)],
        compiler_params=params(),
        cost_estimate=cost(2 * 512 * 256 * 1024, 3 << 20),
        name="first_product",
    )(place, *pieces, mine, other, *sent)


def gate(token, arrays):
    def kernel(*refs):
        pass

    count = len(arrays)
    return pl.pallas_call(
        kernel,
        out_shape=tuple(jax.ShapeDtypeStruct(value.shape, value.dtype) for value in arrays),
        in_specs=[pl.BlockSpec(memory_space=pl.ANY)] * (count + 1),
        out_specs=(pl.BlockSpec(memory_space=pl.ANY),) * count,
        input_output_aliases={i + 1: i for i in range(count)},
        compiler_params=params(),
        cost_estimate=cost(0, 1024),
        name="gate",
    )(token, *arrays)


def turn(place, pieces):
    def kernel(place_ref, v0, v1, v2, v3, out):
        for step, ref in enumerate((v0, v1, v2, v3)):
            start = lax.rem(place_ref[2] + 4 - step, 4) * 256
            lanes = pl.ds(pl.multiple_of(start, 256), 256)
            for k in range(3):
                out[k, :, lanes] = ref[k].astype(F32).T

    return pl.pallas_call(
        kernel,
        out_shape=jax.ShapeDtypeStruct((3, 128, 1024), F32),
        in_specs=[SCALARS] + [VMEM] * 4,
        out_specs=VMEM,
        compiler_params=params(),
        cost_estimate=cost(3 * 128 * 1024, 3 << 20),
        name="turn",
    )(place, *pieces)


def lower_step(base, pieces, tiles, at, dtype):
    count = len(pieces)

    def kernel(*refs):
        parts = refs[:count]
        base_ref, tiles_ref, out, kept, tile, sems = refs[count:]
        copies = [
            pltpu.make_async_copy(
                tiles_ref.at[:, i, pl.ds(at * 512, 512), :], tile.at[:, i], sems.at[i]
            )
            for i in range(4)
        ]
        for copy in copies:
            copy.start()
        kept[...] = add_up(parts).astype(BF16)
        for i, copy in enumerate(copies):
            lanes = slice(i * 256, (i + 1) * 256)
            copy.wait()
            total = base_ref[:, lanes].astype(F32)
            total = total - jnp.dot(kept[:, :512], tile[0, i], preferred_element_type=F32)
            total = total - jnp.dot(kept[:, 512:], tile[1, i], preferred_element_type=F32)
            out[:, lanes] = total.astype(dtype)

    return pl.pallas_call(
        kernel,
        out_shape=(
            jax.ShapeDtypeStruct((128, 1024), dtype),
            jax.ShapeDtypeStruct((128, 1024), BF16),
        ),
        in_specs=[VMEM] * count + [VMEM, HBM],
        out_specs=(VMEM, VMEM),
        scratch_shapes=[
            pltpu.VMEM((2, 4, 512, 256), BF16),
            pltpu.SemaphoreType.DMA((4,)),
        ],
        compiler_params=params(),
        cost_estimate=cost(2 * 128 * 1024 * 1024, 4 << 20),
        name="lower_step",
    )(*pieces, base, tiles)


def fetch_diag(tiles_ref, at, tile, sems):
    copies = [
        pltpu.make_async_copy(
            tiles_ref.at[side, :, pl.ds(at * 512, 512), :], tile.at[side], sems.at[side]
        )
        for side in range(2)
    ]
    for copy in copies:
        copy.start()
    return copies


def times_fetched(copies, vec, tile, out):
    for side, copy in enumerate(copies):
        copy.wait()
        for half in range(2):
            rows = slice(half * 256, (half + 1) * 256)
            total = None
            for x in range(4):
                left = vec[:, x * 256 : (x + 1) * 256]
                term = jnp.dot(left, tile[side, x, rows], preferred_element_type=F32)
                total = term if total is None else total + term
            start = side * 512 + half * 256
            out[:, start : start + 256] = total.astype(BF16)


DIAG_SCRATCH = [
    pltpu.VMEM((128, 1024), BF16),
    pltpu.VMEM((2, 4, 512, 256), BF16),
    pltpu.SemaphoreType.DMA((2,)),
]


def diag_step(pieces, tiles, at):
    def kernel(v0, v1, v2, v3, tiles_ref, out, vec, tile, sems):
        copies = fetch_diag(tiles_ref, at, tile, sems)
        vec[...] = add_up((v0, v1, v2, v3)).astype(BF16)
        times_fetched(copies, vec, tile, out)

    return pl.pallas_call(
        kernel,
        out_shape=jax.ShapeDtypeStruct((128, 1024), BF16),
        in_specs=[VMEM] * 4 + [HBM],
        out_specs=VMEM,
        scratch_shapes=DIAG_SCRATCH,
        compiler_params=params(),
        cost_estimate=cost(2 * 128 * 1024 * 1024, 4 << 20),
        name="diag_step",
    )(*pieces, tiles)


def last_step(place, pieces, tiles, at):
    def kernel(place_ref, v0, v1, v2, v3, tiles_ref, o0, o1, o2, o3, vec, tile, sems, full):
        copies = fetch_diag(tiles_ref, at, tile, sems)
        vec[...] = add_up((v0, v1, v2, v3)).astype(BF16)
        times_fetched(copies, vec, tile, full)
        for by, out in enumerate((o0, o1, o2, o3)):
            start = lax.rem(place_ref[1] + by, 4) * 128
            out[:, :128] = full[:, pl.ds(pl.multiple_of(start, 128), 128)]
            out[:, 128:] = full[:, pl.ds(pl.multiple_of(start + 512, 128), 128)]

    return pl.pallas_call(
        kernel,
        out_shape=(jax.ShapeDtypeStruct((128, 256), BF16),) * 4,
        in_specs=[SCALARS] + [VMEM] * 4 + [HBM],
        out_specs=(VMEM,) * 4,
        scratch_shapes=DIAG_SCRATCH + [pltpu.VMEM((128, 1024), BF16)],
        compiler_params=params(52 * 1024 * 1024),
        cost_estimate=cost(2 * 128 * 1024 * 1024, 4 << 20),
        name="last_step",
    )(place, *pieces, tiles)


def stage(lower_tiles, inverse_diag, orders, owners):
    moves = []
    for number, order in enumerate(orders):
        for at, (kind, index) in enumerate(order):
            if kind == "L":
                moves.append((0, index, slice(None), number, at * 512, 512))
            else:
                moves.append((1, index, slice(0, 256), number, at * 512, 256))
                moves.append((1, index, slice(256, 512), number, at * 512 + 256, 256))
    heights = [512 * len(order) for order in orders]
    heights[-1] += 16
    count = len(orders)

    def kernel(lower_ref, diag_ref, owners_ref, *refs):
        outs, held, sems = refs[:count], refs[count : 2 * count], refs[2 * count]
        plan = [
            ((lower_ref, diag_ref)[which].at[index, :, lanes], number, pl.ds(start, height))
            for which, index, lanes, number, start, height in moves
        ]
        named = pl.ds(heights[-1] - 16, 16)
        spread_out = jnp.broadcast_to(owners_ref[...].astype(F32), (16, 128)).astype(BF16)
        held[-1][named, :128] = spread_out
        held[-1][named, 128:] = jnp.zeros((16, 128), BF16)
        into, onward = [], []
        for at, (source, number, where) in enumerate(plan):
            middle = held[number].at[where]
            into.append(pltpu.make_async_copy(source, middle, sems.at[0, at]))
            onward.append(pltpu.make_async_copy(middle, outs[number].at[where], sems.at[1, at]))
        last = pltpu.make_async_copy(
            held[-1].at[named], outs[-1].at[named], sems.at[1, len(moves)]
        )
        for copy in into:
            copy.start()
        last.start()
        for first, second in zip(into, onward):
            first.wait()
            second.start()
        for copy in onward:
            copy.wait()
        last.wait()

    return pl.pallas_call(
        kernel,
        out_shape=tuple(jax.ShapeDtypeStruct((height, 256), BF16) for height in heights),
        in_specs=[HBM, HBM, VMEM],
        out_specs=(HBM,) * count,
        scratch_shapes=[pltpu.VMEM((height, 256), BF16) for height in heights]
        + [pltpu.SemaphoreType.DMA((2, len(moves) + 1))],
        compiler_params=params(60 * 1024 * 1024),
        cost_estimate=cost(0, 6 << 20),
        name="stage",
    )(lower_tiles, inverse_diag, owners)


def chosen(target, block):
    slots = lax.broadcasted_iota(jnp.int32, (256, 256), 0) + block * 256
    return jnp.where(slots == target, 1.0, 0.0).astype(BF16)


def picked(select, rows):
    return lax.dot_general(
        select, rows, (((1,), (1,)), ((), ())), preferred_element_type=F32
    )


def pack_known(place, target, known):
    def kernel(place_ref, target_ref, x1, x2, x3, out, still):
        block = pl.program_id(0)
        start = pl.multiple_of(place_ref[1] * 128, 128)
        again = pl.multiple_of(place_ref[1] * 128 + 512, 128)
        total = jnp.zeros((256, 128), F32)
        for k, ref in ((1, x1), (2, x2), (3, x3)):
            rows = jnp.concatenate([ref[:, pl.ds(start, 128)], ref[:, pl.ds(again, 128)]], axis=1)
            total = total + picked(chosen(target_ref[k], block), rows)
        out[...] = total.astype(BF16)
        still[...] = chosen(target_ref[0], block)

    return pl.pallas_call(
        kernel,
        grid=(8,),
        out_shape=(
            jax.ShapeDtypeStruct((2048, 128), BF16),
            jax.ShapeDtypeStruct((2048, 256), BF16),
        ),
        in_specs=[SCALARS, whole((4, 1, 256))] + [whole((128, 1024))] * 3,
        out_specs=(
            pl.BlockSpec((256, 128), lambda i: (i, 0)),
            pl.BlockSpec((256, 256), lambda i: (i, 0)),
        ),
        compiler_params=params(),
        cost_estimate=cost(2 * 2048 * 768 * 128, 2 << 20),
        name="pack_known",
    )(place, target, *known)


def pack_last(still, pieces, base):
    def kernel(still_ref, v0, v1, v2, v3, base_ref, out):
        rows = add_up((v0, v1, v2, v3)).astype(BF16)
        out[...] = (base_ref[...].astype(F32) + picked(still_ref[...], rows)).astype(BF16)

    return pl.pallas_call(
        kernel,
        out_shape=jax.ShapeDtypeStruct((2048, 128), BF16),
        in_specs=[VMEM] * 6,
        out_specs=VMEM,
        compiler_params=params(),
        cost_estimate=cost(2 * 2048 * 256 * 128, 2 << 20),
        name="pack_last",
    )(still, *pieces, base)


def unpack(received):
    def kernel(got, out):
        for core in range(2):
            for y in range(4):
                for x in range(4):
                    tile = got[0, core, y, x].astype(F32)
                    lanes = pl.ds((core * 4 + x) * 128, 128)
                    for half in range(2):
                        out[pl.ds(half * 32 + y * 8, 8), lanes] = tile[half * 8 : half * 8 + 8]

    return pl.pallas_call(
        kernel,
        grid=(4,),
        out_shape=jax.ShapeDtypeStruct((256, 1024), F32),
        in_specs=[pl.BlockSpec((1, 2, 4, 4, 16, 128), lambda i: (i, 0, 0, 0, 0, 0))],
        out_specs=pl.BlockSpec((64, 1024), lambda i: (i, 0)),
        compiler_params=params(),
        cost_estimate=cost(256 * 1024, 2 << 20),
        name="unpack",
    )(received.reshape(4, 2, 4, 4, 16, 128))


def slots_of(named):
    same = named[:, :, None] == named[:, None, :]
    earlier = jnp.arange(128)[None, :, None] > jnp.arange(128)[None, None, :]
    ranks = jnp.sum((same & earlier).astype(jnp.int32), axis=2)
    target = named * 16 + jnp.arange(8, dtype=jnp.int32)[:, None] * 2 + ranks
    return target.reshape(8, 4, 32).transpose(1, 0, 2).reshape(4, 1, 256)


def gathered(joined):
    rows = joined.shape[0]
    return lax.all_gather(joined, ("core", "x"), axis=0, tiled=False).reshape(2, 4, rows, 256)


def local(pivot_rhs, bound_sol, border_tiles, lower_tiles, inverse_diag, owner_map):
    z, core, y, x = (lax.axis_index(name) for name in ("z", "core", "y", "x"))
    place = jnp.stack([core, y, x, z]).astype(jnp.int32)
    lead = jnp.where((z == 0) & (core == 0), 1.0, 0.0).astype(F32)

    def tile(j, k):
        return ("L", pair_slot(j, k))

    owners = owner_map[:, :, 0]
    orders = [
        [tile(3, 2), ("D", 2)],
        [tile(3, 1), tile(2, 1), ("D", 1)],
        [tile(3, 0), tile(2, 0), tile(1, 0), ("D", 0)],
    ]
    early, middle, late = map(gathered, stage(lower_tiles, inverse_diag, orders, owners))
    named = late[:, :, 2048, :128].astype(jnp.int32).reshape(8, 128)
    other = swap(inverse_diag[3])

    def term(side):
        start = side * 512
        rhs = lax.dynamic_slice_in_dim(pivot_rhs, start, 512, axis=2)
        bound = lax.dynamic_slice_in_dim(bound_sol, start, 512, axis=1)
        product = lax.dot_general(
            border_tiles, bound, (((0,), (0,)), ((), ())), preferred_element_type=F32
        )
        return (lead * rhs - product).astype(BF16)

    away = swap(term(1 - core))
    home = lax.optimization_barrier(term(core))
    both = (home.astype(F32) + away.astype(F32)).astype(BF16)
    over_z = spread(both[3], "z")
    cut = [
        lax.dynamic_slice_in_dim(both[:3], lax.rem(x + by, 4) * 128, 128, axis=2)
        for by in range(4)
    ]
    rest = deal(cut, "x")
    products = first_product(place, over_z, inverse_diag[3], other, rest[1:])
    base = turn(place, rest)
    own, *others = products
    zero = [along_x(others[by - 1], 0, by) for by in (1, 2, 3)]
    token = lax.ppermute(sum(piece[:8] for piece in zero), "core", [(0, 1)])
    others = gate(token, others)
    one = [along_x(others[by - 1], 1, by) for by in (1, 2, 3)]
    partial = sum(piece.astype(F32) for piece in (own, *zero, *one)).astype(BF16)
    pieces = spread(partial, "y")
    residual, x3 = lower_step(base[2], pieces, early, 0, BF16)
    over_z = spread(residual, "z")
    pieces = spread(diag_step(over_z, early, 1), "y")
    base1, _ = lower_step(base[1], (x3,), middle, 0, F32)
    residual, x2 = lower_step(base1, pieces, middle, 1, BF16)
    over_z = spread(residual, "z")
    pieces = spread(diag_step(over_z, middle, 2), "y")
    base0, _ = lower_step(base[0], (x3,), late, 0, F32)
    base0, _ = lower_step(base0, (x2,), late, 1, F32)
    residual, x1 = lower_step(base0, pieces, late, 2, BF16)
    over_z = spread(residual, "z")
    packed, still = pack_known(place, slots_of(named), (x1, x2, x3))
    rows = deal(last_step(place, over_z, late, 3), "y")
    packed = pack_last(still, rows, packed).reshape(128, 16, 128)
    received = lax.all_to_all(
        packed, ("z", "core", "y", "x"), split_axis=0, concat_axis=0, tiled=True
    )
    return unpack(received)


def solution(mesh):
    fine = Mesh(mesh.devices.reshape(4, 2, 4, 4), ("z", "core", "y", "x"))
    rows, cols = ("z", "core"), ("y", "x")
    placed = (
        P(None, cols, None),
        P(rows, None),
        P(rows, None, cols),
        P(None, rows, cols),
        P(None, cols, rows),
        P(rows + cols, None, None),
    )
    return jax.shard_map(
        local, mesh=fine, in_specs=placed, out_specs=P(rows + cols, None), check_vma=False
    )
```

```python
import jax
import jax.numpy as jnp
from jax import lax
from jax.experimental import pallas as pl
from jax.experimental.pallas import tpu as pltpu
from jax.sharding import Mesh, PartitionSpec as P

BF16 = jnp.bfloat16
F32 = jnp.float32
VMEM_LIMIT = 48 * 1024 * 1024


def pair_slot(later, earlier):
    return later * (later - 1) // 2 + earlier


def shift(value, axis, by):
    return lax.ppermute(value, axis, [(i, (i + by) % 4) for i in range(4)])


def swap(value):
    return lax.ppermute(value, "core", [(0, 1), (1, 0)])


def along_y(value, core, by):
    pairs = [(core * 4 + i, core * 4 + (i + by) % 4) for i in range(4)]
    return lax.ppermute(value, ("core", "y"), pairs)


def spread(value, axis):
    far = shift(value, axis, 2)
    right = shift(value, axis, 1)
    left = shift(value, axis, 3)
    return (value, right, far, left)


def deal(pieces, axis):
    far = shift(pieces[2], axis, 2)
    right = shift(pieces[1], axis, 1)
    left = shift(pieces[3], axis, 3)
    return (pieces[0], right, far, left)


def add_up(refs):
    total = refs[0][...].astype(F32)
    for ref in refs[1:]:
        total = total + ref[...].astype(F32)
    return total


def params(limit=VMEM_LIMIT):
    return pltpu.CompilerParams(vmem_limit_bytes=limit)


def cost(flops, moved):
    return pl.CostEstimate(flops=flops, bytes_accessed=moved, transcendentals=0)


def whole(shape):
    return pl.BlockSpec(shape, lambda *_: (0,) * len(shape))


SCALARS = pl.BlockSpec(memory_space=pltpu.SMEM)
VMEM = pl.BlockSpec(memory_space=pltpu.VMEM)
ANY = pl.BlockSpec(memory_space=pl.ANY)
HBM = pl.BlockSpec(memory_space=pltpu.HBM)


def first_product(place, pieces, mine, other, sent):
    def kernel(place_ref, v0, v1, v2, v3, mine_ref, other_ref, _, *refs):
        outs, full = refs[:4], refs[4]
        core, y = place_ref[0], place_ref[1]
        turned = add_up((v0, v1, v2, v3)).T.astype(BF16)
        for side, tile in ((core, mine_ref), (1 - core, other_ref)):
            product = jnp.dot(turned, tile[...], preferred_element_type=F32)
            full[:, pl.ds(pl.multiple_of(side * 512, 512), 512)] = product.astype(BF16)
        for by, out in enumerate(outs):
            start = lax.rem(y + by, 4) * 128
            out[:, :128] = full[:, pl.ds(pl.multiple_of(start, 128), 128)]
            out[:, 128:] = full[:, pl.ds(pl.multiple_of(start + 512, 128), 128)]

    return pl.pallas_call(
        kernel,
        out_shape=(jax.ShapeDtypeStruct((512, 256), BF16),) * 4,
        in_specs=[SCALARS] + [VMEM] * 6 + [ANY],
        out_specs=(VMEM,) * 4,
        scratch_shapes=[pltpu.VMEM((512, 1024), BF16)],
        compiler_params=params(),
        cost_estimate=cost(2 * 512 * 256 * 1024, 3 << 20),
        name="first_product",
    )(place, *pieces, mine, other, sent)


def first_sum(place, own, zero, one):
    def kernel(place_ref, own_ref, *refs):
        outs = refs[6:]

        def body(parts):
            for step, out in enumerate(outs):
                start = lax.rem(place_ref[2] + step, 4) * 128
                rows = pl.ds(pl.multiple_of(start, 128), 128)
                out[...] = add_up([part.at[rows] for part in (own_ref, *parts)]).astype(BF16)

        @pl.when(place_ref[0] == 0)
        def _():
            body(refs[:3])

        @pl.when(place_ref[0] == 1)
        def _():
            body(refs[3:6])

    return pl.pallas_call(
        kernel,
        out_shape=(jax.ShapeDtypeStruct((128, 256), BF16),) * 4,
        in_specs=[SCALARS] + [VMEM] * 7,
        out_specs=(VMEM,) * 4,
        compiler_params=params(),
        cost_estimate=cost(4 * 512 * 256, 1 << 20),
        name="first_sum",
    )(place, own, *zero, *one)


def gate(events, arrays):
    def kernel(*refs):
        pass

    count, first = len(arrays), len(events)
    return pl.pallas_call(
        kernel,
        out_shape=tuple(jax.ShapeDtypeStruct(value.shape, value.dtype) for value in arrays),
        in_specs=[ANY] * (first + count),
        out_specs=(ANY,) * count,
        input_output_aliases={first + i: i for i in range(count)},
        compiler_params=params(),
        cost_estimate=cost(0, 1024),
        name="gate",
    )(*events, *arrays)


def turn(place, pieces, event):
    def kernel(place_ref, v0, v1, v2, v3, _, out):
        for step, ref in enumerate((v0, v1, v2, v3)):
            start = lax.rem(place_ref[2] + 4 - step, 4) * 256
            lanes = pl.ds(pl.multiple_of(start, 256), 256)
            for k in range(3):
                out[k, :, lanes] = ref[k].astype(F32).T

    return pl.pallas_call(
        kernel,
        out_shape=jax.ShapeDtypeStruct((3, 128, 1024), F32),
        in_specs=[SCALARS] + [VMEM] * 4 + [pl.BlockSpec(memory_space=pl.ANY)],
        out_specs=VMEM,
        compiler_params=params(),
        cost_estimate=cost(3 * 128 * 1024, 3 << 20),
        name="turn",
    )(place, *pieces, event)


def lower_step(base, pieces, tiles, at, dtype, place=None):
    count = len(pieces)
    where = [] if place is None else [place]

    def kernel(*refs):
        place_ref = refs[0]
        refs = refs[len(where) :]
        parts = refs[:count]
        base_ref, tiles_ref, out, kept, tile, sems = refs[count:]
        copies = [
            pltpu.make_async_copy(
                tiles_ref.at[:, i, pl.ds(at * 512, 512), :], tile.at[:, i], sems.at[i]
            )
            for i in range(4)
        ]
        for copy in copies:
            copy.start()
        if where:
            for step, part in enumerate(parts):
                start = lax.rem(place_ref[1] + 4 - step, 4) * 128
                kept[:, pl.ds(pl.multiple_of(start, 128), 128)] = part[:, :128]
                kept[:, pl.ds(pl.multiple_of(start + 512, 128), 128)] = part[:, 128:]
        else:
            kept[...] = add_up(parts).astype(BF16)
        for i, copy in enumerate(copies):
            lanes = slice(i * 256, (i + 1) * 256)
            copy.wait()
            total = base_ref[:, lanes].astype(F32)
            total = total - jnp.dot(kept[:, :512], tile[0, i], preferred_element_type=F32)
            total = total - jnp.dot(kept[:, 512:], tile[1, i], preferred_element_type=F32)
            out[:, lanes] = total.astype(dtype)

    return pl.pallas_call(
        kernel,
        out_shape=(
            jax.ShapeDtypeStruct((128, 1024), dtype),
            jax.ShapeDtypeStruct((128, 1024), BF16),
        ),
        in_specs=[SCALARS] * len(where) + [VMEM] * (count + 1) + [HBM],
        out_specs=(VMEM, VMEM),
        scratch_shapes=[
            pltpu.VMEM((2, 4, 512, 256), BF16),
            pltpu.SemaphoreType.DMA((4,)),
        ],
        compiler_params=params(),
        cost_estimate=cost(2 * 128 * 1024 * 1024, 4 << 20),
        name="lower_step",
    )(*where, *pieces, base, tiles)


def fetch_diag(tiles_ref, at, tile, sems):
    copies = [
        pltpu.make_async_copy(
            tiles_ref.at[side, :, pl.ds(at * 512, 512), :], tile.at[side], sems.at[side]
        )
        for side in range(2)
    ]
    for copy in copies:
        copy.start()
    return copies


def times_fetched(copies, vec, tile, out):
    for side, copy in enumerate(copies):
        copy.wait()
        for half in range(2):
            rows = slice(half * 256, (half + 1) * 256)
            total = None
            for x in range(4):
                left = vec[:, x * 256 : (x + 1) * 256]
                term = jnp.dot(left, tile[side, x, rows], preferred_element_type=F32)
                total = term if total is None else total + term
            start = side * 512 + half * 256
            out[:, start : start + 256] = total.astype(BF16)


DIAG_SCRATCH = [
    pltpu.VMEM((128, 1024), BF16),
    pltpu.VMEM((2, 4, 512, 256), BF16),
    pltpu.SemaphoreType.DMA((2,)),
]


def diag_step(pieces, tiles, at):
    def kernel(v0, v1, v2, v3, tiles_ref, out, vec, tile, sems):
        copies = fetch_diag(tiles_ref, at, tile, sems)
        vec[...] = add_up((v0, v1, v2, v3)).astype(BF16)
        times_fetched(copies, vec, tile, out)

    return pl.pallas_call(
        kernel,
        out_shape=jax.ShapeDtypeStruct((128, 1024), BF16),
        in_specs=[VMEM] * 4 + [HBM],
        out_specs=VMEM,
        scratch_shapes=DIAG_SCRATCH,
        compiler_params=params(),
        cost_estimate=cost(2 * 128 * 1024 * 1024, 4 << 20),
        name="diag_step",
    )(*pieces, tiles)


def last_step(place, pieces, tiles, at):
    def kernel(place_ref, v0, v1, v2, v3, tiles_ref, o0, o1, o2, o3, vec, tile, sems, full):
        copies = fetch_diag(tiles_ref, at, tile, sems)
        vec[...] = add_up((v0, v1, v2, v3)).astype(BF16)
        times_fetched(copies, vec, tile, full)
        for by, out in enumerate((o0, o1, o2, o3)):
            start = lax.rem(place_ref[1] + by, 4) * 128
            out[:, :128] = full[:, pl.ds(pl.multiple_of(start, 128), 128)]
            out[:, 128:] = full[:, pl.ds(pl.multiple_of(start + 512, 128), 128)]

    return pl.pallas_call(
        kernel,
        out_shape=(jax.ShapeDtypeStruct((128, 256), BF16),) * 4,
        in_specs=[SCALARS] + [VMEM] * 4 + [HBM],
        out_specs=(VMEM,) * 4,
        scratch_shapes=DIAG_SCRATCH + [pltpu.VMEM((128, 1024), BF16)],
        compiler_params=params(52 * 1024 * 1024),
        cost_estimate=cost(2 * 128 * 1024 * 1024, 4 << 20),
        name="last_step",
    )(place, *pieces, tiles)


def stage(lower_tiles, inverse_diag, orders, owners):
    moves = []
    for number, order in enumerate(orders):
        for at, (kind, index) in enumerate(order):
            if kind == "L":
                moves.append((0, index, slice(None), number, at * 512, 512))
            else:
                moves.append((1, index, slice(0, 256), number, at * 512, 256))
                moves.append((1, index, slice(256, 512), number, at * 512 + 256, 256))
    heights = [512 * len(order) for order in orders]
    heights[-1] += 16
    count = len(orders)

    def kernel(lower_ref, diag_ref, owners_ref, *refs):
        outs, held, sems = refs[:count], refs[count : 2 * count], refs[2 * count]
        plan = [
            ((lower_ref, diag_ref)[which].at[index, :, lanes], number, pl.ds(start, height))
            for which, index, lanes, number, start, height in moves
        ]
        named = pl.ds(heights[-1] - 16, 16)
        spread_out = jnp.broadcast_to(owners_ref[...].astype(F32), (16, 128)).astype(BF16)
        held[-1][named, :128] = spread_out
        held[-1][named, 128:] = jnp.zeros((16, 128), BF16)
        into, onward = [], []
        for at, (source, number, where) in enumerate(plan):
            middle = held[number].at[where]
            into.append(pltpu.make_async_copy(source, middle, sems.at[0, at]))
            onward.append(pltpu.make_async_copy(middle, outs[number].at[where], sems.at[1, at]))
        last = pltpu.make_async_copy(
            held[-1].at[named], outs[-1].at[named], sems.at[1, len(moves)]
        )
        for copy in into:
            copy.start()
        last.start()
        for first, second in zip(into, onward):
            first.wait()
            second.start()
        for copy in onward:
            copy.wait()
        last.wait()

    return pl.pallas_call(
        kernel,
        out_shape=tuple(jax.ShapeDtypeStruct((height, 256), BF16) for height in heights),
        in_specs=[HBM, HBM, VMEM],
        out_specs=(HBM,) * count,
        scratch_shapes=[pltpu.VMEM((height, 256), BF16) for height in heights]
        + [pltpu.SemaphoreType.DMA((2, len(moves) + 1))],
        compiler_params=params(60 * 1024 * 1024),
        cost_estimate=cost(0, 6 << 20),
        name="stage",
    )(lower_tiles, inverse_diag, owners)


def chosen(target, block):
    slots = lax.broadcasted_iota(jnp.int32, (256, 256), 0) + block * 256
    return jnp.where(slots == target, 1.0, 0.0).astype(BF16)


def picked(select, rows):
    return lax.dot_general(
        select, rows, (((1,), (1,)), ((), ())), preferred_element_type=F32
    )


def pack_known(place, target, known):
    def kernel(place_ref, target_ref, x1, x2, x3, out, still):
        block = pl.program_id(0)
        start = pl.multiple_of(place_ref[1] * 128, 128)
        again = pl.multiple_of(place_ref[1] * 128 + 512, 128)
        total = jnp.zeros((256, 128), F32)
        for k, ref in ((1, x1), (2, x2), (3, x3)):
            rows = jnp.concatenate([ref[:, pl.ds(start, 128)], ref[:, pl.ds(again, 128)]], axis=1)
            total = total + picked(chosen(target_ref[k], block), rows)
        out[...] = total.astype(BF16)
        still[...] = chosen(target_ref[0], block)

    return pl.pallas_call(
        kernel,
        grid=(8,),
        out_shape=(
            jax.ShapeDtypeStruct((2048, 128), BF16),
            jax.ShapeDtypeStruct((2048, 256), BF16),
        ),
        in_specs=[SCALARS, whole((4, 1, 256))] + [whole((128, 1024))] * 3,
        out_specs=(
            pl.BlockSpec((256, 128), lambda i: (i, 0)),
            pl.BlockSpec((256, 256), lambda i: (i, 0)),
        ),
        compiler_params=params(),
        cost_estimate=cost(2 * 2048 * 768 * 128, 2 << 20),
        name="pack_known",
    )(place, target, *known)


def pack_last(still, pieces, base):
    def kernel(still_ref, v0, v1, v2, v3, base_ref, out):
        rows = add_up((v0, v1, v2, v3)).astype(BF16)
        out[...] = (base_ref[...].astype(F32) + picked(still_ref[...], rows)).astype(BF16)

    return pl.pallas_call(
        kernel,
        out_shape=jax.ShapeDtypeStruct((2048, 128), BF16),
        in_specs=[VMEM] * 6,
        out_specs=VMEM,
        compiler_params=params(),
        cost_estimate=cost(2 * 2048 * 256 * 128, 2 << 20),
        name="pack_last",
    )(still, *pieces, base)


def unpack(received):
    def kernel(got, out):
        for core in range(2):
            for y in range(4):
                for x in range(4):
                    tile = got[0, core, y, x].astype(F32)
                    lanes = pl.ds((core * 4 + x) * 128, 128)
                    for half in range(2):
                        out[pl.ds(half * 32 + y * 8, 8), lanes] = tile[half * 8 : half * 8 + 8]

    return pl.pallas_call(
        kernel,
        grid=(4,),
        out_shape=jax.ShapeDtypeStruct((256, 1024), F32),
        in_specs=[pl.BlockSpec((1, 2, 4, 4, 16, 128), lambda i: (i, 0, 0, 0, 0, 0))],
        out_specs=pl.BlockSpec((64, 1024), lambda i: (i, 0)),
        compiler_params=params(),
        cost_estimate=cost(256 * 1024, 2 << 20),
        name="unpack",
    )(received.reshape(4, 2, 4, 4, 16, 128))


def slots_of(named):
    same = named[:, :, None] == named[:, None, :]
    earlier = jnp.arange(128)[None, :, None] > jnp.arange(128)[None, None, :]
    ranks = jnp.sum((same & earlier).astype(jnp.int32), axis=2)
    target = named * 16 + jnp.arange(8, dtype=jnp.int32)[:, None] * 2 + ranks
    return target.reshape(8, 4, 32).transpose(1, 0, 2).reshape(4, 1, 256)


def gathered(joined):
    rows = joined.shape[0]
    return lax.all_gather(joined, ("core", "x"), axis=0, tiled=False).reshape(2, 4, rows, 256)


def local(pivot_rhs, bound_sol, border_tiles, lower_tiles, inverse_diag, owner_map):
    z, core, y, x = (lax.axis_index(name) for name in ("z", "core", "y", "x"))
    place = jnp.stack([core, y, x, z]).astype(jnp.int32)
    lead = jnp.where((z == 0) & (core == 0), 1.0, 0.0).astype(F32)

    def tile(j, k):
        return ("L", pair_slot(j, k))

    owners = owner_map[:, :, 0]
    orders = [
        [tile(3, 2), ("D", 2), tile(3, 1), tile(2, 1), ("D", 1)],
        [tile(3, 0), tile(2, 0), tile(1, 0), ("D", 0)],
    ]
    early, late = map(gathered, stage(lower_tiles, inverse_diag, orders, owners))
    named = late[:, :, 2048, :128].astype(jnp.int32).reshape(8, 128)
    other = swap(inverse_diag[3])

    def term(side):
        start = side * 512
        rhs = lax.dynamic_slice_in_dim(pivot_rhs, start, 512, axis=2)
        bound = lax.dynamic_slice_in_dim(bound_sol, start, 512, axis=1)
        product = lax.dot_general(
            border_tiles, bound, (((0,), (0,)), ((), ())), preferred_element_type=F32
        )
        return (lead * rhs - product).astype(BF16)

    away = swap(term(1 - core))
    home = lax.optimization_barrier(term(core))
    both = (home.astype(F32) + away.astype(F32)).astype(BF16)
    over_z = spread(both[3], "z")
    cut = [
        lax.dynamic_slice_in_dim(both[:3], lax.rem(x + by, 4) * 128, 128, axis=2)
        for by in range(4)
    ]
    rest = deal(cut, "x")
    own, *others = first_product(place, over_z, inverse_diag[3], other, rest[1])
    zero = [along_y(others[by - 1], 0, by) for by in (1, 2, 3)]
    token = lax.ppermute(sum(piece[:8] for piece in zero), "core", [(0, 1)])
    others = gate((token, *rest[2:]), others)
    one = [along_y(others[by - 1], 1, by) for by in (1, 2, 3)]
    over_x = deal(first_sum(place, own, zero, one), "x")
    quarter = sum(piece.astype(F32) for piece in over_x).astype(BF16)
    base = turn(place, rest, quarter)
    quarters = spread(quarter, "y")
    residual, x3 = lower_step(base[2], quarters, early, 0, BF16, place)
    over_z = spread(residual, "z")
    pieces = spread(diag_step(over_z, early, 1), "y")
    base1, _ = lower_step(base[1], (x3,), early, 2, F32)
    residual, x2 = lower_step(base1, pieces, early, 3, BF16)
    over_z = spread(residual, "z")
    pieces = spread(diag_step(over_z, early, 4), "y")
    base0, _ = lower_step(base[0], (x3,), late, 0, F32)
    base0, _ = lower_step(base0, (x2,), late, 1, F32)
    residual, x1 = lower_step(base0, pieces, late, 2, BF16)
    over_z = spread(residual, "z")
    packed, still = pack_known(place, slots_of(named), (x1, x2, x3))
    rows = deal(last_step(place, over_z, late, 3), "y")
    packed = pack_last(still, rows, packed).reshape(128, 16, 128)
    received = lax.all_to_all(
        packed, ("z", "core", "y", "x"), split_axis=0, concat_axis=0, tiled=True
    )
    return unpack(received)


def solution(mesh):
    fine = Mesh(mesh.devices.reshape(4, 2, 4, 4), ("z", "core", "y", "x"))
    rows, cols = ("z", "core"), ("y", "x")
    placed = (
        P(None, cols, None),
        P(rows, None),
        P(rows, None, cols),
        P(None, rows, cols),
        P(None, cols, rows),
        P(rows + cols, None, None),
    )
    return jax.shard_map(
        local, mesh=fine, in_specs=placed, out_specs=P(rows + cols, None), check_vma=False
    )
```

```python
import jax
import jax.numpy as jnp
from jax import lax
from jax.experimental import pallas as pl
from jax.experimental.pallas import tpu as pltpu
from jax.sharding import Mesh, PartitionSpec as P

BF16 = jnp.bfloat16
F32 = jnp.float32
VMEM_LIMIT = 48 * 1024 * 1024


def pair_slot(later, earlier):
    return later * (later - 1) // 2 + earlier


def shift(value, axis, by):
    return lax.ppermute(value, axis, [(i, (i + by) % 4) for i in range(4)])


def swap(value):
    return lax.ppermute(value, "core", [(0, 1), (1, 0)])


def along_y(value, core, by):
    pairs = [(core * 4 + i, core * 4 + (i + by) % 4) for i in range(4)]
    return lax.ppermute(value, ("core", "y"), pairs)


def spread(value, axis):
    far = shift(value, axis, 2)
    right = shift(value, axis, 1)
    left = shift(value, axis, 3)
    return (value, right, far, left)


def deal(pieces, axis):
    far = shift(pieces[2], axis, 2)
    right = shift(pieces[1], axis, 1)
    left = shift(pieces[3], axis, 3)
    return (pieces[0], right, far, left)


def add_up(refs):
    total = refs[0][...].astype(F32)
    for ref in refs[1:]:
        total = total + ref[...].astype(F32)
    return total


def params(limit=VMEM_LIMIT):
    return pltpu.CompilerParams(vmem_limit_bytes=limit)


def cost(flops, moved):
    return pl.CostEstimate(flops=flops, bytes_accessed=moved, transcendentals=0)


def whole(shape):
    return pl.BlockSpec(shape, lambda *_: (0,) * len(shape))


SCALARS = pl.BlockSpec(memory_space=pltpu.SMEM)
VMEM = pl.BlockSpec(memory_space=pltpu.VMEM)
ANY = pl.BlockSpec(memory_space=pl.ANY)
HBM = pl.BlockSpec(memory_space=pltpu.HBM)


def first_product(place, pieces, mine, other, sent):
    def kernel(place_ref, v0, v1, v2, v3, mine_ref, other_ref, *refs):
        outs, full = refs[len(sent) : len(sent) + 4], refs[len(sent) + 4]
        core, y = place_ref[0], place_ref[1]
        turned = add_up((v0, v1, v2, v3)).T.astype(BF16)
        for side, tile in ((core, mine_ref), (1 - core, other_ref)):
            product = jnp.dot(turned, tile[...], preferred_element_type=F32)
            full[:, pl.ds(pl.multiple_of(side * 512, 512), 512)] = product.astype(BF16)
        for by, out in enumerate(outs):
            start = lax.rem(y + by, 4) * 128
            out[:, :128] = full[:, pl.ds(pl.multiple_of(start, 128), 128)]
            out[:, 128:] = full[:, pl.ds(pl.multiple_of(start + 512, 128), 128)]

    return pl.pallas_call(
        kernel,
        out_shape=(jax.ShapeDtypeStruct((512, 256), BF16),) * 4,
        in_specs=[SCALARS] + [VMEM] * 6 + [ANY] * len(sent),
        out_specs=(VMEM,) * 4,
        scratch_shapes=[pltpu.VMEM((512, 1024), BF16)],
        compiler_params=params(),
        cost_estimate=cost(2 * 512 * 256 * 1024, 3 << 20),
        name="first_product",
    )(place, *pieces, mine, other, *sent)


def first_sum(place, own, zero, one):
    def kernel(place_ref, own_ref, *refs):
        outs = refs[6:]

        def body(parts):
            for step, out in enumerate(outs):
                start = lax.rem(place_ref[2] + step, 4) * 128
                rows = pl.ds(pl.multiple_of(start, 128), 128)
                out[...] = add_up([part.at[rows] for part in (own_ref, *parts)]).astype(BF16)

        @pl.when(place_ref[0] == 0)
        def _():
            body(refs[:3])

        @pl.when(place_ref[0] == 1)
        def _():
            body(refs[3:6])

    return pl.pallas_call(
        kernel,
        out_shape=(jax.ShapeDtypeStruct((128, 256), BF16),) * 4,
        in_specs=[SCALARS] + [VMEM] * 7,
        out_specs=(VMEM,) * 4,
        compiler_params=params(),
        cost_estimate=cost(4 * 512 * 256, 1 << 20),
        name="first_sum",
    )(place, own, *zero, *one)


def gate(events, arrays):
    def kernel(*refs):
        pass

    count, first = len(arrays), len(events)
    return pl.pallas_call(
        kernel,
        out_shape=tuple(jax.ShapeDtypeStruct(value.shape, value.dtype) for value in arrays),
        in_specs=[ANY] * (first + count),
        out_specs=(ANY,) * count,
        input_output_aliases={first + i: i for i in range(count)},
        compiler_params=params(),
        cost_estimate=cost(0, 1024),
        name="gate",
    )(*events, *arrays)


def turn(place, pieces, event):
    blocks = pieces[0].shape[0]

    def kernel(place_ref, v0, v1, v2, v3, _, out):
        for step, ref in enumerate((v0, v1, v2, v3)):
            start = lax.rem(place_ref[2] + 4 - step, 4) * 256
            lanes = pl.ds(pl.multiple_of(start, 256), 256)
            for k in range(blocks):
                out[k, :, lanes] = ref[k].astype(F32).T

    return pl.pallas_call(
        kernel,
        out_shape=jax.ShapeDtypeStruct((blocks, 128, 1024), F32),
        in_specs=[SCALARS] + [VMEM] * 4 + [pl.BlockSpec(memory_space=pl.ANY)],
        out_specs=VMEM,
        compiler_params=params(),
        cost_estimate=cost(blocks * 128 * 1024, blocks << 20),
        name="turn",
    )(place, *pieces, event)


def lower_step(base, pieces, tiles, at, dtype, place=None):
    count = len(pieces)
    where = [] if place is None else [place]

    def kernel(*refs):
        place_ref = refs[0]
        refs = refs[len(where) :]
        parts = refs[:count]
        base_ref, tiles_ref, out, kept, tile, sems = refs[count:]
        copies = [
            pltpu.make_async_copy(
                tiles_ref.at[:, i, pl.ds(at * 512, 512), :], tile.at[:, i], sems.at[i]
            )
            for i in range(4)
        ]
        for copy in copies:
            copy.start()
        if where:
            for step, part in enumerate(parts):
                start = lax.rem(place_ref[1] + 4 - step, 4) * 128
                kept[:, pl.ds(pl.multiple_of(start, 128), 128)] = part[:, :128]
                kept[:, pl.ds(pl.multiple_of(start + 512, 128), 128)] = part[:, 128:]
        else:
            kept[...] = add_up(parts).astype(BF16)
        for i, copy in enumerate(copies):
            lanes = slice(i * 256, (i + 1) * 256)
            copy.wait()
            total = base_ref[:, lanes].astype(F32)
            total = total - jnp.dot(kept[:, :512], tile[0, i], preferred_element_type=F32)
            total = total - jnp.dot(kept[:, 512:], tile[1, i], preferred_element_type=F32)
            out[:, lanes] = total.astype(dtype)

    return pl.pallas_call(
        kernel,
        out_shape=(
            jax.ShapeDtypeStruct((128, 1024), dtype),
            jax.ShapeDtypeStruct((128, 1024), BF16),
        ),
        in_specs=[SCALARS] * len(where) + [VMEM] * (count + 1) + [HBM],
        out_specs=(VMEM, VMEM),
        scratch_shapes=[
            pltpu.VMEM((2, 4, 512, 256), BF16),
            pltpu.SemaphoreType.DMA((4,)),
        ],
        compiler_params=params(),
        cost_estimate=cost(2 * 128 * 1024 * 1024, 4 << 20),
        name="lower_step",
    )(*where, *pieces, base, tiles)


def fetch_diag(tiles_ref, at, tile, sems):
    copies = [
        pltpu.make_async_copy(
            tiles_ref.at[side, :, pl.ds(at * 512, 512), :], tile.at[side], sems.at[side]
        )
        for side in range(2)
    ]
    for copy in copies:
        copy.start()
    return copies


def times_fetched(copies, vec, tile, out):
    for side, copy in enumerate(copies):
        copy.wait()
        for half in range(2):
            rows = slice(half * 256, (half + 1) * 256)
            total = None
            for x in range(4):
                left = vec[:, x * 256 : (x + 1) * 256]
                term = jnp.dot(left, tile[side, x, rows], preferred_element_type=F32)
                total = term if total is None else total + term
            start = side * 512 + half * 256
            out[:, start : start + 256] = total.astype(BF16)


DIAG_SCRATCH = [
    pltpu.VMEM((128, 1024), BF16),
    pltpu.VMEM((2, 4, 512, 256), BF16),
    pltpu.SemaphoreType.DMA((2,)),
]


def diag_step(pieces, tiles, at):
    def kernel(v0, v1, v2, v3, tiles_ref, out, vec, tile, sems):
        copies = fetch_diag(tiles_ref, at, tile, sems)
        vec[...] = add_up((v0, v1, v2, v3)).astype(BF16)
        times_fetched(copies, vec, tile, out)

    return pl.pallas_call(
        kernel,
        out_shape=jax.ShapeDtypeStruct((128, 1024), BF16),
        in_specs=[VMEM] * 4 + [HBM],
        out_specs=VMEM,
        scratch_shapes=DIAG_SCRATCH,
        compiler_params=params(),
        cost_estimate=cost(2 * 128 * 1024 * 1024, 4 << 20),
        name="diag_step",
    )(*pieces, tiles)


def last_step(place, pieces, tiles, at):
    def kernel(place_ref, v0, v1, v2, v3, tiles_ref, o0, o1, o2, o3, vec, tile, sems, full):
        copies = fetch_diag(tiles_ref, at, tile, sems)
        vec[...] = add_up((v0, v1, v2, v3)).astype(BF16)
        times_fetched(copies, vec, tile, full)
        for by, out in enumerate((o0, o1, o2, o3)):
            start = lax.rem(place_ref[1] + by, 4) * 128
            out[:, :128] = full[:, pl.ds(pl.multiple_of(start, 128), 128)]
            out[:, 128:] = full[:, pl.ds(pl.multiple_of(start + 512, 128), 128)]

    return pl.pallas_call(
        kernel,
        out_shape=(jax.ShapeDtypeStruct((128, 256), BF16),) * 4,
        in_specs=[SCALARS] + [VMEM] * 4 + [HBM],
        out_specs=(VMEM,) * 4,
        scratch_shapes=DIAG_SCRATCH + [pltpu.VMEM((128, 1024), BF16)],
        compiler_params=params(52 * 1024 * 1024),
        cost_estimate=cost(2 * 128 * 1024 * 1024, 4 << 20),
        name="last_step",
    )(place, *pieces, tiles)


def stage(lower_tiles, inverse_diag, orders, owners):
    moves = []
    for number, order in enumerate(orders):
        for at, (kind, index) in enumerate(order):
            if kind == "L":
                moves.append((0, index, slice(None), number, at * 512, 512))
            else:
                moves.append((1, index, slice(0, 256), number, at * 512, 256))
                moves.append((1, index, slice(256, 512), number, at * 512 + 256, 256))
    heights = [512 * len(order) for order in orders]
    heights[-1] += 16
    count = len(orders)

    def kernel(lower_ref, diag_ref, owners_ref, *refs):
        outs, held, sems = refs[:count], refs[count : 2 * count], refs[2 * count]
        plan = [
            ((lower_ref, diag_ref)[which].at[index, :, lanes], number, pl.ds(start, height))
            for which, index, lanes, number, start, height in moves
        ]
        named = pl.ds(heights[-1] - 16, 16)
        spread_out = jnp.broadcast_to(owners_ref[...].astype(F32), (16, 128)).astype(BF16)
        held[-1][named, :128] = spread_out
        held[-1][named, 128:] = jnp.zeros((16, 128), BF16)
        into, onward = [], []
        for at, (source, number, where) in enumerate(plan):
            middle = held[number].at[where]
            into.append(pltpu.make_async_copy(source, middle, sems.at[0, at]))
            onward.append(pltpu.make_async_copy(middle, outs[number].at[where], sems.at[1, at]))
        last = pltpu.make_async_copy(
            held[-1].at[named], outs[-1].at[named], sems.at[1, len(moves)]
        )
        for copy in into:
            copy.start()
        last.start()
        for first, second in zip(into, onward):
            first.wait()
            second.start()
        for copy in onward:
            copy.wait()
        last.wait()

    return pl.pallas_call(
        kernel,
        out_shape=tuple(jax.ShapeDtypeStruct((height, 256), BF16) for height in heights),
        in_specs=[HBM, HBM, VMEM],
        out_specs=(HBM,) * count,
        scratch_shapes=[pltpu.VMEM((height, 256), BF16) for height in heights]
        + [pltpu.SemaphoreType.DMA((2, len(moves) + 1))],
        compiler_params=params(60 * 1024 * 1024),
        cost_estimate=cost(0, 6 << 20),
        name="stage",
    )(lower_tiles, inverse_diag, owners)


def chosen(target, block):
    slots = lax.broadcasted_iota(jnp.int32, (256, 256), 0) + block * 256
    return jnp.where(slots == target, 1.0, 0.0).astype(BF16)


def picked(select, rows):
    return lax.dot_general(
        select, rows, (((1,), (1,)), ((), ())), preferred_element_type=F32
    )


def pack_known(place, target, known):
    def kernel(place_ref, target_ref, x1, x2, x3, out, still):
        block = pl.program_id(0)
        start = pl.multiple_of(place_ref[1] * 128, 128)
        again = pl.multiple_of(place_ref[1] * 128 + 512, 128)
        total = jnp.zeros((256, 128), F32)
        for k, ref in ((1, x1), (2, x2), (3, x3)):
            rows = jnp.concatenate([ref[:, pl.ds(start, 128)], ref[:, pl.ds(again, 128)]], axis=1)
            total = total + picked(chosen(target_ref[k], block), rows)
        out[...] = total.astype(BF16)
        still[...] = chosen(target_ref[0], block)

    return pl.pallas_call(
        kernel,
        grid=(8,),
        out_shape=(
            jax.ShapeDtypeStruct((2048, 128), BF16),
            jax.ShapeDtypeStruct((2048, 256), BF16),
        ),
        in_specs=[SCALARS, whole((4, 1, 256))] + [whole((128, 1024))] * 3,
        out_specs=(
            pl.BlockSpec((256, 128), lambda i: (i, 0)),
            pl.BlockSpec((256, 256), lambda i: (i, 0)),
        ),
        compiler_params=params(),
        cost_estimate=cost(2 * 2048 * 768 * 128, 2 << 20),
        name="pack_known",
    )(place, target, *known)


def pack_last(still, pieces, base):
    def kernel(still_ref, v0, v1, v2, v3, base_ref, out):
        rows = add_up((v0, v1, v2, v3)).astype(BF16)
        out[...] = (base_ref[...].astype(F32) + picked(still_ref[...], rows)).astype(BF16)

    return pl.pallas_call(
        kernel,
        out_shape=jax.ShapeDtypeStruct((2048, 128), BF16),
        in_specs=[VMEM] * 6,
        out_specs=VMEM,
        compiler_params=params(),
        cost_estimate=cost(2 * 2048 * 256 * 128, 2 << 20),
        name="pack_last",
    )(still, *pieces, base)


def unpack(received):
    def kernel(got, out):
        for core in range(2):
            for y in range(4):
                for x in range(4):
                    tile = got[0, core, y, x].astype(F32)
                    lanes = pl.ds((core * 4 + x) * 128, 128)
                    for half in range(2):
                        out[pl.ds(half * 32 + y * 8, 8), lanes] = tile[half * 8 : half * 8 + 8]

    return pl.pallas_call(
        kernel,
        grid=(4,),
        out_shape=jax.ShapeDtypeStruct((256, 1024), F32),
        in_specs=[pl.BlockSpec((1, 2, 4, 4, 16, 128), lambda i: (i, 0, 0, 0, 0, 0))],
        out_specs=pl.BlockSpec((64, 1024), lambda i: (i, 0)),
        compiler_params=params(),
        cost_estimate=cost(256 * 1024, 2 << 20),
        name="unpack",
    )(received.reshape(4, 2, 4, 4, 16, 128))


def slots_of(named):
    same = named[:, :, None] == named[:, None, :]
    earlier = jnp.arange(128)[None, :, None] > jnp.arange(128)[None, None, :]
    ranks = jnp.sum((same & earlier).astype(jnp.int32), axis=2)
    target = named * 16 + jnp.arange(8, dtype=jnp.int32)[:, None] * 2 + ranks
    return target.reshape(8, 4, 32).transpose(1, 0, 2).reshape(4, 1, 256)


def gathered(joined):
    rows = joined.shape[0]
    return lax.all_gather(joined, ("core", "x"), axis=0, tiled=False).reshape(2, 4, rows, 256)


def local(pivot_rhs, bound_sol, border_tiles, lower_tiles, inverse_diag, owner_map):
    z, core, y, x = (lax.axis_index(name) for name in ("z", "core", "y", "x"))
    place = jnp.stack([core, y, x, z]).astype(jnp.int32)
    lead = jnp.where((z == 0) & (core == 0), 1.0, 0.0).astype(F32)

    def tile(j, k):
        return ("L", pair_slot(j, k))

    owners = owner_map[:, :, 0]
    orders = [
        [tile(3, 2), ("D", 2), tile(3, 1), tile(2, 1), ("D", 1)],
        [tile(3, 0), tile(2, 0), tile(1, 0), ("D", 0)],
    ]
    early, late = map(gathered, stage(lower_tiles, inverse_diag, orders, owners))
    named = late[:, :, 2048, :128].astype(jnp.int32).reshape(8, 128)
    other = swap(inverse_diag[3])

    def term(side):
        start = side * 512
        rhs = lax.dynamic_slice_in_dim(pivot_rhs, start, 512, axis=2)
        bound = lax.dynamic_slice_in_dim(bound_sol, start, 512, axis=1)
        product = lax.dot_general(
            border_tiles, bound, (((0,), (0,)), ((), ())), preferred_element_type=F32
        )
        return (lead * rhs - product).astype(BF16)

    away = swap(term(1 - core))
    home = lax.optimization_barrier(term(core))
    both = (home.astype(F32) + away.astype(F32)).astype(BF16)
    over_z = spread(both[3], "z")
    def cut(part):
        return [
            lax.dynamic_slice_in_dim(part, lax.rem(x + by, 4) * 128, 128, axis=2)
            for by in range(4)
        ]

    near = deal(cut(both[2:3]), "x")
    own, *others = first_product(place, over_z, inverse_diag[3], other, near[1:])
    zero = [along_y(others[by - 1], 0, by) for by in (1, 2, 3)]
    token = lax.ppermute(sum(piece[:8] for piece in zero), "core", [(0, 1)])
    others = gate((token,), others)
    one = [along_y(others[by - 1], 1, by) for by in (1, 2, 3)]
    over_x = deal(first_sum(place, own, zero, one), "x")
    quarter = sum(piece.astype(F32) for piece in over_x).astype(BF16)
    base2 = turn(place, near, quarter)[0]
    quarters = spread(quarter, "y")
    residual, x3 = lower_step(base2, quarters, early, 0, BF16, place)
    over_z = spread(residual, "z")
    base = turn(place, deal(gate((x3,), cut(both[:2])), "x"), over_z[2])
    pieces = spread(diag_step(over_z, early, 1), "y")
    base1, _ = lower_step(base[1], (x3,), early, 2, F32)
    residual, x2 = lower_step(base1, pieces, early, 3, BF16)
    over_z = spread(residual, "z")
    pieces = spread(diag_step(over_z, early, 4), "y")
    base0, _ = lower_step(base[0], (x3,), late, 0, F32)
    base0, _ = lower_step(base0, (x2,), late, 1, F32)
    residual, x1 = lower_step(base0, pieces, late, 2, BF16)
    over_z = spread(residual, "z")
    packed, still = pack_known(place, slots_of(named), (x1, x2, x3))
    rows = deal(last_step(place, over_z, late, 3), "y")
    packed = pack_last(still, rows, packed).reshape(128, 16, 128)
    received = lax.all_to_all(
        packed, ("z", "core", "y", "x"), split_axis=0, concat_axis=0, tiled=True
    )
    return unpack(received)


def solution(mesh):
    fine = Mesh(mesh.devices.reshape(4, 2, 4, 4), ("z", "core", "y", "x"))
    rows, cols = ("z", "core"), ("y", "x")
    placed = (
        P(None, cols, None),
        P(rows, None),
        P(rows, None, cols),
        P(None, rows, cols),
        P(None, cols, rows),
        P(rows + cols, None, None),
    )
    return jax.shard_map(
        local, mesh=fine, in_specs=placed, out_specs=P(rows + cols, None), check_vma=False
    )
```

```python
import jax
import jax.numpy as jnp
from jax import lax
from jax.experimental import pallas as pl
from jax.experimental.pallas import tpu as pltpu
from jax.sharding import Mesh, PartitionSpec as P

BF16 = jnp.bfloat16
F32 = jnp.float32
VMEM_LIMIT = 48 * 1024 * 1024


def pair_slot(later, earlier):
    return later * (later - 1) // 2 + earlier


def shift(value, axis, by):
    return lax.ppermute(value, axis, [(i, (i + by) % 4) for i in range(4)])


def swap(value):
    return lax.ppermute(value, "core", [(0, 1), (1, 0)])


def along_z(value, core, by):
    pairs = [(i * 2 + core, (i + by) % 4 * 2 + core) for i in range(4)]
    return lax.ppermute(value, ("z", "core"), pairs)


def spread(value, axis):
    far = shift(value, axis, 2)
    right = shift(value, axis, 1)
    left = shift(value, axis, 3)
    return (value, right, far, left)


def deal(pieces, axis):
    far = shift(pieces[2], axis, 2)
    right = shift(pieces[1], axis, 1)
    left = shift(pieces[3], axis, 3)
    return (pieces[0], right, far, left)


def add_up(refs):
    total = refs[0][...].astype(F32)
    for ref in refs[1:]:
        total = total + ref[...].astype(F32)
    return total


def params(limit=VMEM_LIMIT):
    return pltpu.CompilerParams(vmem_limit_bytes=limit)


def cost(flops, moved):
    return pl.CostEstimate(flops=flops, bytes_accessed=moved, transcendentals=0)


def whole(shape):
    return pl.BlockSpec(shape, lambda *_: (0,) * len(shape))


SCALARS = pl.BlockSpec(memory_space=pltpu.SMEM)
VMEM = pl.BlockSpec(memory_space=pltpu.VMEM)
ANY = pl.BlockSpec(memory_space=pl.ANY)
HBM = pl.BlockSpec(memory_space=pltpu.HBM)


def first_product(place, own, zero, one, mine, other):
    def kernel(place_ref, own_ref, *refs):
        mine_ref, other_ref = refs[6:8]
        outs, full, turned = refs[8:12], refs[12], refs[13]
        core, y = place_ref[0], place_ref[1]

        @pl.when(core == 0)
        def _():
            turned[...] = add_up((own_ref, *refs[:3])).T.astype(BF16)

        @pl.when(core == 1)
        def _():
            turned[...] = add_up((own_ref, *refs[3:6])).T.astype(BF16)

        for side, tile in ((core, mine_ref), (1 - core, other_ref)):
            product = jnp.dot(turned[...], tile[...], preferred_element_type=F32)
            full[:, pl.ds(pl.multiple_of(side * 512, 512), 512)] = product.astype(BF16)
        for by, out in enumerate(outs):
            start = lax.rem(y + by, 4) * 128
            out[:, :128] = full[:, pl.ds(pl.multiple_of(start, 128), 128)]
            out[:, 128:] = full[:, pl.ds(pl.multiple_of(start + 512, 128), 128)]

    return pl.pallas_call(
        kernel,
        out_shape=(jax.ShapeDtypeStruct((512, 256), BF16),) * 4,
        in_specs=[SCALARS] + [VMEM] * 9,
        out_specs=(VMEM,) * 4,
        scratch_shapes=[pltpu.VMEM((512, 1024), BF16), pltpu.VMEM((512, 256), BF16)],
        compiler_params=params(),
        cost_estimate=cost(2 * 512 * 256 * 1024, 3 << 20),
        name="first_product",
    )(place, own, *zero, *one, mine, other)


def first_sum(place, pieces, sent):
    def kernel(place_ref, v0, v1, v2, v3, *refs):
        for step, out in enumerate(refs[len(sent) :]):
            start = lax.rem(place_ref[2] + step, 4) * 128
            rows = pl.ds(pl.multiple_of(start, 128), 128)
            out[...] = add_up([part.at[rows] for part in (v0, v1, v2, v3)]).astype(BF16)

    return pl.pallas_call(
        kernel,
        out_shape=(jax.ShapeDtypeStruct((128, 256), BF16),) * 4,
        in_specs=[SCALARS] + [VMEM] * 4 + [ANY] * len(sent),
        out_specs=(VMEM,) * 4,
        compiler_params=params(),
        cost_estimate=cost(4 * 512 * 256, 1 << 20),
        name="first_sum",
    )(place, *pieces, *sent)


def gate(events, arrays):
    def kernel(*refs):
        pass

    count, first = len(arrays), len(events)
    return pl.pallas_call(
        kernel,
        out_shape=tuple(jax.ShapeDtypeStruct(value.shape, value.dtype) for value in arrays),
        in_specs=[ANY] * (first + count),
        out_specs=(ANY,) * count,
        input_output_aliases={first + i: i for i in range(count)},
        compiler_params=params(),
        cost_estimate=cost(0, 1024),
        name="gate",
    )(*events, *arrays)


def turn(place, pieces, event):
    blocks = pieces[0].shape[0]

    def kernel(place_ref, v0, v1, v2, v3, _, out):
        for step, ref in enumerate((v0, v1, v2, v3)):
            start = lax.rem(place_ref[2] + 4 - step, 4) * 256
            lanes = pl.ds(pl.multiple_of(start, 256), 256)
            for k in range(blocks):
                out[k, :, lanes] = ref[k].astype(F32).T

    return pl.pallas_call(
        kernel,
        out_shape=jax.ShapeDtypeStruct((blocks, 128, 1024), F32),
        in_specs=[SCALARS] + [VMEM] * 4 + [pl.BlockSpec(memory_space=pl.ANY)],
        out_specs=VMEM,
        compiler_params=params(),
        cost_estimate=cost(blocks * 128 * 1024, blocks << 20),
        name="turn",
    )(place, *pieces, event)


def lower_step(base, pieces, tiles, at, dtype, place=None):
    count = len(pieces)
    where = [] if place is None else [place]

    def kernel(*refs):
        place_ref = refs[0]
        refs = refs[len(where) :]
        parts = refs[:count]
        base_ref, tiles_ref, out, kept, tile, sems = refs[count:]
        copies = [
            pltpu.make_async_copy(
                tiles_ref.at[:, i, pl.ds(at * 512, 512), :], tile.at[:, i], sems.at[i]
            )
            for i in range(4)
        ]
        for copy in copies:
            copy.start()
        if where:
            for step, part in enumerate(parts):
                start = lax.rem(place_ref[1] + 4 - step, 4) * 128
                kept[:, pl.ds(pl.multiple_of(start, 128), 128)] = part[:, :128]
                kept[:, pl.ds(pl.multiple_of(start + 512, 128), 128)] = part[:, 128:]
        else:
            kept[...] = add_up(parts).astype(BF16)
        for i, copy in enumerate(copies):
            lanes = slice(i * 256, (i + 1) * 256)
            copy.wait()
            total = base_ref[:, lanes].astype(F32)
            total = total - jnp.dot(kept[:, :512], tile[0, i], preferred_element_type=F32)
            total = total - jnp.dot(kept[:, 512:], tile[1, i], preferred_element_type=F32)
            out[:, lanes] = total.astype(dtype)

    return pl.pallas_call(
        kernel,
        out_shape=(
            jax.ShapeDtypeStruct((128, 1024), dtype),
            jax.ShapeDtypeStruct((128, 1024), BF16),
        ),
        in_specs=[SCALARS] * len(where) + [VMEM] * (count + 1) + [HBM],
        out_specs=(VMEM, VMEM),
        scratch_shapes=[
            pltpu.VMEM((2, 4, 512, 256), BF16),
            pltpu.SemaphoreType.DMA((4,)),
        ],
        compiler_params=params(),
        cost_estimate=cost(2 * 128 * 1024 * 1024, 4 << 20),
        name="lower_step",
    )(*where, *pieces, base, tiles)


def fetch_diag(tiles_ref, at, tile, sems):
    copies = [
        pltpu.make_async_copy(
            tiles_ref.at[side, :, pl.ds(at * 512, 512), :], tile.at[side], sems.at[side]
        )
        for side in range(2)
    ]
    for copy in copies:
        copy.start()
    return copies


def times_fetched(copies, vec, tile, out):
    for side, copy in enumerate(copies):
        copy.wait()
        for half in range(2):
            rows = slice(half * 256, (half + 1) * 256)
            total = None
            for x in range(4):
                left = vec[:, x * 256 : (x + 1) * 256]
                term = jnp.dot(left, tile[side, x, rows], preferred_element_type=F32)
                total = term if total is None else total + term
            start = side * 512 + half * 256
            out[:, start : start + 256] = total.astype(BF16)


DIAG_SCRATCH = [
    pltpu.VMEM((128, 1024), BF16),
    pltpu.VMEM((2, 4, 512, 256), BF16),
    pltpu.SemaphoreType.DMA((2,)),
]


def diag_step(pieces, tiles, at):
    def kernel(v0, v1, v2, v3, tiles_ref, out, vec, tile, sems):
        copies = fetch_diag(tiles_ref, at, tile, sems)
        vec[...] = add_up((v0, v1, v2, v3)).astype(BF16)
        times_fetched(copies, vec, tile, out)

    return pl.pallas_call(
        kernel,
        out_shape=jax.ShapeDtypeStruct((128, 1024), BF16),
        in_specs=[VMEM] * 4 + [HBM],
        out_specs=VMEM,
        scratch_shapes=DIAG_SCRATCH,
        compiler_params=params(),
        cost_estimate=cost(2 * 128 * 1024 * 1024, 4 << 20),
        name="diag_step",
    )(*pieces, tiles)


def last_step(place, pieces, tiles, at):
    def kernel(place_ref, v0, v1, v2, v3, tiles_ref, o0, o1, o2, o3, vec, tile, sems, full):
        copies = fetch_diag(tiles_ref, at, tile, sems)
        vec[...] = add_up((v0, v1, v2, v3)).astype(BF16)
        times_fetched(copies, vec, tile, full)
        for by, out in enumerate((o0, o1, o2, o3)):
            start = lax.rem(place_ref[1] + by, 4) * 128
            out[:, :128] = full[:, pl.ds(pl.multiple_of(start, 128), 128)]
            out[:, 128:] = full[:, pl.ds(pl.multiple_of(start + 512, 128), 128)]

    return pl.pallas_call(
        kernel,
        out_shape=(jax.ShapeDtypeStruct((128, 256), BF16),) * 4,
        in_specs=[SCALARS] + [VMEM] * 4 + [HBM],
        out_specs=(VMEM,) * 4,
        scratch_shapes=DIAG_SCRATCH + [pltpu.VMEM((128, 1024), BF16)],
        compiler_params=params(52 * 1024 * 1024),
        cost_estimate=cost(2 * 128 * 1024 * 1024, 4 << 20),
        name="last_step",
    )(place, *pieces, tiles)


def stage(lower_tiles, inverse_diag, orders, owners):
    moves = []
    for number, order in enumerate(orders):
        for at, (kind, index) in enumerate(order):
            if kind == "L":
                moves.append((0, index, slice(None), number, at * 512, 512))
            else:
                moves.append((1, index, slice(0, 256), number, at * 512, 256))
                moves.append((1, index, slice(256, 512), number, at * 512 + 256, 256))
    heights = [512 * len(order) for order in orders]
    heights[-1] += 16
    count = len(orders)

    def kernel(lower_ref, diag_ref, owners_ref, *refs):
        outs, held, sems = refs[:count], refs[count : 2 * count], refs[2 * count]
        plan = [
            ((lower_ref, diag_ref)[which].at[index, :, lanes], number, pl.ds(start, height))
            for which, index, lanes, number, start, height in moves
        ]
        named = pl.ds(heights[-1] - 16, 16)
        spread_out = jnp.broadcast_to(owners_ref[...].astype(F32), (16, 128)).astype(BF16)
        held[-1][named, :128] = spread_out
        held[-1][named, 128:] = jnp.zeros((16, 128), BF16)
        into, onward = [], []
        for at, (source, number, where) in enumerate(plan):
            middle = held[number].at[where]
            into.append(pltpu.make_async_copy(source, middle, sems.at[0, at]))
            onward.append(pltpu.make_async_copy(middle, outs[number].at[where], sems.at[1, at]))
        last = pltpu.make_async_copy(
            held[-1].at[named], outs[-1].at[named], sems.at[1, len(moves)]
        )
        for copy in into:
            copy.start()
        last.start()
        for first, second in zip(into, onward):
            first.wait()
            second.start()
        for copy in onward:
            copy.wait()
        last.wait()

    return pl.pallas_call(
        kernel,
        out_shape=tuple(jax.ShapeDtypeStruct((height, 256), BF16) for height in heights),
        in_specs=[HBM, HBM, VMEM],
        out_specs=(HBM,) * count,
        scratch_shapes=[pltpu.VMEM((height, 256), BF16) for height in heights]
        + [pltpu.SemaphoreType.DMA((2, len(moves) + 1))],
        compiler_params=params(60 * 1024 * 1024),
        cost_estimate=cost(0, 6 << 20),
        name="stage",
    )(lower_tiles, inverse_diag, owners)


def chosen(target, block):
    slots = lax.broadcasted_iota(jnp.int32, (256, 256), 0) + block * 256
    return jnp.where(slots == target, 1.0, 0.0).astype(BF16)


def picked(select, rows):
    return lax.dot_general(
        select, rows, (((1,), (1,)), ((), ())), preferred_element_type=F32
    )


def pack_known(place, target, known):
    def kernel(place_ref, target_ref, x1, x2, x3, out, still):
        block = pl.program_id(0)
        start = pl.multiple_of(place_ref[1] * 128, 128)
        again = pl.multiple_of(place_ref[1] * 128 + 512, 128)
        total = jnp.zeros((256, 128), F32)
        for k, ref in ((1, x1), (2, x2), (3, x3)):
            rows = jnp.concatenate([ref[:, pl.ds(start, 128)], ref[:, pl.ds(again, 128)]], axis=1)
            total = total + picked(chosen(target_ref[k], block), rows)
        out[...] = total.astype(BF16)
        still[...] = chosen(target_ref[0], block)

    return pl.pallas_call(
        kernel,
        grid=(8,),
        out_shape=(
            jax.ShapeDtypeStruct((2048, 128), BF16),
            jax.ShapeDtypeStruct((2048, 256), BF16),
        ),
        in_specs=[SCALARS, whole((4, 1, 256))] + [whole((128, 1024))] * 3,
        out_specs=(
            pl.BlockSpec((256, 128), lambda i: (i, 0)),
            pl.BlockSpec((256, 256), lambda i: (i, 0)),
        ),
        compiler_params=params(),
        cost_estimate=cost(2 * 2048 * 768 * 128, 2 << 20),
        name="pack_known",
    )(place, target, *known)


def pack_last(still, pieces, base):
    def kernel(still_ref, v0, v1, v2, v3, base_ref, out):
        rows = add_up((v0, v1, v2, v3)).astype(BF16)
        out[...] = (base_ref[...].astype(F32) + picked(still_ref[...], rows)).astype(BF16)

    return pl.pallas_call(
        kernel,
        out_shape=jax.ShapeDtypeStruct((2048, 128), BF16),
        in_specs=[VMEM] * 6,
        out_specs=VMEM,
        compiler_params=params(),
        cost_estimate=cost(2 * 2048 * 256 * 128, 2 << 20),
        name="pack_last",
    )(still, *pieces, base)


def unpack(received):
    def kernel(got, out):
        for core in range(2):
            for y in range(4):
                for x in range(4):
                    tile = got[0, core, y, x].astype(F32)
                    lanes = pl.ds((core * 4 + x) * 128, 128)
                    for half in range(2):
                        out[pl.ds(half * 32 + y * 8, 8), lanes] = tile[half * 8 : half * 8 + 8]

    return pl.pallas_call(
        kernel,
        grid=(4,),
        out_shape=jax.ShapeDtypeStruct((256, 1024), F32),
        in_specs=[pl.BlockSpec((1, 2, 4, 4, 16, 128), lambda i: (i, 0, 0, 0, 0, 0))],
        out_specs=pl.BlockSpec((64, 1024), lambda i: (i, 0)),
        compiler_params=params(),
        cost_estimate=cost(256 * 1024, 2 << 20),
        name="unpack",
    )(received.reshape(4, 2, 4, 4, 16, 128))


def slots_of(named):
    same = named[:, :, None] == named[:, None, :]
    earlier = jnp.arange(128)[None, :, None] > jnp.arange(128)[None, None, :]
    ranks = jnp.sum((same & earlier).astype(jnp.int32), axis=2)
    target = named * 16 + jnp.arange(8, dtype=jnp.int32)[:, None] * 2 + ranks
    return target.reshape(8, 4, 32).transpose(1, 0, 2).reshape(4, 1, 256)


def gathered(joined):
    rows = joined.shape[0]
    return lax.all_gather(joined, ("core", "x"), axis=0, tiled=False).reshape(2, 4, rows, 256)


def local(pivot_rhs, bound_sol, border_tiles, lower_tiles, inverse_diag, owner_map):
    z, core, y, x = (lax.axis_index(name) for name in ("z", "core", "y", "x"))
    place = jnp.stack([core, y, x, z]).astype(jnp.int32)
    lead = jnp.where((z == 0) & (core == 0), 1.0, 0.0).astype(F32)

    def tile(j, k):
        return ("L", pair_slot(j, k))

    owners = owner_map[:, :, 0]
    orders = [
        [tile(3, 2), ("D", 2), tile(3, 1), tile(2, 1), ("D", 1)],
        [tile(3, 0), tile(2, 0), tile(1, 0), ("D", 0)],
    ]
    early, late = map(gathered, stage(lower_tiles, inverse_diag, orders, owners))
    named = late[:, :, 2048, :128].astype(jnp.int32).reshape(8, 128)
    other = swap(inverse_diag[3])

    def term(side):
        start = side * 512
        rhs = lax.dynamic_slice_in_dim(pivot_rhs, start, 512, axis=2)
        bound = lax.dynamic_slice_in_dim(bound_sol, start, 512, axis=1)
        product = lax.dot_general(
            border_tiles, bound, (((0,), (0,)), ((), ())), preferred_element_type=F32
        )
        return (lead * rhs - product).astype(BF16)

    away = swap(term(1 - core))
    home = lax.optimization_barrier(term(core))
    both = (home.astype(F32) + away.astype(F32)).astype(BF16)
    def cut(part):
        return [
            lax.dynamic_slice_in_dim(part, lax.rem(x + by, 4) * 128, 128, axis=2)
            for by in range(4)
        ]

    near = deal(cut(both[2:3]), "x")
    own = both[3]
    zero = [along_z(own, 0, by) for by in (1, 2, 3)]
    token = lax.ppermute(sum(piece[:8] for piece in zero), "core", [(0, 1)])
    (held,) = gate((token,), (own,))
    one = [along_z(held, 1, by) for by in (1, 2, 3)]
    over_y = deal(first_product(place, own, zero, one, inverse_diag[3], other), "y")
    over_x = deal(first_sum(place, over_y, near[1:]), "x")
    quarter = sum(piece.astype(F32) for piece in over_x).astype(BF16)
    base2 = turn(place, near, quarter)[0]
    quarters = spread(quarter, "y")
    residual, x3 = lower_step(base2, quarters, early, 0, BF16, place)
    over_z = spread(residual, "z")
    base = turn(place, deal(gate((x3,), cut(both[:2])), "x"), over_z[2])
    pieces = spread(diag_step(over_z, early, 1), "y")
    base1, _ = lower_step(base[1], (x3,), early, 2, F32)
    residual, x2 = lower_step(base1, pieces, early, 3, BF16)
    over_z = spread(residual, "z")
    pieces = spread(diag_step(over_z, early, 4), "y")
    base0, _ = lower_step(base[0], (x3,), late, 0, F32)
    base0, _ = lower_step(base0, (x2,), late, 1, F32)
    residual, x1 = lower_step(base0, pieces, late, 2, BF16)
    over_z = spread(residual, "z")
    packed, still = pack_known(place, slots_of(named), (x1, x2, x3))
    rows = deal(last_step(place, over_z, late, 3), "y")
    packed = pack_last(still, rows, packed).reshape(128, 16, 128)
    received = lax.all_to_all(
        packed, ("z", "core", "y", "x"), split_axis=0, concat_axis=0, tiled=True
    )
    return unpack(received)


def solution(mesh):
    fine = Mesh(mesh.devices.reshape(4, 2, 4, 4), ("z", "core", "y", "x"))
    rows, cols = ("z", "core"), ("y", "x")
    placed = (
        P(None, cols, None),
        P(rows, None),
        P(rows, None, cols),
        P(None, rows, cols),
        P(None, cols, rows),
        P(rows + cols, None, None),
    )
    return jax.shard_map(
        local, mesh=fine, in_specs=placed, out_specs=P(rows + cols, None), check_vma=False
    )
```

```python
import jax
import jax.numpy as jnp
from jax import lax
from jax.experimental import pallas as pl
from jax.experimental.pallas import tpu as pltpu
from jax.sharding import Mesh, PartitionSpec as P

BF16 = jnp.bfloat16
F32 = jnp.float32
VMEM_LIMIT = 48 * 1024 * 1024


def pair_slot(later, earlier):
    return later * (later - 1) // 2 + earlier


def shift(value, axis, by):
    return lax.ppermute(value, axis, [(i, (i + by) % 4) for i in range(4)])


def swap(value):
    return lax.ppermute(value, "core", [(0, 1), (1, 0)])


def along_z(value, core, by):
    pairs = [(i * 2 + core, (i + by) % 4 * 2 + core) for i in range(4)]
    return lax.ppermute(value, ("z", "core"), pairs)


def spread(value, axis):
    far = shift(value, axis, 2)
    right = shift(value, axis, 1)
    left = shift(value, axis, 3)
    return (value, right, far, left)


def deal(pieces, axis):
    far = shift(pieces[2], axis, 2)
    right = shift(pieces[1], axis, 1)
    left = shift(pieces[3], axis, 3)
    return (pieces[0], right, far, left)


def add_up(refs):
    total = refs[0][...].astype(F32)
    for ref in refs[1:]:
        total = total + ref[...].astype(F32)
    return total


def params(limit=VMEM_LIMIT):
    return pltpu.CompilerParams(vmem_limit_bytes=limit)


def cost(flops, moved):
    return pl.CostEstimate(flops=flops, bytes_accessed=moved, transcendentals=0)


def whole(shape):
    return pl.BlockSpec(shape, lambda *_: (0,) * len(shape))


SCALARS = pl.BlockSpec(memory_space=pltpu.SMEM)
VMEM = pl.BlockSpec(memory_space=pltpu.VMEM)
ANY = pl.BlockSpec(memory_space=pl.ANY)
HBM = pl.BlockSpec(memory_space=pltpu.HBM)


def first_product(place, own, zero, one, mine, other, sent):
    def kernel(place_ref, own_ref, *refs):
        mine_ref, other_ref = refs[6:8]
        outs, full, turned = refs[-6:-2], refs[-2], refs[-1]
        core, y = place_ref[0], place_ref[1]

        @pl.when(core == 0)
        def _():
            turned[...] = add_up((own_ref, *refs[:3])).T.astype(BF16)

        @pl.when(core == 1)
        def _():
            turned[...] = add_up((own_ref, *refs[3:6])).T.astype(BF16)

        for side, tile in ((core, mine_ref), (1 - core, other_ref)):
            product = jnp.dot(turned[...], tile[...], preferred_element_type=F32)
            full[:, pl.ds(pl.multiple_of(side * 512, 512), 512)] = product.astype(BF16)
        for by, out in enumerate(outs):
            start = lax.rem(y + by, 4) * 128
            out[:, :128] = full[:, pl.ds(pl.multiple_of(start, 128), 128)]
            out[:, 128:] = full[:, pl.ds(pl.multiple_of(start + 512, 128), 128)]

    return pl.pallas_call(
        kernel,
        out_shape=(jax.ShapeDtypeStruct((512, 256), BF16),) * 4,
        in_specs=[SCALARS] + [VMEM] * 9 + [ANY] * len(sent),
        out_specs=(VMEM,) * 4,
        scratch_shapes=[pltpu.VMEM((512, 1024), BF16), pltpu.VMEM((512, 256), BF16)],
        compiler_params=params(),
        cost_estimate=cost(2 * 512 * 256 * 1024, 3 << 20),
        name="first_product",
    )(place, own, *zero, *one, mine, other, *sent)


def first_sum(place, pieces):
    def kernel(place_ref, v0, v1, v2, v3, *outs):
        for step, out in enumerate(outs):
            start = lax.rem(place_ref[2] + step, 4) * 128
            rows = pl.ds(pl.multiple_of(start, 128), 128)
            out[...] = add_up([part.at[rows] for part in (v0, v1, v2, v3)]).astype(BF16)

    return pl.pallas_call(
        kernel,
        out_shape=(jax.ShapeDtypeStruct((128, 256), BF16),) * 4,
        in_specs=[SCALARS] + [VMEM] * 4,
        out_specs=(VMEM,) * 4,
        compiler_params=params(),
        cost_estimate=cost(4 * 512 * 256, 1 << 20),
        name="first_sum",
    )(place, *pieces)


def gate(events, arrays):
    def kernel(*refs):
        pass

    count, first = len(arrays), len(events)
    return pl.pallas_call(
        kernel,
        out_shape=tuple(jax.ShapeDtypeStruct(value.shape, value.dtype) for value in arrays),
        in_specs=[ANY] * (first + count),
        out_specs=(ANY,) * count,
        input_output_aliases={first + i: i for i in range(count)},
        compiler_params=params(),
        cost_estimate=cost(0, 1024),
        name="gate",
    )(*events, *arrays)


def turn(place, pieces, event):
    blocks = pieces[0].shape[0]

    def kernel(place_ref, v0, v1, v2, v3, _, out):
        for step, ref in enumerate((v0, v1, v2, v3)):
            start = lax.rem(place_ref[2] + 4 - step, 4) * 256
            lanes = pl.ds(pl.multiple_of(start, 256), 256)
            for k in range(blocks):
                out[k, :, lanes] = ref[k].astype(F32).T

    return pl.pallas_call(
        kernel,
        out_shape=jax.ShapeDtypeStruct((blocks, 128, 1024), F32),
        in_specs=[SCALARS] + [VMEM] * 4 + [pl.BlockSpec(memory_space=pl.ANY)],
        out_specs=VMEM,
        compiler_params=params(),
        cost_estimate=cost(blocks * 128 * 1024, blocks << 20),
        name="turn",
    )(place, *pieces, event)


def lower_step(base, pieces, tiles, at, dtype, place=None):
    count = len(pieces)
    where = [] if place is None else [place]

    def kernel(*refs):
        place_ref = refs[0]
        refs = refs[len(where) :]
        parts = refs[:count]
        base_ref, tiles_ref, out, kept, tile, sems = refs[count:]
        copies = [
            pltpu.make_async_copy(
                tiles_ref.at[:, i, pl.ds(at * 512, 512), :], tile.at[:, i], sems.at[i]
            )
            for i in range(4)
        ]
        for copy in copies:
            copy.start()
        if where:
            for step, part in enumerate(parts):
                start = lax.rem(place_ref[1] + 4 - step, 4) * 128
                kept[:, pl.ds(pl.multiple_of(start, 128), 128)] = part[:, :128]
                kept[:, pl.ds(pl.multiple_of(start + 512, 128), 128)] = part[:, 128:]
        else:
            kept[...] = add_up(parts).astype(BF16)
        for i, copy in enumerate(copies):
            lanes = slice(i * 256, (i + 1) * 256)
            copy.wait()
            total = base_ref[:, lanes].astype(F32)
            total = total - jnp.dot(kept[:, :512], tile[0, i], preferred_element_type=F32)
            total = total - jnp.dot(kept[:, 512:], tile[1, i], preferred_element_type=F32)
            out[:, lanes] = total.astype(dtype)

    return pl.pallas_call(
        kernel,
        out_shape=(
            jax.ShapeDtypeStruct((128, 1024), dtype),
            jax.ShapeDtypeStruct((128, 1024), BF16),
        ),
        in_specs=[SCALARS] * len(where) + [VMEM] * (count + 1) + [HBM],
        out_specs=(VMEM, VMEM),
        scratch_shapes=[
            pltpu.VMEM((2, 4, 512, 256), BF16),
            pltpu.SemaphoreType.DMA((4,)),
        ],
        compiler_params=params(),
        cost_estimate=cost(2 * 128 * 1024 * 1024, 4 << 20),
        name="lower_step",
    )(*where, *pieces, base, tiles)


def fetch_diag(tiles_ref, at, tile, sems):
    copies = [
        pltpu.make_async_copy(
            tiles_ref.at[side, :, pl.ds(at * 512, 512), :], tile.at[side], sems.at[side]
        )
        for side in range(2)
    ]
    for copy in copies:
        copy.start()
    return copies


def times_fetched(copies, vec, tile, out):
    for side, copy in enumerate(copies):
        copy.wait()
        for half in range(2):
            rows = slice(half * 256, (half + 1) * 256)
            total = None
            for x in range(4):
                left = vec[:, x * 256 : (x + 1) * 256]
                term = jnp.dot(left, tile[side, x, rows], preferred_element_type=F32)
                total = term if total is None else total + term
            start = side * 512 + half * 256
            out[:, start : start + 256] = total.astype(BF16)


DIAG_SCRATCH = [
    pltpu.VMEM((128, 1024), BF16),
    pltpu.VMEM((2, 4, 512, 256), BF16),
    pltpu.SemaphoreType.DMA((2,)),
]


def diag_step(pieces, tiles, at):
    def kernel(v0, v1, v2, v3, tiles_ref, out, vec, tile, sems):
        copies = fetch_diag(tiles_ref, at, tile, sems)
        vec[...] = add_up((v0, v1, v2, v3)).astype(BF16)
        times_fetched(copies, vec, tile, out)

    return pl.pallas_call(
        kernel,
        out_shape=jax.ShapeDtypeStruct((128, 1024), BF16),
        in_specs=[VMEM] * 4 + [HBM],
        out_specs=VMEM,
        scratch_shapes=DIAG_SCRATCH,
        compiler_params=params(),
        cost_estimate=cost(2 * 128 * 1024 * 1024, 4 << 20),
        name="diag_step",
    )(*pieces, tiles)


def last_step(place, pieces, tiles, at):
    def kernel(place_ref, v0, v1, v2, v3, tiles_ref, o0, o1, o2, o3, vec, tile, sems, full):
        copies = fetch_diag(tiles_ref, at, tile, sems)
        vec[...] = add_up((v0, v1, v2, v3)).astype(BF16)
        times_fetched(copies, vec, tile, full)
        for by, out in enumerate((o0, o1, o2, o3)):
            start = lax.rem(place_ref[1] + by, 4) * 128
            out[:, :128] = full[:, pl.ds(pl.multiple_of(start, 128), 128)]
            out[:, 128:] = full[:, pl.ds(pl.multiple_of(start + 512, 128), 128)]

    return pl.pallas_call(
        kernel,
        out_shape=(jax.ShapeDtypeStruct((128, 256), BF16),) * 4,
        in_specs=[SCALARS] + [VMEM] * 4 + [HBM],
        out_specs=(VMEM,) * 4,
        scratch_shapes=DIAG_SCRATCH + [pltpu.VMEM((128, 1024), BF16)],
        compiler_params=params(52 * 1024 * 1024),
        cost_estimate=cost(2 * 128 * 1024 * 1024, 4 << 20),
        name="last_step",
    )(place, *pieces, tiles)


def stage(lower_tiles, inverse_diag, orders, owners):
    moves = []
    for number, order in enumerate(orders):
        for at, (kind, index) in enumerate(order):
            if kind == "L":
                moves.append((0, index, slice(None), number, at * 512, 512))
            else:
                moves.append((1, index, slice(0, 256), number, at * 512, 256))
                moves.append((1, index, slice(256, 512), number, at * 512 + 256, 256))
    heights = [512 * len(order) for order in orders]
    heights[-1] += 16
    count = len(orders)

    def kernel(lower_ref, diag_ref, owners_ref, *refs):
        outs, held, sems = refs[:count], refs[count : 2 * count], refs[2 * count]
        plan = [
            ((lower_ref, diag_ref)[which].at[index, :, lanes], number, pl.ds(start, height))
            for which, index, lanes, number, start, height in moves
        ]
        named = pl.ds(heights[-1] - 16, 16)
        spread_out = jnp.broadcast_to(owners_ref[...].astype(F32), (16, 128)).astype(BF16)
        held[-1][named, :128] = spread_out
        held[-1][named, 128:] = jnp.zeros((16, 128), BF16)
        into, onward = [], []
        for at, (source, number, where) in enumerate(plan):
            middle = held[number].at[where]
            into.append(pltpu.make_async_copy(source, middle, sems.at[0, at]))
            onward.append(pltpu.make_async_copy(middle, outs[number].at[where], sems.at[1, at]))
        last = pltpu.make_async_copy(
            held[-1].at[named], outs[-1].at[named], sems.at[1, len(moves)]
        )
        for copy in into:
            copy.start()
        last.start()
        for first, second in zip(into, onward):
            first.wait()
            second.start()
        for copy in onward:
            copy.wait()
        last.wait()

    return pl.pallas_call(
        kernel,
        out_shape=tuple(jax.ShapeDtypeStruct((height, 256), BF16) for height in heights),
        in_specs=[HBM, HBM, VMEM],
        out_specs=(HBM,) * count,
        scratch_shapes=[pltpu.VMEM((height, 256), BF16) for height in heights]
        + [pltpu.SemaphoreType.DMA((2, len(moves) + 1))],
        compiler_params=params(60 * 1024 * 1024),
        cost_estimate=cost(0, 6 << 20),
        name="stage",
    )(lower_tiles, inverse_diag, owners)


def chosen(target, block):
    slots = lax.broadcasted_iota(jnp.int32, (256, 256), 0) + block * 256
    return jnp.where(slots == target, 1.0, 0.0).astype(BF16)


def picked(select, rows):
    return lax.dot_general(
        select, rows, (((1,), (1,)), ((), ())), preferred_element_type=F32
    )


def pack_known(place, target, known):
    def kernel(place_ref, target_ref, x1, x2, x3, out, still):
        block = pl.program_id(0)
        start = pl.multiple_of(place_ref[1] * 128, 128)
        again = pl.multiple_of(place_ref[1] * 128 + 512, 128)
        total = jnp.zeros((256, 128), F32)
        for k, ref in ((1, x1), (2, x2), (3, x3)):
            rows = jnp.concatenate([ref[:, pl.ds(start, 128)], ref[:, pl.ds(again, 128)]], axis=1)
            total = total + picked(chosen(target_ref[k], block), rows)
        out[...] = total.astype(BF16)
        still[...] = chosen(target_ref[0], block)

    return pl.pallas_call(
        kernel,
        grid=(8,),
        out_shape=(
            jax.ShapeDtypeStruct((2048, 128), BF16),
            jax.ShapeDtypeStruct((2048, 256), BF16),
        ),
        in_specs=[SCALARS, whole((4, 1, 256))] + [whole((128, 1024))] * 3,
        out_specs=(
            pl.BlockSpec((256, 128), lambda i: (i, 0)),
            pl.BlockSpec((256, 256), lambda i: (i, 0)),
        ),
        compiler_params=params(),
        cost_estimate=cost(2 * 2048 * 768 * 128, 2 << 20),
        name="pack_known",
    )(place, target, *known)


def pack_last(still, pieces, base):
    def kernel(still_ref, v0, v1, v2, v3, base_ref, out):
        rows = add_up((v0, v1, v2, v3)).astype(BF16)
        out[...] = (base_ref[...].astype(F32) + picked(still_ref[...], rows)).astype(BF16)

    return pl.pallas_call(
        kernel,
        out_shape=jax.ShapeDtypeStruct((2048, 128), BF16),
        in_specs=[VMEM] * 6,
        out_specs=VMEM,
        compiler_params=params(),
        cost_estimate=cost(2 * 2048 * 256 * 128, 2 << 20),
        name="pack_last",
    )(still, *pieces, base)


def unpack(received):
    def kernel(got, out):
        for core in range(2):
            for y in range(4):
                for x in range(4):
                    tile = got[0, core, y, x].astype(F32)
                    lanes = pl.ds((core * 4 + x) * 128, 128)
                    for half in range(2):
                        out[pl.ds(half * 32 + y * 8, 8), lanes] = tile[half * 8 : half * 8 + 8]

    return pl.pallas_call(
        kernel,
        grid=(4,),
        out_shape=jax.ShapeDtypeStruct((256, 1024), F32),
        in_specs=[pl.BlockSpec((1, 2, 4, 4, 16, 128), lambda i: (i, 0, 0, 0, 0, 0))],
        out_specs=pl.BlockSpec((64, 1024), lambda i: (i, 0)),
        compiler_params=params(),
        cost_estimate=cost(256 * 1024, 2 << 20),
        name="unpack",
    )(received.reshape(4, 2, 4, 4, 16, 128))


def slots_of(named):
    same = named[:, :, None] == named[:, None, :]
    earlier = jnp.arange(128)[None, :, None] > jnp.arange(128)[None, None, :]
    ranks = jnp.sum((same & earlier).astype(jnp.int32), axis=2)
    target = named * 16 + jnp.arange(8, dtype=jnp.int32)[:, None] * 2 + ranks
    return target.reshape(8, 4, 32).transpose(1, 0, 2).reshape(4, 1, 256)


def gathered(joined):
    rows = joined.shape[0]
    return lax.all_gather(joined, ("core", "x"), axis=0, tiled=False).reshape(2, 4, rows, 256)


def local(pivot_rhs, bound_sol, border_tiles, lower_tiles, inverse_diag, owner_map):
    z, core, y, x = (lax.axis_index(name) for name in ("z", "core", "y", "x"))
    place = jnp.stack([core, y, x, z]).astype(jnp.int32)
    lead = jnp.where((z == 0) & (core == 0), 1.0, 0.0).astype(F32)

    def tile(j, k):
        return ("L", pair_slot(j, k))

    owners = owner_map[:, :, 0]
    orders = [
        [tile(3, 2), ("D", 2), tile(3, 1), tile(2, 1), ("D", 1)],
        [tile(3, 0), tile(2, 0), tile(1, 0), ("D", 0)],
    ]
    early, late = map(gathered, stage(lower_tiles, inverse_diag, orders, owners))
    named = late[:, :, 2048, :128].astype(jnp.int32).reshape(8, 128)
    other = swap(inverse_diag[3])

    def term(side):
        start = side * 512
        rhs = lax.dynamic_slice_in_dim(pivot_rhs, start, 512, axis=2)
        bound = lax.dynamic_slice_in_dim(bound_sol, start, 512, axis=1)
        product = lax.dot_general(
            border_tiles, bound, (((0,), (0,)), ((), ())), preferred_element_type=F32
        )
        return (lead * rhs - product).astype(BF16)

    away = swap(term(1 - core))
    home = lax.optimization_barrier(term(core))
    both = (home.astype(F32) + away.astype(F32)).astype(BF16)
    def cut(part):
        return [
            lax.dynamic_slice_in_dim(part, lax.rem(x + by, 4) * 128, 128, axis=2)
            for by in range(4)
        ]

    near = deal(cut(both[2:3]), "x")
    own = both[3]
    zero = [along_z(own, 0, by) for by in (1, 2, 3)]
    token = lax.ppermute(sum(piece[:8] for piece in zero), "core", [(0, 1)])
    (held,) = gate((token, *near[1:]), (own,))
    one = [along_z(held, 1, by) for by in (1, 2, 3)]
    products = first_product(place, own, zero, one, inverse_diag[3], other, near[1:])
    over_x = deal(first_sum(place, deal(products, "y")), "x")
    quarter = sum(piece.astype(F32) for piece in over_x).astype(BF16)
    base2 = turn(place, near, quarter)[0]
    quarters = spread(quarter, "y")
    residual, x3 = lower_step(base2, quarters, early, 0, BF16, place)
    over_z = spread(residual, "z")
    base = turn(place, deal(gate((x3,), cut(both[:2])), "x"), over_z[2])
    pieces = spread(diag_step(over_z, early, 1), "y")
    base1, _ = lower_step(base[1], (x3,), early, 2, F32)
    residual, x2 = lower_step(base1, pieces, early, 3, BF16)
    over_z = spread(residual, "z")
    pieces = spread(diag_step(over_z, early, 4), "y")
    base0, _ = lower_step(base[0], (x3,), late, 0, F32)
    base0, _ = lower_step(base0, (x2,), late, 1, F32)
    residual, x1 = lower_step(base0, pieces, late, 2, BF16)
    over_z = spread(residual, "z")
    packed, still = pack_known(place, slots_of(named), (x1, x2, x3))
    rows = deal(last_step(place, over_z, late, 3), "y")
    packed = pack_last(still, rows, packed).reshape(128, 16, 128)
    received = lax.all_to_all(
        packed, ("z", "core", "y", "x"), split_axis=0, concat_axis=0, tiled=True
    )
    return unpack(received)


def solution(mesh):
    fine = Mesh(mesh.devices.reshape(4, 2, 4, 4), ("z", "core", "y", "x"))
    rows, cols = ("z", "core"), ("y", "x")
    placed = (
        P(None, cols, None),
        P(rows, None),
        P(rows, None, cols),
        P(None, rows, cols),
        P(None, cols, rows),
        P(rows + cols, None, None),
    )
    return jax.shard_map(
        local, mesh=fine, in_specs=placed, out_specs=P(rows + cols, None), check_vma=False
    )
```

```python
import jax
import jax.numpy as jnp
from jax import lax
from jax.experimental import pallas as pl
from jax.experimental.pallas import tpu as pltpu
from jax.sharding import Mesh, PartitionSpec as P

BF16 = jnp.bfloat16
F32 = jnp.float32
VMEM_LIMIT = 48 * 1024 * 1024


def pair_slot(later, earlier):
    return later * (later - 1) // 2 + earlier


def shift(value, axis, by):
    return lax.ppermute(value, axis, [(i, (i + by) % 4) for i in range(4)])


def swap(value):
    return lax.ppermute(value, "core", [(0, 1), (1, 0)])


def along_z(value, core, by):
    pairs = [(i * 2 + core, (i + by) % 4 * 2 + core) for i in range(4)]
    return lax.ppermute(value, ("z", "core"), pairs)


def spread(value, axis):
    far = shift(value, axis, 2)
    right = shift(value, axis, 1)
    left = shift(value, axis, 3)
    return (value, right, far, left)


def deal(pieces, axis):
    far = shift(pieces[2], axis, 2)
    right = shift(pieces[1], axis, 1)
    left = shift(pieces[3], axis, 3)
    return (pieces[0], right, far, left)


def add_up(refs):
    total = refs[0][...].astype(F32)
    for ref in refs[1:]:
        total = total + ref[...].astype(F32)
    return total


def params(limit=VMEM_LIMIT):
    return pltpu.CompilerParams(vmem_limit_bytes=limit)


def cost(flops, moved):
    return pl.CostEstimate(flops=flops, bytes_accessed=moved, transcendentals=0)


def whole(shape):
    return pl.BlockSpec(shape, lambda *_: (0,) * len(shape))


SCALARS = pl.BlockSpec(memory_space=pltpu.SMEM)
VMEM = pl.BlockSpec(memory_space=pltpu.VMEM)
ANY = pl.BlockSpec(memory_space=pl.ANY)
HBM = pl.BlockSpec(memory_space=pltpu.HBM)


def first_product(place, own, zero, one, mine, other, sent):
    def kernel(place_ref, own_ref, *refs):
        mine_ref, other_ref = refs[6:8]
        outs, full, turned = refs[-6:-2], refs[-2], refs[-1]
        core, y = place_ref[0], place_ref[1]

        @pl.when(core == 0)
        def _():
            turned[...] = add_up((own_ref, *refs[:3])).T.astype(BF16)

        @pl.when(core == 1)
        def _():
            turned[...] = add_up((own_ref, *refs[3:6])).T.astype(BF16)

        for side, tile in ((core, mine_ref), (1 - core, other_ref)):
            product = jnp.dot(turned[...], tile[...], preferred_element_type=F32)
            full[:, pl.ds(pl.multiple_of(side * 512, 512), 512)] = product.astype(BF16)
        for by, out in enumerate(outs):
            start = lax.rem(y + by, 4) * 128
            out[:, :128] = full[:, pl.ds(pl.multiple_of(start, 128), 128)]
            out[:, 128:] = full[:, pl.ds(pl.multiple_of(start + 512, 128), 128)]

    return pl.pallas_call(
        kernel,
        out_shape=(jax.ShapeDtypeStruct((512, 256), BF16),) * 4,
        in_specs=[SCALARS] + [VMEM] * 9 + [ANY] * len(sent),
        out_specs=(VMEM,) * 4,
        scratch_shapes=[pltpu.VMEM((512, 1024), BF16), pltpu.VMEM((512, 256), BF16)],
        compiler_params=params(),
        cost_estimate=cost(2 * 512 * 256 * 1024, 3 << 20),
        name="first_product",
    )(place, own, *zero, *one, mine, other, *sent)


def first_sum(place, pieces):
    def kernel(place_ref, v0, v1, v2, v3, *outs):
        for step, out in enumerate(outs):
            start = lax.rem(place_ref[2] + step, 4) * 128
            rows = pl.ds(pl.multiple_of(start, 128), 128)
            out[...] = add_up([part.at[rows] for part in (v0, v1, v2, v3)]).astype(BF16)

    return pl.pallas_call(
        kernel,
        out_shape=(jax.ShapeDtypeStruct((128, 256), BF16),) * 4,
        in_specs=[SCALARS] + [VMEM] * 4,
        out_specs=(VMEM,) * 4,
        compiler_params=params(),
        cost_estimate=cost(4 * 512 * 256, 1 << 20),
        name="first_sum",
    )(place, *pieces)


def gate(events, arrays):
    def kernel(*refs):
        pass

    count, first = len(arrays), len(events)
    return pl.pallas_call(
        kernel,
        out_shape=tuple(jax.ShapeDtypeStruct(value.shape, value.dtype) for value in arrays),
        in_specs=[ANY] * (first + count),
        out_specs=(ANY,) * count,
        input_output_aliases={first + i: i for i in range(count)},
        compiler_params=params(),
        cost_estimate=cost(0, 1024),
        name="gate",
    )(*events, *arrays)


def in_turn(value, events):
    zero = [along_z(value, 0, by) for by in (1, 2, 3)]
    token = lax.ppermute(sum(piece[:8] for piece in zero), "core", [(0, 1)])
    (held,) = gate((token, *events), (value,))
    one = [along_z(held, 1, by) for by in (1, 2, 3)]
    return (value, *zero, *one)


def turn(place, pieces, event):
    blocks = pieces[0].shape[0]

    def kernel(place_ref, v0, v1, v2, v3, _, out):
        for step, ref in enumerate((v0, v1, v2, v3)):
            start = lax.rem(place_ref[2] + 4 - step, 4) * 256
            lanes = pl.ds(pl.multiple_of(start, 256), 256)
            for k in range(blocks):
                out[k, :, lanes] = ref[k].astype(F32).T

    return pl.pallas_call(
        kernel,
        out_shape=jax.ShapeDtypeStruct((blocks, 128, 1024), F32),
        in_specs=[SCALARS] + [VMEM] * 4 + [pl.BlockSpec(memory_space=pl.ANY)],
        out_specs=VMEM,
        compiler_params=params(),
        cost_estimate=cost(blocks * 128 * 1024, blocks << 20),
        name="turn",
    )(place, *pieces, event)


def lower_step(base, pieces, tiles, at, dtype, place=None):
    count = len(pieces)
    where = [] if place is None else [place]

    def kernel(*refs):
        place_ref = refs[0]
        refs = refs[len(where) :]
        parts = refs[:count]
        base_ref, tiles_ref, out, kept, tile, sems = refs[count:]
        copies = [
            pltpu.make_async_copy(
                tiles_ref.at[:, i, pl.ds(at * 512, 512), :], tile.at[:, i], sems.at[i]
            )
            for i in range(4)
        ]
        for copy in copies:
            copy.start()
        if where:
            for step, part in enumerate(parts):
                start = lax.rem(place_ref[1] + 4 - step, 4) * 128
                kept[:, pl.ds(pl.multiple_of(start, 128), 128)] = part[:, :128]
                kept[:, pl.ds(pl.multiple_of(start + 512, 128), 128)] = part[:, 128:]
        else:
            kept[...] = add_up(parts).astype(BF16)
        for i, copy in enumerate(copies):
            lanes = slice(i * 256, (i + 1) * 256)
            copy.wait()
            total = base_ref[:, lanes].astype(F32)
            total = total - jnp.dot(kept[:, :512], tile[0, i], preferred_element_type=F32)
            total = total - jnp.dot(kept[:, 512:], tile[1, i], preferred_element_type=F32)
            out[:, lanes] = total.astype(dtype)

    return pl.pallas_call(
        kernel,
        out_shape=(
            jax.ShapeDtypeStruct((128, 1024), dtype),
            jax.ShapeDtypeStruct((128, 1024), BF16),
        ),
        in_specs=[SCALARS] * len(where) + [VMEM] * (count + 1) + [HBM],
        out_specs=(VMEM, VMEM),
        scratch_shapes=[
            pltpu.VMEM((2, 4, 512, 256), BF16),
            pltpu.SemaphoreType.DMA((4,)),
        ],
        compiler_params=params(),
        cost_estimate=cost(2 * 128 * 1024 * 1024, 4 << 20),
        name="lower_step",
    )(*where, *pieces, base, tiles)


def fetch_diag(tiles_ref, at, tile, sems):
    copies = [
        pltpu.make_async_copy(
            tiles_ref.at[side, :, pl.ds(at * 512, 512), :], tile.at[side], sems.at[side]
        )
        for side in range(2)
    ]
    for copy in copies:
        copy.start()
    return copies


def times_fetched(copies, vec, tile, out):
    for side, copy in enumerate(copies):
        copy.wait()
        for half in range(2):
            rows = slice(half * 256, (half + 1) * 256)
            total = None
            for x in range(4):
                left = vec[:, x * 256 : (x + 1) * 256]
                term = jnp.dot(left, tile[side, x, rows], preferred_element_type=F32)
                total = term if total is None else total + term
            start = side * 512 + half * 256
            out[:, start : start + 256] = total.astype(BF16)


DIAG_SCRATCH = [
    pltpu.VMEM((128, 1024), BF16),
    pltpu.VMEM((2, 4, 512, 256), BF16),
    pltpu.SemaphoreType.DMA((2,)),
]


def diag_step(pieces, tiles, at, place=None):
    count = len(pieces)
    where = [] if place is None else [place]

    def kernel(*refs):
        place_ref = refs[0]
        refs = refs[len(where) :]
        tiles_ref, out, vec, tile, sems = refs[count:]
        copies = fetch_diag(tiles_ref, at, tile, sems)
        if where:

            @pl.when(place_ref[0] == 0)
            def _():
                vec[...] = add_up(refs[:4]).astype(BF16)

            @pl.when(place_ref[0] == 1)
            def _():
                vec[...] = add_up((refs[0], *refs[4:7])).astype(BF16)

        else:
            vec[...] = add_up(refs[:4]).astype(BF16)
        times_fetched(copies, vec, tile, out)

    return pl.pallas_call(
        kernel,
        out_shape=jax.ShapeDtypeStruct((128, 1024), BF16),
        in_specs=[SCALARS] * len(where) + [VMEM] * count + [HBM],
        out_specs=VMEM,
        scratch_shapes=DIAG_SCRATCH,
        compiler_params=params(),
        cost_estimate=cost(2 * 128 * 1024 * 1024, 4 << 20),
        name="diag_step",
    )(*where, *pieces, tiles)


def last_step(place, pieces, tiles, at):
    def kernel(place_ref, v0, v1, v2, v3, tiles_ref, o0, o1, o2, o3, vec, tile, sems, full):
        copies = fetch_diag(tiles_ref, at, tile, sems)
        vec[...] = add_up((v0, v1, v2, v3)).astype(BF16)
        times_fetched(copies, vec, tile, full)
        for by, out in enumerate((o0, o1, o2, o3)):
            start = lax.rem(place_ref[1] + by, 4) * 128
            out[:, :128] = full[:, pl.ds(pl.multiple_of(start, 128), 128)]
            out[:, 128:] = full[:, pl.ds(pl.multiple_of(start + 512, 128), 128)]

    return pl.pallas_call(
        kernel,
        out_shape=(jax.ShapeDtypeStruct((128, 256), BF16),) * 4,
        in_specs=[SCALARS] + [VMEM] * 4 + [HBM],
        out_specs=(VMEM,) * 4,
        scratch_shapes=DIAG_SCRATCH + [pltpu.VMEM((128, 1024), BF16)],
        compiler_params=params(52 * 1024 * 1024),
        cost_estimate=cost(2 * 128 * 1024 * 1024, 4 << 20),
        name="last_step",
    )(place, *pieces, tiles)


def stage(lower_tiles, inverse_diag, orders, owners):
    moves = []
    for number, order in enumerate(orders):
        for at, (kind, index) in enumerate(order):
            if kind == "L":
                moves.append((0, index, slice(None), number, at * 512, 512))
            else:
                moves.append((1, index, slice(0, 256), number, at * 512, 256))
                moves.append((1, index, slice(256, 512), number, at * 512 + 256, 256))
    heights = [512 * len(order) for order in orders]
    heights[-1] += 16
    count = len(orders)

    def kernel(lower_ref, diag_ref, owners_ref, *refs):
        outs, held, sems = refs[:count], refs[count : 2 * count], refs[2 * count]
        plan = [
            ((lower_ref, diag_ref)[which].at[index, :, lanes], number, pl.ds(start, height))
            for which, index, lanes, number, start, height in moves
        ]
        named = pl.ds(heights[-1] - 16, 16)
        spread_out = jnp.broadcast_to(owners_ref[...].astype(F32), (16, 128)).astype(BF16)
        held[-1][named, :128] = spread_out
        held[-1][named, 128:] = jnp.zeros((16, 128), BF16)
        into, onward = [], []
        for at, (source, number, where) in enumerate(plan):
            middle = held[number].at[where]
            into.append(pltpu.make_async_copy(source, middle, sems.at[0, at]))
            onward.append(pltpu.make_async_copy(middle, outs[number].at[where], sems.at[1, at]))
        last = pltpu.make_async_copy(
            held[-1].at[named], outs[-1].at[named], sems.at[1, len(moves)]
        )
        for copy in into:
            copy.start()
        last.start()
        for first, second in zip(into, onward):
            first.wait()
            second.start()
        for copy in onward:
            copy.wait()
        last.wait()

    return pl.pallas_call(
        kernel,
        out_shape=tuple(jax.ShapeDtypeStruct((height, 256), BF16) for height in heights),
        in_specs=[HBM, HBM, VMEM],
        out_specs=(HBM,) * count,
        scratch_shapes=[pltpu.VMEM((height, 256), BF16) for height in heights]
        + [pltpu.SemaphoreType.DMA((2, len(moves) + 1))],
        compiler_params=params(60 * 1024 * 1024),
        cost_estimate=cost(0, 6 << 20),
        name="stage",
    )(lower_tiles, inverse_diag, owners)


def chosen(target, block):
    slots = lax.broadcasted_iota(jnp.int32, (256, 256), 0) + block * 256
    return jnp.where(slots == target, 1.0, 0.0).astype(BF16)


def picked(select, rows):
    return lax.dot_general(
        select, rows, (((1,), (1,)), ((), ())), preferred_element_type=F32
    )


def pack_known(place, target, known):
    def kernel(place_ref, target_ref, x1, x2, x3, out, still):
        block = pl.program_id(0)
        start = pl.multiple_of(place_ref[1] * 128, 128)
        again = pl.multiple_of(place_ref[1] * 128 + 512, 128)
        total = jnp.zeros((256, 128), F32)
        for k, ref in ((1, x1), (2, x2), (3, x3)):
            rows = jnp.concatenate([ref[:, pl.ds(start, 128)], ref[:, pl.ds(again, 128)]], axis=1)
            total = total + picked(chosen(target_ref[k], block), rows)
        out[...] = total.astype(BF16)
        still[...] = chosen(target_ref[0], block)

    return pl.pallas_call(
        kernel,
        grid=(8,),
        out_shape=(
            jax.ShapeDtypeStruct((2048, 128), BF16),
            jax.ShapeDtypeStruct((2048, 256), BF16),
        ),
        in_specs=[SCALARS, whole((4, 1, 256))] + [whole((128, 1024))] * 3,
        out_specs=(
            pl.BlockSpec((256, 128), lambda i: (i, 0)),
            pl.BlockSpec((256, 256), lambda i: (i, 0)),
        ),
        compiler_params=params(),
        cost_estimate=cost(2 * 2048 * 768 * 128, 2 << 20),
        name="pack_known",
    )(place, target, *known)


def pack_last(still, pieces, base):
    def kernel(still_ref, v0, v1, v2, v3, base_ref, out):
        rows = add_up((v0, v1, v2, v3)).astype(BF16)
        out[...] = (base_ref[...].astype(F32) + picked(still_ref[...], rows)).astype(BF16)

    return pl.pallas_call(
        kernel,
        out_shape=jax.ShapeDtypeStruct((2048, 128), BF16),
        in_specs=[VMEM] * 6,
        out_specs=VMEM,
        compiler_params=params(),
        cost_estimate=cost(2 * 2048 * 256 * 128, 2 << 20),
        name="pack_last",
    )(still, *pieces, base)


def unpack(received):
    def kernel(got, out):
        for core in range(2):
            for y in range(4):
                for x in range(4):
                    tile = got[0, core, y, x].astype(F32)
                    lanes = pl.ds((core * 4 + x) * 128, 128)
                    for half in range(2):
                        out[pl.ds(half * 32 + y * 8, 8), lanes] = tile[half * 8 : half * 8 + 8]

    return pl.pallas_call(
        kernel,
        grid=(4,),
        out_shape=jax.ShapeDtypeStruct((256, 1024), F32),
        in_specs=[pl.BlockSpec((1, 2, 4, 4, 16, 128), lambda i: (i, 0, 0, 0, 0, 0))],
        out_specs=pl.BlockSpec((64, 1024), lambda i: (i, 0)),
        compiler_params=params(),
        cost_estimate=cost(256 * 1024, 2 << 20),
        name="unpack",
    )(received.reshape(4, 2, 4, 4, 16, 128))


def slots_of(named):
    same = named[:, :, None] == named[:, None, :]
    earlier = jnp.arange(128)[None, :, None] > jnp.arange(128)[None, None, :]
    ranks = jnp.sum((same & earlier).astype(jnp.int32), axis=2)
    target = named * 16 + jnp.arange(8, dtype=jnp.int32)[:, None] * 2 + ranks
    return target.reshape(8, 4, 32).transpose(1, 0, 2).reshape(4, 1, 256)


def gathered(joined):
    rows = joined.shape[0]
    return lax.all_gather(joined, ("core", "x"), axis=0, tiled=False).reshape(2, 4, rows, 256)


def local(pivot_rhs, bound_sol, border_tiles, lower_tiles, inverse_diag, owner_map):
    z, core, y, x = (lax.axis_index(name) for name in ("z", "core", "y", "x"))
    place = jnp.stack([core, y, x, z]).astype(jnp.int32)
    lead = jnp.where((z == 0) & (core == 0), 1.0, 0.0).astype(F32)

    def tile(j, k):
        return ("L", pair_slot(j, k))

    owners = owner_map[:, :, 0]
    orders = [
        [tile(3, 2), ("D", 2), tile(3, 1), tile(2, 1), ("D", 1)],
        [tile(3, 0), tile(2, 0), tile(1, 0), ("D", 0)],
    ]
    early, late = map(gathered, stage(lower_tiles, inverse_diag, orders, owners))
    named = late[:, :, 2048, :128].astype(jnp.int32).reshape(8, 128)
    other = swap(inverse_diag[3])

    def term(side):
        start = side * 512
        rhs = lax.dynamic_slice_in_dim(pivot_rhs, start, 512, axis=2)
        bound = lax.dynamic_slice_in_dim(bound_sol, start, 512, axis=1)
        product = lax.dot_general(
            border_tiles, bound, (((0,), (0,)), ((), ())), preferred_element_type=F32
        )
        return (lead * rhs - product).astype(BF16)

    away = swap(term(1 - core))
    home = lax.optimization_barrier(term(core))
    both = (home.astype(F32) + away.astype(F32)).astype(BF16)
    def cut(part):
        return [
            lax.dynamic_slice_in_dim(part, lax.rem(x + by, 4) * 128, 128, axis=2)
            for by in range(4)
        ]

    near = deal(cut(both[2:3]), "x")
    own = both[3]
    over_z = in_turn(own, near[1:])
    zero, one = over_z[1:4], over_z[4:]
    products = first_product(place, own, zero, one, inverse_diag[3], other, near[1:])
    over_x = deal(first_sum(place, deal(products, "y")), "x")
    quarter = sum(piece.astype(F32) for piece in over_x).astype(BF16)
    base2 = turn(place, near, quarter)[0]
    quarters = spread(quarter, "y")
    residual, x3 = lower_step(base2, quarters, early, 0, BF16, place)
    over_z = in_turn(residual, ())
    pieces = spread(diag_step(over_z, early, 1, place), "y")
    base = turn(place, deal(gate((x3,), cut(both[:2])), "x"), pieces[0])
    base1, _ = lower_step(base[1], (x3,), early, 2, F32)
    residual, x2 = lower_step(base1, pieces, early, 3, BF16)
    over_z = spread(residual, "z")
    pieces = spread(diag_step(over_z, early, 4), "y")
    base0, _ = lower_step(base[0], (x3,), late, 0, F32)
    base0, _ = lower_step(base0, (x2,), late, 1, F32)
    residual, x1 = lower_step(base0, pieces, late, 2, BF16)
    over_z = spread(residual, "z")
    packed, still = pack_known(place, slots_of(named), (x1, x2, x3))
    rows = deal(last_step(place, over_z, late, 3), "y")
    packed = pack_last(still, rows, packed).reshape(128, 16, 128)
    received = lax.all_to_all(
        packed, ("z", "core", "y", "x"), split_axis=0, concat_axis=0, tiled=True
    )
    return unpack(received)


def solution(mesh):
    fine = Mesh(mesh.devices.reshape(4, 2, 4, 4), ("z", "core", "y", "x"))
    rows, cols = ("z", "core"), ("y", "x")
    placed = (
        P(None, cols, None),
        P(rows, None),
        P(rows, None, cols),
        P(None, rows, cols),
        P(None, cols, rows),
        P(rows + cols, None, None),
    )
    return jax.shard_map(
        local, mesh=fine, in_specs=placed, out_specs=P(rows + cols, None), check_vma=False
    )
```

```python
import jax
import jax.numpy as jnp
from jax import lax
from jax.experimental import pallas as pl
from jax.experimental.pallas import tpu as pltpu
from jax.sharding import Mesh, PartitionSpec as P

BF16 = jnp.bfloat16
F32 = jnp.float32
VMEM_LIMIT = 48 * 1024 * 1024


def pair_slot(later, earlier):
    return later * (later - 1) // 2 + earlier


def shift(value, axis, by):
    return lax.ppermute(value, axis, [(i, (i + by) % 4) for i in range(4)])


def swap(value):
    return lax.ppermute(value, "core", [(0, 1), (1, 0)])


def along_y(value, core, by):
    pairs = [(core * 4 + i, core * 4 + (i + by) % 4) for i in range(4)]
    return lax.ppermute(value, ("core", "y"), pairs)


def spread(value, axis):
    far = shift(value, axis, 2)
    right = shift(value, axis, 1)
    left = shift(value, axis, 3)
    return (value, right, far, left)


def deal(pieces, axis):
    far = shift(pieces[2], axis, 2)
    right = shift(pieces[1], axis, 1)
    left = shift(pieces[3], axis, 3)
    return (pieces[0], right, far, left)


def add_up(refs):
    total = refs[0][...].astype(F32)
    for ref in refs[1:]:
        total = total + ref[...].astype(F32)
    return total


def params(limit=VMEM_LIMIT):
    return pltpu.CompilerParams(vmem_limit_bytes=limit)


def cost(flops, moved):
    return pl.CostEstimate(flops=flops, bytes_accessed=moved, transcendentals=0)


def whole(shape):
    return pl.BlockSpec(shape, lambda *_: (0,) * len(shape))


SCALARS = pl.BlockSpec(memory_space=pltpu.SMEM)
VMEM = pl.BlockSpec(memory_space=pltpu.VMEM)
ANY = pl.BlockSpec(memory_space=pl.ANY)
HBM = pl.BlockSpec(memory_space=pltpu.HBM)


def first_product(place, pieces, mine, other, sent):
    def kernel(place_ref, v0, v1, v2, v3, mine_ref, other_ref, *refs):
        outs, full = refs[len(sent) : len(sent) + 4], refs[len(sent) + 4]
        core, y = place_ref[0], place_ref[1]
        turned = add_up((v0, v1, v2, v3)).T.astype(BF16)
        for side, tile in ((core, mine_ref), (1 - core, other_ref)):
            product = jnp.dot(turned, tile[...], preferred_element_type=F32)
            full[:, pl.ds(pl.multiple_of(side * 512, 512), 512)] = product.astype(BF16)
        for by, out in enumerate(outs):
            start = lax.rem(y + by, 4) * 128
            out[:, :128] = full[:, pl.ds(pl.multiple_of(start, 128), 128)]
            out[:, 128:] = full[:, pl.ds(pl.multiple_of(start + 512, 128), 128)]

    return pl.pallas_call(
        kernel,
        out_shape=(jax.ShapeDtypeStruct((512, 256), BF16),) * 4,
        in_specs=[SCALARS] + [VMEM] * 6 + [ANY] * len(sent),
        out_specs=(VMEM,) * 4,
        scratch_shapes=[pltpu.VMEM((512, 1024), BF16)],
        compiler_params=params(),
        cost_estimate=cost(2 * 512 * 256 * 1024, 3 << 20),
        name="first_product",
    )(place, *pieces, mine, other, *sent)


def first_sum(place, own, zero, one):
    def kernel(place_ref, own_ref, *refs):
        outs = refs[6:]

        def body(parts):
            for step, out in enumerate(outs):
                start = lax.rem(place_ref[2] + step, 4) * 128
                rows = pl.ds(pl.multiple_of(start, 128), 128)
                out[...] = add_up([part.at[rows] for part in (own_ref, *parts)]).astype(BF16)

        @pl.when(place_ref[0] == 0)
        def _():
            body(refs[:3])

        @pl.when(place_ref[0] == 1)
        def _():
            body(refs[3:6])

    return pl.pallas_call(
        kernel,
        out_shape=(jax.ShapeDtypeStruct((128, 256), BF16),) * 4,
        in_specs=[SCALARS] + [VMEM] * 7,
        out_specs=(VMEM,) * 4,
        compiler_params=params(),
        cost_estimate=cost(4 * 512 * 256, 1 << 20),
        name="first_sum",
    )(place, own, *zero, *one)


def gate(events, arrays):
    def kernel(*refs):
        pass

    count, first = len(arrays), len(events)
    return pl.pallas_call(
        kernel,
        out_shape=tuple(jax.ShapeDtypeStruct(value.shape, value.dtype) for value in arrays),
        in_specs=[ANY] * (first + count),
        out_specs=(ANY,) * count,
        input_output_aliases={first + i: i for i in range(count)},
        compiler_params=params(),
        cost_estimate=cost(0, 1024),
        name="gate",
    )(*events, *arrays)


def turn(place, pieces, event):
    blocks = pieces[0].shape[0]

    def kernel(place_ref, v0, v1, v2, v3, _, out):
        for step, ref in enumerate((v0, v1, v2, v3)):
            start = lax.rem(place_ref[2] + 4 - step, 4) * 256
            lanes = pl.ds(pl.multiple_of(start, 256), 256)
            for k in range(blocks):
                out[k, :, lanes] = ref[k].astype(F32).T

    return pl.pallas_call(
        kernel,
        out_shape=jax.ShapeDtypeStruct((blocks, 128, 1024), F32),
        in_specs=[SCALARS] + [VMEM] * 4 + [pl.BlockSpec(memory_space=pl.ANY)],
        out_specs=VMEM,
        compiler_params=params(),
        cost_estimate=cost(blocks * 128 * 1024, blocks << 20),
        name="turn",
    )(place, *pieces, event)


def lower_step(base, pieces, tiles, at, dtype, place=None):
    count = len(pieces)
    where = [] if place is None else [place]

    def kernel(*refs):
        place_ref = refs[0]
        refs = refs[len(where) :]
        parts = refs[:count]
        base_ref, tiles_ref, out, kept, tile, sems = refs[count:]
        copies = [
            pltpu.make_async_copy(
                tiles_ref.at[:, i, pl.ds(at * 512, 512), :], tile.at[:, i], sems.at[i]
            )
            for i in range(4)
        ]
        for copy in copies:
            copy.start()
        if where:
            for step, part in enumerate(parts):
                start = lax.rem(place_ref[1] + 4 - step, 4) * 128
                kept[:, pl.ds(pl.multiple_of(start, 128), 128)] = part[:, :128]
                kept[:, pl.ds(pl.multiple_of(start + 512, 128), 128)] = part[:, 128:]
        else:
            kept[...] = add_up(parts).astype(BF16)
        for i, copy in enumerate(copies):
            lanes = slice(i * 256, (i + 1) * 256)
            copy.wait()
            total = base_ref[:, lanes].astype(F32)
            total = total - jnp.dot(kept[:, :512], tile[0, i], preferred_element_type=F32)
            total = total - jnp.dot(kept[:, 512:], tile[1, i], preferred_element_type=F32)
            out[:, lanes] = total.astype(dtype)

    return pl.pallas_call(
        kernel,
        out_shape=(
            jax.ShapeDtypeStruct((128, 1024), dtype),
            jax.ShapeDtypeStruct((128, 1024), BF16),
        ),
        in_specs=[SCALARS] * len(where) + [VMEM] * (count + 1) + [HBM],
        out_specs=(VMEM, VMEM),
        scratch_shapes=[
            pltpu.VMEM((2, 4, 512, 256), BF16),
            pltpu.SemaphoreType.DMA((4,)),
        ],
        compiler_params=params(),
        cost_estimate=cost(2 * 128 * 1024 * 1024, 4 << 20),
        name="lower_step",
    )(*where, *pieces, base, tiles)


def fetch_diag(tiles_ref, at, tile, sems):
    copies = [
        pltpu.make_async_copy(
            tiles_ref.at[side, :, pl.ds(at * 512, 512), :], tile.at[side], sems.at[side]
        )
        for side in range(2)
    ]
    for copy in copies:
        copy.start()
    return copies


def times_fetched(copies, vec, tile, out):
    for side, copy in enumerate(copies):
        copy.wait()
        for half in range(2):
            rows = slice(half * 256, (half + 1) * 256)
            total = None
            for x in range(4):
                left = vec[:, x * 256 : (x + 1) * 256]
                term = jnp.dot(left, tile[side, x, rows], preferred_element_type=F32)
                total = term if total is None else total + term
            start = side * 512 + half * 256
            out[:, start : start + 256] = total.astype(BF16)


DIAG_SCRATCH = [
    pltpu.VMEM((128, 1024), BF16),
    pltpu.VMEM((2, 4, 512, 256), BF16),
    pltpu.SemaphoreType.DMA((2,)),
]


def diag_step(pieces, tiles, at):
    def kernel(v0, v1, v2, v3, tiles_ref, out, vec, tile, sems):
        copies = fetch_diag(tiles_ref, at, tile, sems)
        vec[...] = add_up((v0, v1, v2, v3)).astype(BF16)
        times_fetched(copies, vec, tile, out)

    return pl.pallas_call(
        kernel,
        out_shape=jax.ShapeDtypeStruct((128, 1024), BF16),
        in_specs=[VMEM] * 4 + [HBM],
        out_specs=VMEM,
        scratch_shapes=DIAG_SCRATCH,
        compiler_params=params(),
        cost_estimate=cost(2 * 128 * 1024 * 1024, 4 << 20),
        name="diag_step",
    )(*pieces, tiles)


def last_step(place, pieces, tiles, at):
    def kernel(place_ref, v0, v1, v2, v3, tiles_ref, o0, o1, o2, o3, vec, tile, sems, full):
        copies = fetch_diag(tiles_ref, at, tile, sems)
        vec[...] = add_up((v0, v1, v2, v3)).astype(BF16)
        times_fetched(copies, vec, tile, full)
        for by, out in enumerate((o0, o1, o2, o3)):
            start = lax.rem(place_ref[1] + by, 4) * 128
            out[:, :128] = full[:, pl.ds(pl.multiple_of(start, 128), 128)]
            out[:, 128:] = full[:, pl.ds(pl.multiple_of(start + 512, 128), 128)]

    return pl.pallas_call(
        kernel,
        out_shape=(jax.ShapeDtypeStruct((128, 256), BF16),) * 4,
        in_specs=[SCALARS] + [VMEM] * 4 + [HBM],
        out_specs=(VMEM,) * 4,
        scratch_shapes=DIAG_SCRATCH + [pltpu.VMEM((128, 1024), BF16)],
        compiler_params=params(52 * 1024 * 1024),
        cost_estimate=cost(2 * 128 * 1024 * 1024, 4 << 20),
        name="last_step",
    )(place, *pieces, tiles)


def stage(lower_tiles, inverse_diag, orders, owners):
    moves = []
    for number, order in enumerate(orders):
        for at, (kind, index) in enumerate(order):
            if kind == "L":
                moves.append((0, index, slice(None), number, at * 512, 512))
            else:
                moves.append((1, index, slice(0, 256), number, at * 512, 256))
                moves.append((1, index, slice(256, 512), number, at * 512 + 256, 256))
    heights = [512 * len(order) for order in orders]
    heights[-1] += 16
    count = len(orders)

    def kernel(lower_ref, diag_ref, owners_ref, *refs):
        outs, held, sems = refs[:count], refs[count : 2 * count], refs[2 * count]
        plan = [
            ((lower_ref, diag_ref)[which].at[index, :, lanes], number, pl.ds(start, height))
            for which, index, lanes, number, start, height in moves
        ]
        named = pl.ds(heights[-1] - 16, 16)
        spread_out = jnp.broadcast_to(owners_ref[...].astype(F32), (16, 128)).astype(BF16)
        held[-1][named, :128] = spread_out
        held[-1][named, 128:] = jnp.zeros((16, 128), BF16)
        into, onward = [], []
        for at, (source, number, where) in enumerate(plan):
            middle = held[number].at[where]
            into.append(pltpu.make_async_copy(source, middle, sems.at[0, at]))
            onward.append(pltpu.make_async_copy(middle, outs[number].at[where], sems.at[1, at]))
        last = pltpu.make_async_copy(
            held[-1].at[named], outs[-1].at[named], sems.at[1, len(moves)]
        )
        for copy in into:
            copy.start()
        last.start()
        for first, second in zip(into, onward):
            first.wait()
            second.start()
        for copy in onward:
            copy.wait()
        last.wait()

    return pl.pallas_call(
        kernel,
        out_shape=tuple(jax.ShapeDtypeStruct((height, 256), BF16) for height in heights),
        in_specs=[HBM, HBM, VMEM],
        out_specs=(HBM,) * count,
        scratch_shapes=[pltpu.VMEM((height, 256), BF16) for height in heights]
        + [pltpu.SemaphoreType.DMA((2, len(moves) + 1))],
        compiler_params=params(60 * 1024 * 1024),
        cost_estimate=cost(0, 6 << 20),
        name="stage",
    )(lower_tiles, inverse_diag, owners)


def chosen(target, block):
    slots = lax.broadcasted_iota(jnp.int32, (256, 256), 0) + block * 256
    return jnp.where(slots == target, 1.0, 0.0).astype(BF16)


def picked(select, rows):
    return lax.dot_general(
        select, rows, (((1,), (1,)), ((), ())), preferred_element_type=F32
    )


def pack_known(place, target, known):
    def kernel(place_ref, target_ref, x1, x2, x3, out, still):
        block = pl.program_id(0)
        start = pl.multiple_of(place_ref[1] * 128, 128)
        again = pl.multiple_of(place_ref[1] * 128 + 512, 128)
        total = jnp.zeros((256, 128), F32)
        for k, ref in ((1, x1), (2, x2), (3, x3)):
            rows = jnp.concatenate([ref[:, pl.ds(start, 128)], ref[:, pl.ds(again, 128)]], axis=1)
            total = total + picked(chosen(target_ref[k], block), rows)
        out[...] = total.astype(BF16)
        still[...] = chosen(target_ref[0], block)

    return pl.pallas_call(
        kernel,
        grid=(8,),
        out_shape=(
            jax.ShapeDtypeStruct((2048, 128), BF16),
            jax.ShapeDtypeStruct((2048, 256), BF16),
        ),
        in_specs=[SCALARS, whole((4, 1, 256))] + [whole((128, 1024))] * 3,
        out_specs=(
            pl.BlockSpec((256, 128), lambda i: (i, 0)),
            pl.BlockSpec((256, 256), lambda i: (i, 0)),
        ),
        compiler_params=params(),
        cost_estimate=cost(2 * 2048 * 768 * 128, 2 << 20),
        name="pack_known",
    )(place, target, *known)


def pack_last(still, pieces, base):
    def kernel(still_ref, v0, v1, v2, v3, base_ref, out):
        rows = add_up((v0, v1, v2, v3)).astype(BF16)
        out[...] = (base_ref[...].astype(F32) + picked(still_ref[...], rows)).astype(BF16)

    return pl.pallas_call(
        kernel,
        out_shape=jax.ShapeDtypeStruct((2048, 128), BF16),
        in_specs=[VMEM] * 6,
        out_specs=VMEM,
        compiler_params=params(),
        cost_estimate=cost(2 * 2048 * 256 * 128, 2 << 20),
        name="pack_last",
    )(still, *pieces, base)


def unpack(received):
    def kernel(got, out):
        for core in range(2):
            for y in range(4):
                for x in range(4):
                    tile = got[0, core, y, x].astype(F32)
                    lanes = pl.ds((core * 4 + x) * 128, 128)
                    for half in range(2):
                        out[pl.ds(half * 32 + y * 8, 8), lanes] = tile[half * 8 : half * 8 + 8]

    return pl.pallas_call(
        kernel,
        grid=(4,),
        out_shape=jax.ShapeDtypeStruct((256, 1024), F32),
        in_specs=[pl.BlockSpec((1, 2, 4, 4, 16, 128), lambda i: (i, 0, 0, 0, 0, 0))],
        out_specs=pl.BlockSpec((64, 1024), lambda i: (i, 0)),
        compiler_params=params(),
        cost_estimate=cost(256 * 1024, 2 << 20),
        name="unpack",
    )(received.reshape(4, 2, 4, 4, 16, 128))


def slots_of(named):
    same = named[:, :, None] == named[:, None, :]
    earlier = jnp.arange(128)[None, :, None] > jnp.arange(128)[None, None, :]
    ranks = jnp.sum((same & earlier).astype(jnp.int32), axis=2)
    target = named * 16 + jnp.arange(8, dtype=jnp.int32)[:, None] * 2 + ranks
    return target.reshape(8, 4, 32).transpose(1, 0, 2).reshape(4, 1, 256)


def gathered(joined):
    rows = joined.shape[0]
    return lax.all_gather(joined, ("core", "x"), axis=0, tiled=False).reshape(2, 4, rows, 256)


def local(pivot_rhs, bound_sol, border_tiles, lower_tiles, inverse_diag, owner_map):
    z, core, y, x = (lax.axis_index(name) for name in ("z", "core", "y", "x"))
    place = jnp.stack([core, y, x, z]).astype(jnp.int32)
    lead = jnp.where((z == 0) & (core == 0), 1.0, 0.0).astype(F32)

    def tile(j, k):
        return ("L", pair_slot(j, k))

    owners = owner_map[:, :, 0]
    orders = [
        [tile(3, 2), ("D", 2), tile(3, 1), tile(2, 1), ("D", 1)],
        [tile(3, 0), tile(2, 0), tile(1, 0), ("D", 0)],
    ]
    early, late = map(gathered, stage(lower_tiles, inverse_diag, orders, owners))
    named = late[:, :, 2048, :128].astype(jnp.int32).reshape(8, 128)
    other = swap(inverse_diag[3])

    def term(side):
        start = side * 512
        rhs = lax.dynamic_slice_in_dim(pivot_rhs, start, 512, axis=2)
        bound = lax.dynamic_slice_in_dim(bound_sol, start, 512, axis=1)
        product = lax.dot_general(
            border_tiles, bound, (((0,), (0,)), ((), ())), preferred_element_type=F32
        )
        return (lead * rhs - product).astype(BF16)

    away = swap(term(1 - core))
    home = lax.optimization_barrier(term(core))
    both = (home.astype(F32) + away.astype(F32)).astype(BF16)
    over_z = spread(both[3], "z")
    def cut(part):
        return [
            lax.dynamic_slice_in_dim(part, lax.rem(x + by, 4) * 128, 128, axis=2)
            for by in range(4)
        ]

    near = deal(cut(both[2:3]), "x")
    own, *others = first_product(place, over_z, inverse_diag[3], other, near[1:2])
    zero = [along_y(others[by - 1], 0, by) for by in (1, 2, 3)]
    token = lax.ppermute(sum(piece[:8] for piece in zero), "core", [(0, 1)])
    others = gate((token, *near[2:]), others)
    one = [along_y(others[by - 1], 1, by) for by in (1, 2, 3)]
    over_x = deal(first_sum(place, own, zero, one), "x")
    quarter = sum(piece.astype(F32) for piece in over_x).astype(BF16)
    base2 = turn(place, near, quarter)[0]
    quarters = spread(quarter, "y")
    residual, x3 = lower_step(base2, quarters, early, 0, BF16, place)
    over_z = spread(residual, "z")
    base = turn(place, deal(gate((x3,), cut(both[:2])), "x"), over_z[2])
    pieces = spread(diag_step(over_z, early, 1), "y")
    base1, _ = lower_step(base[1], (x3,), early, 2, F32)
    residual, x2 = lower_step(base1, pieces, early, 3, BF16)
    over_z = spread(residual, "z")
    pieces = spread(diag_step(over_z, early, 4), "y")
    base0, _ = lower_step(base[0], (x3,), late, 0, F32)
    base0, _ = lower_step(base0, (x2,), late, 1, F32)
    residual, x1 = lower_step(base0, pieces, late, 2, BF16)
    over_z = spread(residual, "z")
    packed, still = pack_known(place, slots_of(named), (x1, x2, x3))
    rows = deal(last_step(place, over_z, late, 3), "y")
    packed = pack_last(still, rows, packed).reshape(128, 16, 128)
    received = lax.all_to_all(
        packed, ("z", "core", "y", "x"), split_axis=0, concat_axis=0, tiled=True
    )
    return unpack(received)


def solution(mesh):
    fine = Mesh(mesh.devices.reshape(4, 2, 4, 4), ("z", "core", "y", "x"))
    rows, cols = ("z", "core"), ("y", "x")
    placed = (
        P(None, cols, None),
        P(rows, None),
        P(rows, None, cols),
        P(None, rows, cols),
        P(None, cols, rows),
        P(rows + cols, None, None),
    )
    return jax.shard_map(
        local, mesh=fine, in_specs=placed, out_specs=P(rows + cols, None), check_vma=False
    )
```
